32 devices in a mesh: dp: 8 (over y, x, core), seq: 4 (over z).
Axes of the slice: x: 2, y: 2, z: 4, core: 2. Of those that a mesh axis runs over, the one named last changes fastest.
Arguments:
- tokens: bfloat16 [4096, 2048], P(('dp', 'seq')), may hold values from -6 to 6
- doc_lengths: int32 [8, 4], P('dp'), may hold values from 1 to 384, 512 in all within a row
- qkv_weight: bfloat16 [2048, 6144], P('dp'), may hold values from -0.125 to 0.125
- qkv_bias: bfloat16 [6144], P('dp'), may hold values from -1.5 to 1.5
- dense_weight: bfloat16 [2048, 2048], P('dp'), may hold values from -1 to 1
- dense_bias: bfloat16 [2048], P('dp'), may hold values from -1.5 to 1.5
- up_weight: bfloat16 [2048, 8192], P('dp'), may hold values from -0.125 to 0.125
- up_bias: bfloat16 [8192], P('dp'), may hold values from -2.5 to 2.5
- down_weight: bfloat16 [8192, 2048], P('dp'), may hold values from -0.0625 to 0.0625
- down_bias: bfloat16 [2048], P('dp'), may hold values from -1.5 to 1.5
- norm1_gain: bfloat16 [2048], P('dp'), may hold values from 0.5 to 1.5
- norm1_shift: bfloat16 [2048], P('dp'), may hold values from -1.5 to 1.5
- norm2_gain: bfloat16 [2048], P('dp'), may hold values from 0.5 to 1.5
- norm2_shift: bfloat16 [2048], P('dp'), may hold values from -1.5 to 1.5
- cotangent: bfloat16 [4096, 2048], P(('dp', 'seq')), may hold values from -6 to 6
Outputs:
- output: bfloat16 [4096, 2048], P(('dp', 'seq'))
- input_grad: bfloat16 [4096, 2048], P(('dp', 'seq'))
- qkv_weight_grad: float32 [2048, 6144], P('dp', 'seq')
- qkv_bias_grad: float32 [6144], P(('dp', 'seq'))
- dense_weight_grad: float32 [2048, 2048], P('seq', 'dp')
- dense_bias_grad: float32 [2048], P(('dp', 'seq'))
- up_weight_grad: float32 [2048, 8192], P('dp', 'seq')
- up_bias_grad: float32 [8192], P(('dp', 'seq'))
- down_weight_grad: float32 [8192, 2048], P('seq', 'dp')
- down_bias_grad: float32 [2048], P(('dp', 'seq'))
- norm1_gain_grad: float32 [2048], P(('dp', 'seq'))
- norm1_shift_grad: float32 [2048], P(('dp', 'seq'))
- norm2_gain_grad: float32 [2048], P(('dp', 'seq'))
- norm2_shift_grad: float32 [2048], P(('dp', 'seq'))
The draws below stay inside these ranges and needn't reach their ends.
Inputs may be any that keep to these rules, and one draw needn't show every extreme that they name: `doc_lengths`: each stream's 4 document lengths sum to 512, and the longest of each stream is exactly 384.
All inputs are finite; a program needn't handle non-finite values.
Results may differ from the reference program's by a relative error of at most 0.0094.
Values may be sent and summed in bfloat16 or wider, within the bound.
No kernel may reach another device: no remote copies, remote signals or barrier semaphores. Data moves between devices by JAX's collectives and lax.ppermute only.
A program may use at most 320 MiB of HBM per device.

```python
import math
import jax
import jax.numpy as jnp
import numpy as np
from jax import lax

D = 2048
H = 8
HS = 256
ROT = 64
FF = 8192
NDOC = 4
SEQLEN = 512
TOKENS = 4096
MAXDOC = 384
N_DP = 8


def steps_of(rng, shape, split, least, high):
    def one(position, blocks):
        draws = jax.random.uniform(jax.random.fold_in(jax.random.fold_in(rng, 6), position), (blocks,), jnp.float32, least / len(split), high / len(split))
        return jnp.repeat(jnp.exp(draws), shape[position] // blocks).reshape((-1,) + (1,) * (len(shape) - position - 1))

    level = one(*split[0])
    for cut in split[1:]:
        level = level * one(*cut)
    return level


def length_profile(number_of, total, most, slope):
    portions = [(1 << 20) // math.isqrt(rank ** slope) + 1 for rank in range(2, number_of + 1)]
    spare, holding = total - most - (number_of - 1), [1] * (number_of - 1)
    while spare > 0:
        free = [i for i in range(number_of - 1) if holding[i] < most]
        mass, remaining = sum([portions[i] for i in free]), spare
        for i in free:
            extra = min(most - holding[i], max(1, remaining * portions[i] // mass), spare)
            holding[i] = holding[i] + extra
            spare = spare - extra
    return np.array([most] + holding)


def uneven(own_key, number_of, total, limit, slope):
    if number_of == 2:
        one = jax.random.randint(own_key, (), max(1, total - limit), min(limit, total - 1) + 1)
        return jnp.stack([one, total - one])
    sizes = jnp.asarray(length_profile(number_of, total, limit, slope), jnp.int32)
    pairs = (number_of - 1) // 2
    giver, receiver = sizes[1:1 + 2 * pairs:2], sizes[2:2 + 2 * pairs:2]
    room = jnp.minimum(giver - 1, limit - receiver)
    moved = jax.random.randint(jax.random.fold_in(own_key, 1), (pairs,), 0, 1 << 20) % (room + 1)
    sizes = sizes.at[1:1 + 2 * pairs:2].set(giver - moved).at[2:2 + 2 * pairs:2].set(receiver + moved)
    return sizes[jax.random.permutation(jax.random.fold_in(own_key, 2), number_of)]


def bell_draw(rng, dims, deviation, reach, split=(), kind=jnp.bfloat16):
    factor_of = steps_of(rng, dims, split, -0.22, 0.18) if split else 1.0
    drawn = jax.random.normal(rng, dims, jnp.float32) * deviation * factor_of
    return jnp.minimum(jnp.maximum(drawn, -reach), reach).astype(kind)


def setup_inputs(seed: int = 0) -> dict:
    seeds = jax.random.split(jax.random.key(seed), 16)
    return {
        "tokens": bell_draw(seeds[0], (TOKENS, D), 1.0, 6.0, ((0, 32),)),
        "doc_lengths": jax.vmap(lambda own: uneven(own, NDOC, SEQLEN, MAXDOC, 2))(jax.random.split(seeds[1], N_DP)).reshape((N_DP, NDOC)).astype(jnp.int32),
        "qkv_weight": bell_draw(seeds[2], (D, 3 * D), D ** -0.5, 0.125, ((0, 8),)),
        "qkv_bias": bell_draw(seeds[3], (3 * D,), 0.3, 1.5, ((0, 8),)),
        "dense_weight": bell_draw(seeds[4], (D, D), (D // 64) ** -0.5, 1.0, ((0, 8),)),
        "dense_bias": bell_draw(seeds[5], (D,), 0.3, 1.5, ((0, 8),)),
        "up_weight": bell_draw(seeds[6], (D, FF), D ** -0.5, 0.125, ((0, 8),)),
        "up_bias": bell_draw(seeds[7], (FF,), 0.5, 2.5, ((0, 8),)),
        "down_weight": bell_draw(seeds[8], (FF, D), FF ** -0.5, 0.0625, ((0, 8),)),
        "down_bias": bell_draw(seeds[9], (D,), 0.3, 1.5, ((0, 8),)),
        "norm1_gain": jnp.clip(1.0 + 0.1 * jax.random.normal(seeds[10], (D,), jnp.float32), 0.5, 1.5).astype(jnp.bfloat16),
        "norm1_shift": bell_draw(seeds[11], (D,), 0.3, 1.5, ((0, 8),)),
        "norm2_gain": jnp.clip(1.0 + 0.1 * jax.random.normal(seeds[12], (D,), jnp.float32), 0.5, 1.5).astype(jnp.bfloat16),
        "norm2_shift": bell_draw(seeds[13], (D,), 0.3, 1.5, ((0, 8),)),
        "cotangent": bell_draw(seeds[14], (TOKENS, D), 1.0, 6.0, ((0, 32),)),
    }


@jax.custom_vjp
def low(v):
    return lax.optimization_barrier(v.astype(jnp.bfloat16)).astype(jnp.float32)

@jax.custom_vjp
def low_back(v):
    return v

def low_keep(v):
    return (low(v), None)

def low_pass(kept, grad):
    return (grad,)

def back_keep(v):
    return (v, None)

def back_low(kept, grad):
    return (low(grad),)
low.defvjp(low_keep, low_pass)
low_back.defvjp(back_keep, back_low)
HIGHEST_PRECISION = lax.Precision.HIGHEST

def layer_norm(values, gain, shift):
    average = lax.optimization_barrier(jnp.mean(values, axis=-1, keepdims=True))
    centred = values - average
    variance = lax.optimization_barrier(jnp.mean(centred * centred, axis=-1, keepdims=True))
    return centred * lax.rsqrt(variance + 1e-05) * gain + shift

def doc_layout(lengths_row, places):
    lengths_row = lengths_row.astype(jnp.int32)
    starts = (jnp.cumsum(lengths_row) - lengths_row).astype(jnp.int32)
    after = places[:, None] >= starts[None, :]
    doc_ids = lax.optimization_barrier(jnp.sum(after.astype(jnp.int32), axis=1)).astype(jnp.int32)
    begins = lax.optimization_barrier(jnp.max(jnp.where(after, starts[None, :], 0), axis=1)).astype(jnp.int32)
    return (doc_ids, (places - begins).astype(jnp.int32))

def turn_tables(positions, rot_dims):
    half_rot = rot_dims // 2
    inverse = 10000.0 ** (-(jnp.arange(half_rot, dtype=jnp.float32) * 2.0 / rot_dims))
    angles = positions.astype(jnp.float32)[:, None] * inverse[None, :]
    angles = jnp.concatenate([angles, angles], axis=1)
    return (jnp.cos(angles), jnp.sin(angles))

def rotate(values, cosine, sine_table):
    rot_dims = cosine.shape[1]
    half_rot = rot_dims // 2
    leading = values[..., :rot_dims]
    swapped = jnp.concatenate([-leading[..., half_rot:], leading[..., :half_rot]], axis=-1)
    turned = leading * cosine[:, None, :] + swapped * sine_table[:, None, :]
    return jnp.concatenate([turned, values[..., rot_dims:]], axis=-1)

def stream_forward(inputs, parameters, doc_ids, positions):
    w_qkv, b_qkv, w_dense, b_dense, w_up, b_up, w_down, b_down, gain_one, shift_one, gain_two, shift_two = parameters
    seq_len = inputs.shape[0]
    normed_one = low(layer_norm(inputs, gain_one, shift_one))
    normed_two = low(layer_norm(inputs, gain_two, shift_two))
    projected = jnp.dot(normed_one, w_qkv, precision=HIGHEST_PRECISION) + b_qkv
    projected = low_back(projected).reshape(seq_len, H, 3 * HS)
    cosine, sine_table = turn_tables(positions, ROT)
    queries = low(rotate(projected[..., :HS], cosine, sine_table))
    keys_all = low(rotate(projected[..., HS:2 * HS], cosine, sine_table))
    values_all = low(projected[..., 2 * HS:])
    places = jnp.arange(seq_len, dtype=jnp.int32)
    allowed = (doc_ids[:, None] == doc_ids[None, :]) & (places[None, :] <= places[:, None])

    def one_head(pieces):
        head_q, head_k, head_v = pieces
        scores = low_back(jnp.dot(head_q, head_k.T, precision=HIGHEST_PRECISION) * HS ** (-0.5))
        masked = jnp.where(allowed, scores, -1e+30)
        largest = lax.optimization_barrier(jnp.max(masked, axis=-1, keepdims=True))
        exponent = jnp.exp(masked - largest)
        probs = exponent / lax.optimization_barrier(jnp.sum(exponent, axis=-1, keepdims=True))
        return low(jnp.dot(low(probs), head_v, precision=HIGHEST_PRECISION))
    mixed_heads = lax.map(jax.checkpoint(one_head), (queries.transpose(1, 0, 2), keys_all.transpose(1, 0, 2), values_all.transpose(1, 0, 2)))
    attended = low_back(mixed_heads).transpose(1, 0, 2).reshape(seq_len, H * HS)
    hidden = low_back(jnp.dot(normed_two, w_up, precision=HIGHEST_PRECISION) + b_up)
    activated = low(jax.nn.gelu(hidden, approximate=False))
    branch_att = jnp.dot(attended, w_dense, precision=HIGHEST_PRECISION) + b_dense
    branch_ffn = jnp.dot(activated, w_down, precision=HIGHEST_PRECISION) + b_down
    return inputs + branch_att + branch_ffn

def reference(tokens, doc_lengths, qkv_weight, qkv_bias, dense_weight, dense_bias, up_weight, up_bias, down_weight, down_bias, norm1_gain, norm1_shift, norm2_gain, norm2_shift, cotangent):
    parameters = tuple((p.astype(jnp.float32) for p in (qkv_weight, qkv_bias, dense_weight, dense_bias, up_weight, up_bias, down_weight, down_bias, norm1_gain, norm1_shift, norm2_gain, norm2_shift)))
    stream_inputs = tokens.astype(jnp.float32).reshape(N_DP, SEQLEN, D)
    stream_cotans = cotangent.astype(jnp.float32).reshape(N_DP, SEQLEN, D)

    def stream_step(totals, stream_item):
        inputs, cotan_rows, lengths_row = stream_item
        places = jnp.arange(SEQLEN, dtype=jnp.int32)
        doc_ids, positions = doc_layout(lengths_row, places)

        def forward(values, params_now):
            return stream_forward(values, params_now, doc_ids, positions)
        result, pullback = jax.vjp(forward, inputs, parameters)
        input_grad, param_grads = pullback(cotan_rows)
        totals = tuple((t + d for t, d in zip(totals, param_grads)))
        return (totals, (result.astype(jnp.bfloat16), input_grad.astype(jnp.bfloat16)))
    zero_grads = tuple((jnp.zeros_like(p) for p in parameters))
    totals, (results, input_grads) = lax.scan(stream_step, zero_grads, (stream_inputs, stream_cotans, doc_lengths))
    g_qkv, g_qkv_b, g_dense, g_dense_b, g_up, g_up_b, g_down, g_down_b, g_gain1, g_shift1, g_gain2, g_shift2 = totals
    return (results.reshape(TOKENS, D), input_grads.reshape(TOKENS, D), g_qkv, g_qkv_b, g_dense, g_dense_b, g_up, g_up_b, g_down, g_down_b, g_gain1, g_shift1, g_gain2, g_shift2)
```

```python
import jax
import jax.numpy as jnp
from jax import lax
from jax.sharding import PartitionSpec as P

H = 8
HS = 256
ROT = 64
F32 = jnp.float32
BF16 = jnp.bfloat16


def matmul(left, right):
    return jnp.dot(left, right, preferred_element_type=F32)


def times_transposed(left, right):
    return lax.dot_general(left, right, (((1,), (1,)), ((), ())), preferred_element_type=F32)


def left_transposed(left, right):
    return lax.dot_general(left, right, (((0,), (0,)), ((), ())), preferred_element_type=F32)


def doc_layout(lengths_row, places):
    starts = jnp.cumsum(lengths_row) - lengths_row
    after = places[:, None] >= starts[None, :]
    doc_ids = jnp.sum(after.astype(jnp.int32), axis=1)
    begins = jnp.max(jnp.where(after, starts[None, :], 0), axis=1)
    return (doc_ids, places - begins)


def turn_tables(positions, rot_dims):
    half_rot = rot_dims // 2
    inverse = 10000.0 ** (-(jnp.arange(half_rot, dtype=F32) * 2.0 / rot_dims))
    angles = positions.astype(F32)[:, None] * inverse[None, :]
    angles = jnp.concatenate([angles, angles], axis=1)
    return (jnp.cos(angles), jnp.sin(angles))


def rotate(values, cosine, sine_table):
    half_rot = ROT // 2
    leading = values[..., :ROT]
    swapped = jnp.concatenate([-leading[..., half_rot:], leading[..., :half_rot]], axis=-1)
    turned = leading * cosine[..., None, :] + swapped * sine_table[..., None, :]
    return jnp.concatenate([turned, values[..., ROT:]], axis=-1)


def unrotate(gradient, cosine, sine_table):
    half_rot = ROT // 2
    leading = gradient[..., :ROT]
    scaled = leading * sine_table[..., None, :]
    moved = jnp.concatenate([scaled[..., half_rot:], -scaled[..., :half_rot]], axis=-1)
    return jnp.concatenate(
        [leading * cosine[..., None, :] + moved, gradient[..., ROT:]], axis=-1
    )


class Place:
    def __init__(self):
        self.n_dp = lax.axis_size("dp")
        self.n_seq = lax.axis_size("seq")
        assert self.n_dp == 2 * self.n_seq
        self.split = 2 if H % (2 * self.n_seq) == 0 else 1
        self.blocks = self.n_dp // self.split
        self.dp = lax.axis_index("dp")
        self.z = lax.axis_index("seq")
        self.block = self.dp // self.split
        self.part = self.dp % self.split
        self.masks = [1 << k for k in range(self.blocks.bit_length() - 1)]
        self.order = [k ^ (k >> 1) for k in range(self.blocks)]

    def swap(self, value, mask):
        return lax.ppermute(value, "dp", [(i, i ^ mask) for i in range(self.n_dp)])

    def to_relative(self, value, axis):
        size = value.shape[axis] // self.blocks
        return jnp.concatenate(
            [
                lax.dynamic_slice_in_dim(value, (self.block ^ off) * size, size, axis)
                for off in self.order
            ],
            axis=axis,
        )

    def to_natural(self, value, axis):
        size = value.shape[axis] // self.blocks
        table = [0] * self.blocks
        for position, off in enumerate(self.order):
            table[off] = position
        table = jnp.array(table, jnp.int32)
        return jnp.concatenate(
            [
                lax.dynamic_slice_in_dim(value, table[self.block ^ k] * size, size, axis)
                for k in range(self.blocks)
            ],
            axis=axis,
        )

    def pair(self, own, other, axis):
        return jnp.where(
            self.part == 0,
            jnp.concatenate([own, other], axis=axis),
            jnp.concatenate([other, own], axis=axis),
        )

    def gather(self, piece):
        half = piece.shape[0] // 2
        gathered = []
        for rows, masks in ((piece[:half], self.masks), (piece[half:], self.masks[::-1])):
            have = {0: rows}
            for mask in masks:
                offs = list(have)
                sent = jnp.concatenate([have[o] for o in offs], 0) if len(offs) > 1 else have[offs[0]]
                got = self.swap(sent, mask * self.split)
                for k, o in enumerate(offs):
                    have[o ^ mask] = got[k * half : (k + 1) * half]
            gathered.append(have)
        return gathered

    def spread(self, piece):
        chips = self.n_dp // 2
        masks = [1 << k for k in range(chips.bit_length() - 1)]
        offset = (self.dp // 2) ^ self.z
        half = piece.shape[0] // 2
        result = []
        for rows, order in ((piece[:half], masks), (piece[half:], masks[::-1])):
            held = [0]
            for mask in order:
                pairs = [
                    (
                        (2 * (z ^ o) + c) * self.n_seq + z,
                        (2 * (z ^ o ^ mask) + c) * self.n_seq + z,
                    )
                    for z in range(self.n_seq)
                    for o in held
                    for c in range(2)
                ]
                got = lax.ppermute(rows, ("dp", "seq"), pairs)
                takes = jnp.zeros((), jnp.bool_)
                for o in held:
                    takes = takes | (offset == (o ^ mask))
                rows = jnp.where(takes, got, rows)
                held = held + [o ^ mask for o in held]
            result.append(rows)
        return jnp.concatenate(result, axis=0)

    def scatter_sum(self, product, halves):
        out = []
        for half, masks in zip(halves, (self.masks, self.masks[::-1])):
            live = list(range(self.blocks))
            extra = {}

            def total(offs):
                whole = product(half, offs)
                if all(o not in extra for o in offs):
                    return whole
                axis, size = whole.ndim and product.axis, whole.shape[product.axis] // len(offs)
                parts = []
                for k, o in enumerate(offs):
                    value = lax.slice_in_dim(whole, k * size, (k + 1) * size, axis=axis)
                    for more in extra.get(o, ()):
                        value = value + more.astype(F32)
                    parts.append(value)
                return parts[0] if len(parts) == 1 else jnp.concatenate(parts, axis=axis)

            for mask in masks:
                away = [o for o in self.order if o in live and o & mask]
                sent = total(away).astype(BF16)
                got = self.swap(sent, mask * self.split)
                size = got.shape[product.axis] // len(away)
                for k, o in enumerate(away):
                    extra.setdefault(o ^ mask, []).append(
                        lax.slice_in_dim(got, k * size, (k + 1) * size, axis=product.axis)
                    )
                live = [o for o in live if not o & mask]
            out.append(total([0]))
        return out


class Product:
    def __init__(self, place, by_block, other, axis):
        self.place, self.by_block, self.other, self.axis = place, by_block, other, axis
        self.size = by_block.shape[1] // place.blocks

    def __call__(self, half, offs):
        where = [self.place.order.index(o) for o in offs]
        if where == list(range(where[0], where[0] + len(where))):
            blocks = self.by_block[:, where[0] * self.size : (where[-1] + 1) * self.size]
        else:
            blocks = jnp.concatenate(
                [self.by_block[:, w * self.size : (w + 1) * self.size] for w in where], axis=1
            )
        width = self.other.shape[1] // 2
        others = self.other[:, half * width : (half + 1) * width]
        if self.axis == 0:
            return left_transposed(blocks, others)
        return left_transposed(others, blocks)


def on_device(
    tokens,
    doc_lengths,
    qkv_weight,
    qkv_bias,
    dense_weight,
    dense_bias,
    up_weight,
    up_bias,
    down_weight,
    down_bias,
    norm1_gain,
    norm1_shift,
    norm2_gain,
    norm2_shift,
    cotangent,
):
    here = Place()
    n_dp, n_seq, split, blocks = here.n_dp, here.n_seq, here.split, here.blocks
    z, part = here.z, here.part
    rows_here, width = tokens.shape
    seq_len = rows_here * n_seq
    hidden_rows = down_weight.shape[0]
    slice_rows = hidden_rows // n_seq
    heads_here = H // (n_seq * split)
    head_cols = heads_here * 3 * HS

    tokens_rel = here.to_relative(tokens, 1)
    x_stream = lax.all_gather(tokens_rel, "seq", axis=0, tiled=True)
    g_stream = lax.all_gather(cotangent, "seq", axis=0, tiled=True)
    if split == 2:
        x_all = jnp.concatenate([x_stream, here.swap(x_stream, 1)], axis=0)
        g_all = jnp.concatenate([g_stream, here.swap(g_stream, 1)], axis=0)
        lengths = jnp.concatenate([doc_lengths, here.swap(doc_lengths, 1)], axis=0)
    else:
        x_all, g_all, lengths = x_stream, g_stream, doc_lengths
    g_rel = here.to_relative(g_all, 1)

    def up_columns(core):
        return jnp.concatenate(
            [
                lax.dynamic_slice_in_dim(
                    up_weight, (k * split + core) * hidden_rows + z * slice_rows, slice_rows, 1
                )
                for k in range(blocks)
            ],
            axis=1,
        )

    def qkv_columns(core):
        return lax.dynamic_slice_in_dim(qkv_weight, (z * split + core) * head_cols, head_cols, 1)

    def rows_of_d(columns):
        piece = columns(part)
        if split == 2:
            piece = here.pair(piece, here.swap(columns(1 - part), 1), 0)
        gathered = here.gather(piece)
        return jnp.concatenate(
            [half[o] for o in here.order for half in gathered], axis=0
        )

    w_up = rows_of_d(up_columns)
    down_piece = lax.dynamic_slice_in_dim(down_weight, z * slice_rows, slice_rows, 0)
    down_halves = here.gather(down_piece)
    w_down = jnp.zeros((blocks * slice_rows, width), BF16)
    half_rows = slice_rows // 2
    for index, half in enumerate(down_halves):
        for o in range(blocks):
            w_down = lax.dynamic_update_slice_in_dim(
                w_down, half[o], (here.block ^ o) * slice_rows + index * half_rows, 0
            )
    w_qkv = rows_of_d(qkv_columns)
    w_dense = here.spread(dense_weight)
    if split == 1:
        other = here.swap(w_dense, 1)
        w_dense = jnp.where(
            here.dp % 2 == 0,
            jnp.concatenate([w_dense, other], 0),
            jnp.concatenate([other, w_dense], 0),
        )

    small = (qkv_bias, up_bias, dense_bias, down_bias, norm1_gain, norm1_shift, norm2_gain, norm2_shift)
    packed_small = lax.all_gather(jnp.concatenate(small)[None], "dp", axis=0, tiled=True)
    spans, first = [], 0
    for value in small:
        spans.append(packed_small[:, first : first + value.shape[0]].astype(F32))
        first += value.shape[0]
    b_qkv, b_up, b_dense, b_down, gain_one, shift_one, gain_two, shift_two = spans
    b_qkv = lax.dynamic_slice_in_dim(b_qkv.reshape(-1), (z * split + part) * head_cols, head_cols, 0)
    b_up = lax.dynamic_slice_in_dim(b_up, z * slice_rows, slice_rows, 1).reshape(
        blocks, split, slice_rows
    )
    b_up = lax.dynamic_index_in_dim(b_up, part, 1, keepdims=False).reshape(-1)
    b_out = (b_dense + b_down).reshape(-1)
    gain_one, shift_one, gain_two, shift_two = (
        here.to_relative(v.reshape(-1), 0) for v in (gain_one, shift_one, gain_two, shift_two)
    )

    def standardize(values):
        values = values.astype(F32)
        average = jnp.mean(values, axis=-1, keepdims=True)
        centred = values - average
        variance = jnp.mean(centred * centred, axis=-1, keepdims=True)
        inverse = lax.rsqrt(variance + 1e-05)
        return centred * inverse, inverse

    xhat, _ = standardize(x_all)
    normed_one = (xhat * gain_one + shift_one).astype(BF16)
    normed_two = (xhat * gain_two + shift_two).astype(BF16)

    hidden = matmul(normed_two, w_up) + b_up
    cdf = 0.5 + 0.5 * lax.erf(hidden * (0.5**0.5))
    activated = (hidden * cdf).astype(BF16)
    slope = cdf + hidden * (jnp.exp(-0.5 * hidden * hidden) * 0.3989422804014327)
    sum_down = here.scatter_sum(Product(here, g_rel, activated, 1), (0, 1))
    branches = matmul(activated, w_down)
    grad_hidden = (times_transposed(g_all, w_down) * slope).astype(BF16)
    grad_up_bias = jnp.sum(grad_hidden.astype(F32), axis=0)
    sum_up = here.scatter_sum(Product(here, normed_two, grad_hidden, 0), (0, 1))
    grad_two = times_transposed(grad_hidden, w_up)

    places = jnp.arange(seq_len, dtype=jnp.int32)
    doc_ids, positions = jax.vmap(lambda row: doc_layout(row, places))(lengths)
    cosine, sine = jax.vmap(lambda p: turn_tables(p, ROT))(positions)
    allowed = (doc_ids[:, :, None] == doc_ids[:, None, :]) & (
        places[None, None, :] <= places[None, :, None]
    )
    allowed = allowed[:, None]
    projected = (matmul(normed_one, w_qkv) + b_qkv).reshape(split, seq_len, heads_here, 3 * HS)
    queries = rotate(projected[..., :HS], cosine, sine).astype(BF16)
    keys = rotate(projected[..., HS : 2 * HS], cosine, sine).astype(BF16)
    values = projected[..., 2 * HS :].astype(BF16)
    scale = HS ** (-0.5)
    scores = jnp.einsum("bqhd,bkhd->bhqk", queries, keys, preferred_element_type=F32) * scale
    masked = jnp.where(allowed, scores, -1e30)
    largest = jnp.max(masked, axis=-1, keepdims=True)
    exponent = jnp.exp(masked - largest)
    probs = exponent / jnp.sum(exponent, axis=-1, keepdims=True)
    probs_low = probs.astype(BF16)
    attended = jnp.einsum("bhqk,bkhd->bqhd", probs_low, values, preferred_element_type=F32)
    attended = attended.astype(BF16).reshape(split * seq_len, heads_here * HS)
    sum_dense = here.scatter_sum(Product(here, g_rel, attended, 1), (0, 1))
    branches = branches + matmul(attended, w_dense)
    grad_attended = times_transposed(g_all, w_dense).astype(BF16)
    grad_attended = grad_attended.reshape(split, seq_len, heads_here, HS)
    grad_probs = jnp.einsum("bqhd,bkhd->bhqk", grad_attended, values, preferred_element_type=F32)
    inner = jnp.sum(probs * grad_probs, axis=-1, keepdims=True)
    grad_scores = (probs * (grad_probs - inner)).astype(BF16)
    grad_queries = jnp.einsum("bhqk,bkhd->bqhd", grad_scores, keys, preferred_element_type=F32)
    grad_keys = jnp.einsum("bhqk,bqhd->bkhd", grad_scores, queries, preferred_element_type=F32)
    grad_values = jnp.einsum("bhqk,bqhd->bkhd", probs_low, grad_attended, preferred_element_type=F32)
    grad_projected = jnp.concatenate(
        [
            unrotate(grad_queries * scale, cosine, sine),
            unrotate(grad_keys * scale, cosine, sine),
            grad_values,
        ],
        axis=-1,
    ).astype(BF16)
    grad_projected = grad_projected.reshape(split * seq_len, head_cols)
    grad_qkv_bias = jnp.sum(grad_projected.astype(F32), axis=0)
    sum_qkv = here.scatter_sum(Product(here, normed_one, grad_projected, 0), (0, 1))
    grad_one = times_transposed(grad_projected, w_qkv)

    def join(partial_sum):
        own = partial_sum[:seq_len]
        if split == 2:
            own = own + here.swap(partial_sum[seq_len:].astype(BF16), 1).astype(F32)
        return lax.psum_scatter(own.astype(BF16), "seq", scatter_dimension=0, tiled=True).astype(F32)

    branch_rows = join(branches)
    term_rows = join(grad_one * gain_one + grad_two * gain_two)
    output = (tokens.astype(F32) + branch_rows + b_out).astype(BF16)
    xhat_here, inverse_here = standardize(tokens_rel)
    term = (
        term_rows
        - jnp.mean(term_rows, axis=-1, keepdims=True)
        - xhat_here * jnp.mean(term_rows * xhat_here, axis=-1, keepdims=True)
    ) * inverse_here
    cotan_rows = cotangent.astype(F32)
    input_grad = (cotan_rows + here.to_natural(term, 1)).astype(BF16)

    norm_sums = [
        jnp.sum(grad_one * xhat, axis=0),
        jnp.sum(grad_one, axis=0),
        jnp.sum(grad_two * xhat, axis=0),
        jnp.sum(grad_two, axis=0),
    ]
    norm_sums = [here.to_natural(v, 0) for v in norm_sums]
    wide_qkv = lax.dynamic_update_slice_in_dim(
        jnp.zeros((H * 3 * HS,), F32), grad_qkv_bias, (z * split + part) * head_cols, 0
    )
    wide_up = lax.dynamic_update_slice(
        jnp.zeros((blocks, split, n_seq, slice_rows), F32),
        grad_up_bias.reshape(blocks, 1, 1, slice_rows),
        (0, part, z, 0),
    )
    column_total = jnp.sum(cotan_rows, axis=0)
    devices = n_dp * n_seq
    wide = [wide_qkv, wide_up, column_total] + norm_sums
    wide = [v.reshape(devices, -1) for v in wide]
    sizes = [v.shape[1] for v in wide]
    swapped = lax.all_to_all(
        jnp.concatenate(wide, axis=1), ("dp", "seq"), split_axis=0, concat_axis=0, tiled=True
    )
    total = jnp.sum(swapped, axis=0)
    sums, first = [], 0
    for size in sizes:
        sums.append(total[first : first + size])
        first += size
    sum_qkv_bias, sum_up_bias, sum_column, sum_gain_one, sum_shift_one, sum_gain_two, sum_shift_two = sums

    def to_plane(halves, axis):
        whole = jnp.concatenate(halves, axis=axis).astype(BF16)
        moved = lax.all_to_all(whole, "seq", split_axis=axis, concat_axis=axis, tiled=True)
        if split == 1:
            per = moved.shape[axis] // (n_seq * 2)
            if axis == 0:
                moved = moved.reshape(n_seq, 2, per, -1).transpose(1, 0, 2, 3).reshape(moved.shape)
            else:
                moved = moved.reshape(-1, n_seq, 2, per).transpose(0, 2, 1, 3).reshape(moved.shape)
        return moved

    def to_cores(value, axis):
        if split == 1:
            return value.astype(F32)
        size = value.shape[axis] // 2
        mine = lax.dynamic_slice_in_dim(value, part * size, size, axis)
        other = lax.dynamic_slice_in_dim(value, (1 - part) * size, size, axis)
        return here.pair(mine, here.swap(other, 1), 1 - axis).astype(F32)

    grad_up = to_cores(to_plane(sum_up, 1), 0)
    grad_down = to_cores(to_plane(sum_down, 0), 1)
    grad_qkv = to_cores(jnp.concatenate(sum_qkv, axis=1), 0)
    grad_dense = to_cores(jnp.concatenate(sum_dense, axis=0), 1)
    return (
        output,
        input_grad,
        grad_qkv,
        sum_qkv_bias,
        grad_dense,
        sum_column,
        grad_up,
        sum_up_bias,
        grad_down,
        sum_column,
        sum_gain_one,
        sum_shift_one,
        sum_gain_two,
        sum_shift_two,
    )


def solution(mesh):
    rows = P(("dp", "seq"), None)
    flat = P(("dp", "seq"))
    placed = (rows,) + (P("dp", None),) * 2 + (P("dp"), P("dp", None)) * 3 + (P("dp"),) * 5 + (rows,)
    return jax.shard_map(
        on_device,
        mesh=mesh,
        in_specs=placed,
        out_specs=(
            rows,
            rows,
            P("dp", "seq"),
            flat,
            P("seq", "dp"),
            flat,
            P("dp", "seq"),
            flat,
            P("seq", "dp"),
            flat,
            flat,
            flat,
            flat,
            flat,
        ),
        check_vma=False,
    )
```

```python
import jax
import jax.numpy as jnp
from jax import lax
from jax.experimental import pallas as pl
from jax.experimental.pallas import tpu as pltpu
from jax.sharding import PartitionSpec as P

H = 8
HS = 256
ROT = 64
HINT = 0.05
F32 = jnp.float32
BF16 = jnp.bfloat16


def matmul(left, right):
    return jnp.dot(left, right, preferred_element_type=F32)


def times_transposed(left, right):
    return lax.dot_general(left, right, (((1,), (1,)), ((), ())), preferred_element_type=F32)


def left_transposed(left, right):
    return lax.dot_general(left, right, (((0,), (0,)), ((), ())), preferred_element_type=F32)


def doc_layout(lengths_row, places):
    starts = jnp.cumsum(lengths_row) - lengths_row
    after = places[:, None] >= starts[None, :]
    doc_ids = jnp.sum(after.astype(jnp.int32), axis=1)
    begins = jnp.max(jnp.where(after, starts[None, :], 0), axis=1)
    return (doc_ids, places - begins)


def turn_tables(positions, rot_dims):
    half_rot = rot_dims // 2
    inverse = 10000.0 ** (-(jnp.arange(half_rot, dtype=F32) * 2.0 / rot_dims))
    angles = positions.astype(F32)[:, None] * inverse[None, :]
    angles = jnp.concatenate([angles, angles], axis=1)
    return (jnp.cos(angles), jnp.sin(angles))


def cost(flops, reads, writes, transcendentals=0):
    return pl.CostEstimate(
        flops=int(flops * HINT),
        bytes_accessed=int((reads + writes) * HINT),
        transcendentals=int(transcendentals * HINT),
    )


VMEM = pl.BlockSpec(memory_space=pltpu.VMEM)
SMEM = pl.BlockSpec(memory_space=pltpu.SMEM)


def on_chip(body, name, arrays, shapes, estimate, scalars=()):
    return pl.pallas_call(
        body,
        in_specs=[SMEM] * len(scalars) + [VMEM] * len(arrays),
        out_specs=[VMEM] * len(shapes),
        out_shape=[jax.ShapeDtypeStruct(*shape) for shape in shapes],
        compiler_params=pltpu.CompilerParams(vmem_limit_bytes=16 * 1024 * 1024),
        cost_estimate=estimate,
        name=name,
    )(*scalars, *arrays)


def chunks(total, size):
    return [(at, min(size, total - at)) for at in range(0, total, size)]


def two_norms(arrays, scales):
    rows, width = arrays[0].shape
    total = rows * len(arrays)
    tile = 32

    def body(scales_ref, *refs):
        one_ref, two_ref, stats_ref = refs[-3:]
        for k in range(len(arrays)):

            @pl.loop(0, rows // tile)
            def _(i, k=k):
                values = refs[k][pl.ds(pl.multiple_of(i * tile, tile), tile), :].astype(F32)
                average = jnp.mean(values, axis=-1, keepdims=True)
                centred = values - average
                variance = jnp.mean(centred * centred, axis=-1, keepdims=True)
                inverse = lax.rsqrt(variance + 1e-05)
                xhat = centred * inverse
                span = pl.ds(pl.multiple_of(k * rows + i * tile, tile), tile)
                one_ref[span, :] = (xhat * scales_ref[0:1, :] + scales_ref[1:2, :]).astype(BF16)
                two_ref[span, :] = (xhat * scales_ref[2:3, :] + scales_ref[3:4, :]).astype(BF16)
                stats_ref[span, :] = jnp.concatenate([average, inverse], axis=1)

    return on_chip(
        body,
        "two_norms",
        [scales, *arrays],
        [((total, width), BF16), ((total, width), BF16), ((total, 2), F32)],
        cost(total * width * 24, total * width * 2, total * width * 4),
    )


class Pieces:
    def __init__(self, arrays, tiles, size, blocks=None):
        self.arrays, self.tiles, self.size, self.blocks = arrays, tiles, size, blocks

    def runs(self):
        found = []
        for k, tile in enumerate(self.tiles):
            at = 0
            for which, first, count in tile:
                last = found[-1] if found else None
                joins = last and self.blocks is None and last[0] == which and last[1] + last[2] == first
                if joins:
                    found[-1] = (which, last[1], last[2] + count, last[3], last[4])
                else:
                    found.append((which, first, count, k, at))
                at += count
        return found


def feed_up(x, pieces, b):
    rows, width = x.shape
    units = pieces.arrays[0].shape[1]

    def body(x_ref, b_ref, *refs):
        w_refs, (act_ref, slope_ref) = refs[:-2], refs[-2:]
        for col, cols in chunks(units, 512):
            for row, count in chunks(rows, 256):
                at = (pl.ds(row, count), pl.ds(col, cols))
                hidden = b_ref[:, at[1]]
                for which, first, depth, k, place in pieces.runs():
                    start = k * pieces.size + place
                    hidden = hidden + matmul(
                        x_ref[at[0], start : start + depth], w_refs[which][first : first + depth, at[1]]
                    )
                cdf = 0.5 + 0.5 * lax.erf(hidden * (0.5**0.5))
                act_ref[at] = (hidden * cdf).astype(BF16)
                slope_ref[at] = cdf + hidden * (jnp.exp(-0.5 * hidden * hidden) * 0.3989422804014327)

    return on_chip(
        body,
        "feed_up",
        [x, b, *pieces.arrays],
        [((rows, units), BF16), ((rows, units), F32)],
        cost(4 * rows * width * units, 2 * (rows + units) * width, 6 * rows * units, 2 * rows * units),
    )


def hidden_grad(g, pieces, slope):
    rows, width = g.shape
    units = slope.shape[1]

    def body(blocks_ref, g_ref, slope_ref, *refs):
        w_refs, (out_ref, sum_ref) = refs[:-2], refs[-2:]
        for which, first, count, k, place in pieces.runs():
            columns = pl.ds(pl.multiple_of(blocks_ref[k] * pieces.size + place, 128), count)
            total = jnp.zeros((1, count), F32)
            for row, size in chunks(rows, 256):
                span = pl.ds(row, size)
                value = times_transposed(g_ref[span, :], w_refs[which][first : first + count, :])
                value = (value * slope_ref[span, columns]).astype(BF16)
                out_ref[span, columns] = value
                total = total + jnp.sum(value.astype(F32), axis=0, keepdims=True)
            sum_ref[:, columns] = total

    return on_chip(
        body,
        "hidden_grad",
        [g, slope, *pieces.arrays],
        [((rows, units), BF16), ((1, units), F32)],
        cost(4 * rows * width * units, 2 * (rows + units) * width + 4 * rows * units, 2 * rows * units),
        [pieces.blocks],
    )


def turn(values, cosine, before, after, sign):
    lanes = cosine.shape[1]
    half = ROT // 2
    first = values[:, :lanes]
    first = first * cosine + sign * (
        pltpu.roll(first, lanes - half, 1) * before + pltpu.roll(first, half, 1) * after
    )
    return jnp.concatenate([first, values[:, lanes:]], axis=1)


def attention_forward(x, pieces, bias, tables, begins):
    count, size, width = x.shape
    columns = bias.shape[1]

    def body(x_ref, b_ref, cos_ref, before_ref, after_ref, begin_ref, *refs):
        w_refs, (qkv_ref, probs_ref, out_ref) = refs[:-3], refs[-3:]
        for n in range(count):
            turns = (cos_ref[n], before_ref[n], after_ref[n])
            projected = b_ref[...]
            for which, first, rows, k, place in pieces.runs():
                start = k * pieces.size + place
                projected = projected + matmul(
                    x_ref[n, :, start : start + rows], w_refs[which][first : first + rows, :]
                )
            queries = turn(projected[:, :HS], *turns, 1.0).astype(BF16)
            keys = turn(projected[:, HS : 2 * HS], *turns, 1.0).astype(BF16)
            values = projected[:, 2 * HS :].astype(BF16)
            qkv_ref[n, :, :HS] = queries
            qkv_ref[n, :, HS : 2 * HS] = keys
            qkv_ref[n, :, 2 * HS :] = values
            for row, tile in chunks(size, 256):
                rows = slice(row, row + tile)
                scores = times_transposed(queries[rows], keys) * (HS**-0.5)
                places = lax.broadcasted_iota(jnp.int32, (tile, size), 1)
                here = lax.broadcasted_iota(jnp.int32, (tile, size), 0) + row
                allowed = (places >= begin_ref[n, rows, :]) & (places <= here)
                masked = jnp.where(allowed, scores, -1e30)
                exponent = jnp.exp(masked - jnp.max(masked, axis=-1, keepdims=True))
                probs = exponent / jnp.sum(exponent, axis=-1, keepdims=True)
                probs_ref[n, rows, :] = probs
                out_ref[n, rows, :] = matmul(probs.astype(BF16), values).astype(BF16)

    return on_chip(
        body,
        "attention_forward",
        [x, bias, *tables, begins, *pieces.arrays],
        [
            ((count, size, columns), BF16),
            ((count, size, size), F32),
            ((count, size, HS), BF16),
        ],
        cost(
            count * size * (size * HS * 8 + 4 * width * columns),
            count * size * width * 2,
            count * size * (columns * 2 + size * 4),
            count * size * size,
        ),
    )


def attention_backward(qkv, probs, g, w_dense, tables):
    count, size, columns = qkv.shape
    scale = HS**-0.5

    def body(qkv_ref, probs_ref, g_ref, w_ref, cos_ref, before_ref, after_ref, out_ref, sum_ref):
        total = jnp.zeros((1, columns), F32)
        for n in range(count):
            turns = (cos_ref[n], before_ref[n], after_ref[n])
            queries = qkv_ref[n, :, :HS]
            keys = qkv_ref[n, :, HS : 2 * HS]
            values = qkv_ref[n, :, 2 * HS :]
            grad = times_transposed(g_ref[n], w_ref[...]).astype(BF16)
            probs_now = probs_ref[n]
            grad_probs = times_transposed(grad, values)
            inner = jnp.sum(probs_now * grad_probs, axis=-1, keepdims=True)
            grad_scores = (probs_now * (grad_probs - inner)).astype(BF16)
            grad_queries = turn(matmul(grad_scores, keys) * scale, *turns, -1.0).astype(BF16)
            grad_keys = turn(left_transposed(grad_scores, queries) * scale, *turns, -1.0).astype(BF16)
            grad_values = left_transposed(probs_now.astype(BF16), grad).astype(BF16)
            whole = jnp.concatenate([grad_queries, grad_keys, grad_values], axis=1)
            out_ref[n] = whole
            total = total + jnp.sum(whole.astype(F32), axis=0, keepdims=True)
        sum_ref[...] = total

    return on_chip(
        body,
        "attention_backward",
        [qkv, probs, g, w_dense, *tables],
        [((count, size, columns), BF16), ((1, columns), F32)],
        cost(
            count * size * (size * HS * 16 + 4 * HS * g.shape[2]),
            count * size * (columns * 4 + size * 4),
            count * size * columns * 2,
        ),
    )


def branch_rows_of(attended, w_dense, activated, pieces, first, count, extra=None):
    width = w_dense.shape[1]
    inner, units = attended.shape[1], activated.shape[1]
    arrays = [attended, w_dense, activated] + ([] if extra is None else [extra])

    def body(blocks_ref, a_ref, wa_ref, b_ref, *refs):
        if extra is not None:
            extra_ref, *refs = refs
        for row, rows in chunks(count, 256):
            span = pl.ds(first * count + row, rows)
            for col, cols in chunks(width, 512):
                at = pl.ds(col, cols)
                value = matmul(a_ref[span, :], wa_ref[:, at])
                for which, start, depth, k, place in pieces.runs():
                    columns = pl.ds(pl.multiple_of(blocks_ref[k] * pieces.size + place, 128), depth)
                    value = value + matmul(b_ref[span, columns], refs[which][start : start + depth, at])
                if extra is not None:
                    value = value + extra_ref[pl.ds(row, rows), at].astype(F32)
                refs[-1][pl.ds(row, rows), at] = value.astype(BF16)

    return on_chip(
        body,
        "branch_rows",
        arrays + pieces.arrays,
        [((count, width), BF16)],
        cost(4 * count * (inner + units) * width, 2 * (inner + units) * (width + count), 2 * count * width),
        [pieces.blocks],
    )[0]


def input_terms(grad_proj, qkv_pieces, grad_hid, up_pieces, x, stats, scales, first, extra=None):
    count, width = x.shape
    tile = up_pieces.size
    columns, units = grad_proj.shape[1], grad_hid.shape[1]
    weights = qkv_pieces.arrays + up_pieces.arrays
    arrays = [grad_proj, grad_hid, x, stats, scales] + ([] if extra is None else [extra])

    def body(gp_ref, gh_ref, x_ref, stats_ref, scales_ref, *refs):
        if extra is not None:
            extra_ref, *refs = refs
        out_ref, sums_ref = refs[-2:]
        split = len(qkv_pieces.arrays)
        for k, (qkv_tile, up_tile) in enumerate(zip(qkv_pieces.tiles, up_pieces.tiles)):
            (which, start, _), = qkv_tile
            wq = refs[which][start : start + tile, :]
            (which, start, _), = up_tile
            wu = refs[split + which][start : start + tile, :]
            at = pl.ds(k * tile, tile)
            sums = [jnp.zeros((1, tile), F32)] * 4
            for row, rows in chunks(count, 256):
                span = pl.ds(row, rows)
                there = pl.ds(first * count + row, rows)
                one = times_transposed(gp_ref[there, :], wq)
                two = times_transposed(gh_ref[there, :], wu)
                xhat = (x_ref[span, at].astype(F32) - stats_ref[there, 0:1]) * stats_ref[there, 1:2]
                value = one * scales_ref[0:1, at] + two * scales_ref[2:3, at]
                if extra is not None:
                    value = value + extra_ref[span, at].astype(F32)
                out_ref[span, at] = value.astype(BF16)
                for n, term in enumerate((one * xhat, one, two * xhat, two)):
                    sums[n] = sums[n] + jnp.sum(term, axis=0, keepdims=True)
            sums_ref[:, at] = jnp.concatenate(sums, axis=0)

    return on_chip(
        body,
        "input_terms",
        arrays + weights,
        [((count, width), BF16), ((4, width), F32)],
        cost(
            4 * count * (columns + units) * width,
            2 * (columns + units) * (width + count) + 2 * count * width,
            2 * count * width,
        ),
    )


def weight_grad(left, right, left_at, right_block, rows, cols, extras=(), halves=False, kind=BF16):
    depth = left.shape[0]

    def body(block_ref, l_ref, r_ref, *refs):
        extra_refs, outs = refs[: len(extras)], refs[len(extras) :]
        where = pl.ds(pl.multiple_of(block_ref[0] * cols, 128), cols)
        tile = min(256, rows // 2)
        for row, size in chunks(rows, tile):
            value = left_transposed(l_ref[:, pl.ds(left_at + row, size)], r_ref[:, where])
            for ref, (array, first) in zip(extra_refs, extras):
                if first <= row < first + array.shape[0]:
                    value = value + ref[pl.ds(row - first, size), :].astype(F32)
            if halves:
                half = rows // 2
                outs[row // half][pl.ds(row % half, size), :] = value.astype(kind)
            else:
                outs[0][pl.ds(row, size), :] = value.astype(kind)

    shapes = [((rows // 2, cols), kind)] * 2 if halves else [((rows, cols), kind)]
    found = on_chip(
        body,
        "weight_grad",
        [left, right, *[e[0] for e in extras]],
        shapes,
        cost(4 * depth * rows * cols, 2 * depth * (rows + cols), rows * cols * 2),
        [jnp.reshape(right_block, (1,)).astype(jnp.int32)],
    )
    return found if halves else found[0]


class Place:
    def __init__(self):
        self.n_dp = lax.axis_size("dp")
        self.n_seq = lax.axis_size("seq")
        assert self.n_dp == 2 * self.n_seq
        self.split = 2 if H % (2 * self.n_seq) == 0 else 1
        self.blocks = self.n_dp // self.split
        self.dp = lax.axis_index("dp")
        self.z = lax.axis_index("seq")
        self.block = self.dp // self.split
        self.part = self.dp % self.split
        self.masks = [1 << k for k in range(self.blocks.bit_length() - 1)]
        self.order = list(range(self.blocks))
        self.paired = self.split == 2 and self.blocks == 4

    def swap(self, value, mask):
        return lax.ppermute(value, "dp", [(i, i ^ mask) for i in range(self.n_dp)])

    def to_relative(self, value, axis):
        size = value.shape[axis] // self.blocks
        return jnp.concatenate(
            [
                lax.dynamic_slice_in_dim(value, (self.block ^ off) * size, size, axis)
                for off in self.order
            ],
            axis=axis,
        )

    def to_natural(self, value, axis):
        return self.to_relative(value, axis)

    def pair(self, own, other, axis):
        return jnp.where(
            self.part == 0,
            jnp.concatenate([own, other], axis=axis),
            jnp.concatenate([other, own], axis=axis),
        )

    def gather(self, piece):
        half = piece.shape[0] // 2
        gathered = []
        for rows, masks in ((piece[:half], self.masks), (piece[half:], self.masks[::-1])):
            have = {0: rows}
            for mask in masks:
                offs = list(have)
                sent = jnp.concatenate([have[o] for o in offs], 0) if len(offs) > 1 else have[offs[0]]
                got = self.swap(sent, mask * self.split)
                for k, o in enumerate(offs):
                    have[o ^ mask] = got[k * half : (k + 1) * half]
            gathered.append(have)
        return gathered

    def spread(self, piece, chain):
        chips = self.n_dp // 2
        masks = [1 << k for k in range(chips.bit_length() - 1)]
        offset = (self.dp // 2) ^ self.z
        half = piece.shape[0] // 2
        states = [(piece[:half], masks, [0]), (piece[half:], masks[::-1], [0])]
        for step in range(len(masks)):
            got = []
            for rows, order, held in states:
                pairs = [
                    (
                        (2 * (z ^ o) + c) * self.n_seq + z,
                        (2 * (z ^ o ^ order[step]) + c) * self.n_seq + z,
                    )
                    for z in range(self.n_seq)
                    for o in held
                    for c in range(2)
                ]
                got.append(lax.ppermute(rows, ("dp", "seq"), pairs))
            yield
            got = chain(*got)
            after = []
            for new, (rows, order, held) in zip(got, states):
                takes = jnp.zeros((), jnp.bool_)
                for o in held:
                    takes = takes | (offset == (o ^ order[step]))
                after.append(
                    (jnp.where(takes, new, rows), order, held + [o ^ order[step] for o in held])
                )
            states = after
            chain.done(tuple(state[0] for state in states))
        self.spread_rows = jnp.concatenate([state[0] for state in states], axis=0)
        yield

    def scatter_sum(self, product, halves):
        out = []
        for half, masks in zip(halves, (self.masks, self.masks[::-1])):
            live = list(range(self.blocks))
            extra = {}

            def total(offs):
                whole = product(half, offs)
                if all(o not in extra for o in offs):
                    return whole
                axis, size = whole.ndim and product.axis, whole.shape[product.axis] // len(offs)
                parts = []
                for k, o in enumerate(offs):
                    value = lax.slice_in_dim(whole, k * size, (k + 1) * size, axis=axis)
                    for more in extra.get(o, ()):
                        value = value + more.astype(F32)
                    parts.append(value)
                return parts[0] if len(parts) == 1 else jnp.concatenate(parts, axis=axis)

            for mask in masks:
                away = [o for o in self.order if o in live and o & mask]
                sent = total(away).astype(BF16)
                got = self.swap(sent, mask * self.split)
                size = got.shape[product.axis] // len(away)
                for k, o in enumerate(away):
                    extra.setdefault(o ^ mask, []).append(
                        lax.slice_in_dim(got, k * size, (k + 1) * size, axis=product.axis)
                    )
                live = [o for o in live if not o & mask]
            out.append(total([0]))
        return out


class Product:
    def __init__(self, place, by_block, other, axis):
        self.place, self.by_block, self.other, self.axis = place, by_block, other, axis
        self.size = by_block.shape[1] // place.blocks

    def __call__(self, half, offs):
        where = [self.place.order.index(o) for o in offs]
        if where == list(range(where[0], where[0] + len(where))):
            blocks = self.by_block[:, where[0] * self.size : (where[-1] + 1) * self.size]
        else:
            blocks = jnp.concatenate(
                [self.by_block[:, w * self.size : (w + 1) * self.size] for w in where], axis=1
            )
        width = self.other.shape[1] // 2
        others = self.other[:, half * width : (half + 1) * width]
        if self.axis == 0:
            return left_transposed(blocks, others)
        return left_transposed(others, blocks)


class Chain:
    def __init__(self):
        self.last = None

    def __call__(self, *values):
        if self.last is not None:
            values = tuple(lax.optimization_barrier((values, self.last))[0])
        return values if len(values) > 1 else values[0]

    def done(self, value):
        self.last = value
        return value


class Gathered:
    def __init__(self, here, piece):
        self.here, self.piece = here, piece
        self.half = piece.shape[0] // 2
        if here.paired:
            self.by_x, self.by_y = here.swap(piece, 2), here.swap(piece, 4)

    def hand_on(self, chain):
        if self.here.paired:
            by_x, by_y = chain(self.by_x, self.by_y)
            first, second = by_x[: self.half], by_y[self.half :]
            chain.done((first, second))
            self.handed = (self.here.swap(first, 4), self.here.swap(second, 2))

    def rows(self, size, moving):
        here, block = self.here, self.piece.shape[0]
        if here.paired:
            arrays = [self.piece, self.by_x, self.by_y, *self.handed]
            parts = [(k, r, block) for k in range(3) for r in (0,)] + [(3, 0, self.half), (4, 0, self.half)]
            tiles, now, left = [], [], size
            for which, first, count in parts:
                while count:
                    take = min(left, count)
                    now.append((which, first, take))
                    first, count, left = first + take, count - take, left - take
                    if not left:
                        tiles.append(now)
                        now, left = [], size
            blocks = None
            if moving:
                assert size == block
                blocks = here.block ^ jnp.arange(here.blocks, dtype=jnp.int32)
            return Pieces(arrays, tiles, size, blocks)
        halves = here.gather(self.piece)
        order = [here.block ^ k for k in range(here.blocks)] if moving else None
        whole = jnp.concatenate([half[o] for o in range(here.blocks) for half in halves], axis=0)
        if moving:
            whole = here.to_natural(whole, 0)
        count = whole.shape[0] // size
        blocks = jnp.arange(count, dtype=jnp.int32) if moving else None
        return Pieces([whole], [[(0, k * size, size)] for k in range(count)], size, blocks)


class Scattered:
    def __init__(self, here, left, right, axis):
        self.here, self.left, self.right, self.axis = here, left, right, axis
        self.size = (left if axis == 0 else right).shape[1] // here.blocks

    def part(self, off, **more):
        if self.axis == 0:
            return weight_grad(
                self.left, self.right, off * self.size, jnp.int32(0), self.size, self.right.shape[1], **more
            )
        return weight_grad(
            self.left, self.right, 0, self.here.block ^ off, self.left.shape[1], self.size, **more
        )

    def first(self, chain):
        if self.here.paired:
            self.left, self.right = chain(self.left, self.right)
            one, two = chain.done(self.part(3, halves=True))
            self.by_x, self.by_y = self.here.swap(one, 2), self.here.swap(two, 4)

    def second(self, chain):
        if self.here.paired:
            by_x, by_y = chain(self.by_x, self.by_y)
            half = by_x.shape[0]
            to_x = self.part(1, extras=((by_y, half),))
            to_y = self.part(2, extras=((by_x, 0),))
            chain.done((to_x, to_y))
            self.by_x, self.by_y = self.here.swap(to_x, 2), self.here.swap(to_y, 4)

    def last(self, chain, kind):
        if self.here.paired:
            by_x, by_y = chain(self.by_x, self.by_y)
            return chain.done(self.part(0, extras=((by_x, 0), (by_y, 0)), kind=kind))
        right = self.right
        if self.axis == 1:
            right = self.here.to_relative(right, 1)
            product = Product(self.here, right, self.left, 1)
        else:
            product = Product(self.here, self.left, right, 0)
        halves = self.here.scatter_sum(product, (0, 1))
        return jnp.concatenate(halves, axis=1 - self.axis).astype(kind)


def on_device(
    tokens,
    doc_lengths,
    qkv_weight,
    qkv_bias,
    dense_weight,
    dense_bias,
    up_weight,
    up_bias,
    down_weight,
    down_bias,
    norm1_gain,
    norm1_shift,
    norm2_gain,
    norm2_shift,
    cotangent,
):
    here = Place()
    chain = Chain()
    n_dp, n_seq, split, blocks = here.n_dp, here.n_seq, here.split, here.blocks
    z, part = here.z, here.part
    rows_here, width = tokens.shape
    seq_len = rows_here * n_seq
    hidden_rows = down_weight.shape[0]
    slice_rows = hidden_rows // n_seq
    assert H == n_seq * split
    head_cols = 3 * HS

    tokens_rel = chain.done(here.to_relative(tokens, 1))
    x_own = lax.all_gather(tokens_rel, "seq", axis=0, tiled=True)

    def up_columns(weight, core):
        return jnp.concatenate(
            [
                lax.dynamic_slice_in_dim(
                    weight, (k * split + core) * hidden_rows + z * slice_rows, slice_rows, 1
                )
                for k in range(blocks)
            ],
            axis=1,
        )

    def qkv_columns(weight, core):
        return lax.dynamic_slice_in_dim(weight, (z * split + core) * head_cols, head_cols, 1)

    def first_exchange(columns, weight):
        if split == 2:
            return here.swap(chain.done(columns(chain(weight), 1 - part)), 1)
        return None

    def chip_rows(columns, weight, got):
        own = columns(chain(weight), part)
        return chain.done(own if got is None else here.pair(own, got, 0))

    up_got = first_exchange(up_columns, up_weight)
    qkv_got = first_exchange(qkv_columns, qkv_weight)
    dense_steps = here.spread(dense_weight, chain)
    next(dense_steps)
    up_rows = Gathered(here, chip_rows(up_columns, up_weight, up_got))
    qkv_rows = Gathered(here, chip_rows(qkv_columns, qkv_weight, qkv_got))
    g_own = lax.all_gather(chain(cotangent), "seq", axis=0, tiled=True)
    down_piece = chain.done(
        lax.dynamic_slice_in_dim(chain(down_weight), z * slice_rows, slice_rows, 0)
    )

    small = (qkv_bias, up_bias, dense_bias, down_bias, norm1_gain, norm1_shift, norm2_gain, norm2_shift)
    packed_small = jnp.concatenate(chain(*small))
    packed_small = chain.done(jnp.broadcast_to(packed_small[None], (n_dp,) + packed_small.shape))
    packed_small = lax.all_to_all(packed_small, "dp", 0, 0, tiled=True)
    lengths = chain(doc_lengths)
    if split == 2:
        lengths = jnp.concatenate([lengths, here.swap(lengths, 1)], axis=0)

    places = jnp.arange(seq_len, dtype=jnp.int32)
    _, positions = jax.vmap(lambda row: doc_layout(row, places))(lengths)
    cosine, sine = jax.vmap(lambda p: turn_tables(p, ROT))(positions)
    lanes = 128
    rest = ((0, 0), (0, 0), (0, lanes - ROT))
    half_rot = ROT // 2
    tables = (
        jnp.pad(cosine, rest, constant_values=1.0),
        jnp.pad(-sine[..., :half_rot], ((0, 0), (0, 0), (0, lanes - half_rot))),
        jnp.pad(sine[..., half_rot:], ((0, 0), (0, 0), (half_rot, lanes - ROT))),
    )
    begins = (places[None] - positions)[..., None]

    spans, first = [], 0
    for value in small:
        spans.append(packed_small[:, first : first + value.shape[0]].astype(F32))
        first += value.shape[0]
    b_qkv, b_up, b_dense, b_down = spans[:4]
    b_qkv = lax.dynamic_slice_in_dim(b_qkv.reshape(-1), (z * split + part) * head_cols, head_cols, 0)
    b_up = lax.dynamic_slice_in_dim(b_up, z * slice_rows, slice_rows, 1).reshape(
        blocks, split, slice_rows
    )
    b_up = lax.dynamic_index_in_dim(b_up, part, 1, keepdims=False).reshape(-1)
    b_out = (b_dense + b_down).reshape(-1)
    scales = here.to_relative(jnp.stack([v.reshape(-1) for v in spans[4:]]), 1)
    if here.paired:
        (b_qkv, b_up, scales, begins) = chain(b_qkv, b_up, scales, begins)
        tables = chain(*tables)
        chain.done((b_qkv, b_up, scales, tables, begins))

    next(dense_steps)
    up_rows.hand_on(chain)
    down_rows = Gathered(here, chain(down_piece))
    x_own = chain(x_own)
    streams = [x_own] + ([here.swap(x_own, 1)] if split == 2 else [])
    for _ in dense_steps:
        pass
    w_dense = here.spread_rows
    if split == 1:
        other = here.swap(w_dense, 1)
        w_dense = jnp.where(
            here.dp % 2 == 0,
            jnp.concatenate([w_dense, other], 0),
            jnp.concatenate([other, w_dense], 0),
        )
    qkv_rows.hand_on(chain)
    normed_one, normed_two, stats = chain.done(two_norms(chain(*streams) if split == 2 else streams, scales))
    up_pieces = up_rows.rows(256, False)
    activated, slope = chain.done(feed_up(chain(normed_two), up_pieces, b_up[None]))
    qkv_pieces = qkv_rows.rows(256, False)
    qkv, probs, attended = chain.done(
        attention_forward(
            chain(normed_one).reshape(split, seq_len, width), qkv_pieces, b_qkv[None], tables, begins
        )
    )
    attended = attended.reshape(split * seq_len, HS)

    g_own = chain(g_own)
    g_all = jnp.concatenate([g_own, here.swap(g_own, 1)], axis=0) if split == 2 else g_own
    down_rows.hand_on(chain)
    sum_down = Scattered(here, activated, g_all, 1)
    sum_dense = Scattered(here, attended, g_all, 1)
    sum_down.first(chain)
    sum_dense.first(chain)
    grad_projected, grad_qkv_bias = chain.done(
        attention_backward(chain(qkv), probs, g_all.reshape(split, seq_len, width), w_dense, tables)
    )
    grad_projected = grad_projected.reshape(split * seq_len, head_cols)
    sum_qkv = Scattered(here, normed_one, grad_projected, 0)
    sum_qkv.first(chain)
    sum_down.second(chain)
    down_pieces = down_rows.rows(down_piece.shape[0] if here.paired else 256, True)

    def join(value):
        return lax.psum_scatter(value, "seq", scatter_dimension=0, tiled=True).astype(F32)

    def branches(first, extra=None):
        return chain.done(
            branch_rows_of(chain(attended), w_dense, activated, down_pieces, first, seq_len, extra)
        )

    def terms(first, extra=None):
        return chain.done(
            input_terms(
                chain(grad_projected),
                qkv_pieces,
                grad_hidden,
                up_pieces,
                streams[first],
                stats,
                scales,
                first,
                extra,
            )
        )

    branch_other = here.swap(branches(1), 1) if split == 2 else None
    grad_hidden, grad_up_bias = chain.done(hidden_grad(chain(g_all), down_pieces, slope))
    sum_up = Scattered(here, normed_two, grad_hidden, 0)
    branch_rows = join(branches(0, branch_other))
    sum_up.first(chain)
    if split == 2:
        term_other, norm_sums = terms(1)
        term_other = here.swap(term_other, 1)
        sum_dense.second(chain)
        term_own, more_sums = terms(0, term_other)
        norm_sums = norm_sums + more_sums
    else:
        term_own, norm_sums = terms(0)
    term_rows = join(term_own)
    sum_up.second(chain)
    output = chain.done((chain(branch_rows) + tokens.astype(F32) + b_out).astype(BF16))
    sum_qkv.second(chain)

    norm_sums = here.to_natural(chain(norm_sums), 1)
    wide_qkv = lax.dynamic_update_slice_in_dim(
        jnp.zeros((H * head_cols,), F32), grad_qkv_bias.reshape(-1), (z * split + part) * head_cols, 0
    )
    wide_up = lax.dynamic_update_slice(
        jnp.zeros((blocks, split, n_seq, slice_rows), F32),
        grad_up_bias.reshape(blocks, 1, 1, slice_rows),
        (0, part, z, 0),
    )
    cotan_rows = cotangent.astype(F32)
    column_total = jnp.sum(cotan_rows, axis=0)
    devices = n_dp * n_seq
    wide = [wide_qkv, wide_up, column_total] + [norm_sums[k] for k in range(4)]
    wide = [v.reshape(devices, -1) for v in wide]
    sizes = [v.shape[1] for v in wide]
    swapped = lax.all_to_all(
        chain.done(jnp.concatenate(wide, axis=1)), ("dp", "seq"), split_axis=0, concat_axis=0, tiled=True
    )
    total = jnp.sum(swapped, axis=0)
    sums, first = [], 0
    for size in sizes:
        sums.append(total[first : first + size])
        first += size
    sum_qkv_bias, sum_up_bias, sum_column, sum_gain_one, sum_shift_one, sum_gain_two, sum_shift_two = sums

    def to_plane(whole, axis):
        moved = lax.all_to_all(whole, "seq", split_axis=axis, concat_axis=axis, tiled=True)
        if split == 1:
            per = moved.shape[axis] // (n_seq * 2)
            if axis == 0:
                moved = moved.reshape(n_seq, 2, per, -1).transpose(1, 0, 2, 3).reshape(moved.shape)
            else:
                moved = moved.reshape(-1, n_seq, 2, per).transpose(0, 2, 1, 3).reshape(moved.shape)
        return moved

    def to_cores(value, axis):
        if split == 1:
            return value.astype(F32)
        size = value.shape[axis] // 2
        mine = lax.dynamic_slice_in_dim(value, part * size, size, axis)
        other = lax.dynamic_slice_in_dim(value, (1 - part) * size, size, axis)
        return here.pair(mine, here.swap(other, 1), 1 - axis).astype(F32)

    grad_down = to_cores(to_plane(sum_down.last(chain, BF16), 0), 1)
    grad_dense = to_cores(sum_dense.last(chain, F32), 1)
    grad_up = to_cores(to_plane(sum_up.last(chain, BF16), 1), 0)
    grad_qkv = to_cores(sum_qkv.last(chain, F32), 0)

    values = tokens_rel.astype(F32)
    centred = values - jnp.mean(values, axis=-1, keepdims=True)
    inverse = lax.rsqrt(jnp.mean(centred * centred, axis=-1, keepdims=True) + 1e-05)
    xhat = centred * inverse
    term = (
        term_rows
        - jnp.mean(term_rows, axis=-1, keepdims=True)
        - xhat * jnp.mean(term_rows * xhat, axis=-1, keepdims=True)
    ) * inverse
    input_grad = (cotan_rows + here.to_natural(term, 1)).astype(BF16)
    return (
        output,
        input_grad,
        grad_qkv,
        sum_qkv_bias,
        grad_dense,
        sum_column,
        grad_up,
        sum_up_bias,
        grad_down,
        sum_column,
        sum_gain_one,
        sum_shift_one,
        sum_gain_two,
        sum_shift_two,
    )


def solution(mesh):
    rows = P(("dp", "seq"), None)
    flat = P(("dp", "seq"))
    placed = (rows,) + (P("dp", None),) * 2 + (P("dp"), P("dp", None)) * 3 + (P("dp"),) * 5 + (rows,)
    return jax.shard_map(
        on_device,
        mesh=mesh,
        in_specs=placed,
        out_specs=(
            rows,
            rows,
            P("dp", "seq"),
            flat,
            P("seq", "dp"),
            flat,
            P("dp", "seq"),
            flat,
            P("seq", "dp"),
            flat,
            flat,
            flat,
            flat,
            flat,
        ),
        check_vma=False,
    )
```

```python
import jax
import jax.numpy as jnp
import numpy as np
from jax import lax
from jax.experimental import pallas as pl
from jax.experimental.pallas import tpu as pltpu
from jax.sharding import PartitionSpec as P

H = 8
HS = 256
ROT = 64
HINT = 1.0
LIMIT = 16 * 1024 * 1024
F32 = jnp.float32
BF16 = jnp.bfloat16


def matmul(left, right):
    return jnp.dot(left, right, preferred_element_type=F32)


def times_transposed(left, right):
    return lax.dot_general(left, right, (((1,), (1,)), ((), ())), preferred_element_type=F32)


def left_transposed(left, right):
    return lax.dot_general(left, right, (((0,), (0,)), ((), ())), preferred_element_type=F32)


def cost(flops, reads, writes, transcendentals=0):
    return pl.CostEstimate(
        flops=int(flops * HINT),
        bytes_accessed=int((reads + writes) * HINT),
        transcendentals=int(transcendentals * HINT),
    )


VMEM = pl.BlockSpec(memory_space=pltpu.VMEM)
SMEM = pl.BlockSpec(memory_space=pltpu.SMEM)


def on_chip(body, name, arrays, shapes, estimate, scalars=()):
    return pl.pallas_call(
        body,
        in_specs=[SMEM] * len(scalars) + [VMEM] * len(arrays),
        out_specs=[VMEM] * len(shapes),
        out_shape=[jax.ShapeDtypeStruct(*shape) for shape in shapes],
        compiler_params=pltpu.CompilerParams(vmem_limit_bytes=LIMIT),
        cost_estimate=estimate,
        name=name,
    )(*scalars, *arrays)


def each(total, size, step):
    if total <= size:
        return step(0)

    @pl.loop(0, total // size)
    def _(i):
        step(pl.multiple_of(i * size, size))


def chunks(total, size):
    return [(at, min(size, total - at)) for at in range(0, total, size)]


def two_norms(arrays, scales, blocks):
    rows, width = arrays[0].shape
    total = rows * len(arrays)
    tile = 32

    size = width // blocks

    def body(scales_ref, *refs):
        ones, twos, stats_ref = refs[len(arrays) : -1 - blocks], refs[-1 - blocks : -1], refs[-1]
        for k in range(len(arrays)):

            @pl.loop(0, rows // tile)
            def _(i, k=k):
                values = refs[k][pl.ds(pl.multiple_of(i * tile, tile), tile), :].astype(F32)
                average = jnp.mean(values, axis=-1, keepdims=True)
                centred = values - average
                variance = jnp.mean(centred * centred, axis=-1, keepdims=True)
                inverse = lax.rsqrt(variance + 1e-05)
                xhat = centred * inverse
                span = pl.ds(pl.multiple_of(k * rows + i * tile, tile), tile)
                one = (xhat * scales_ref[0:1, :] + scales_ref[1:2, :]).astype(BF16)
                two = (xhat * scales_ref[2:3, :] + scales_ref[3:4, :]).astype(BF16)
                for n in range(blocks):
                    ones[n][span, :] = one[:, n * size : (n + 1) * size]
                    twos[n][span, :] = two[:, n * size : (n + 1) * size]
                stats_ref[span, :] = jnp.concatenate([average, inverse], axis=1)

    return on_chip(
        body,
        "two_norms",
        [scales, *arrays],
        [((total, size), BF16)] * (2 * blocks) + [((total, 2), F32)],
        cost(total * width * 24, total * width * 2, total * width * 4),
    )


class Pieces:
    def __init__(self, arrays, tiles, size, blocks=None, columns=None):
        self.arrays, self.tiles, self.size, self.blocks = arrays, tiles, size, blocks
        self.first, self.width = columns or (0, arrays[0].shape[1])

    def inside(self, size):
        cut = []
        for which, first, count, k, place in self.runs():
            start = k * self.size + place
            while count:
                take = min(count, size - start % size)
                cut.append((which, first, take, start // size, start % size))
                first, start, count = first + take, start + take, count - take
        return cut

    def runs(self):
        found = []
        for k, tile in enumerate(self.tiles):
            at = 0
            for which, first, count in tile:
                last = found[-1] if found else None
                joins = last and self.blocks is None and last[0] == which and last[1] + last[2] == first
                if joins:
                    found[-1] = (which, last[1], last[2] + count, last[3], last[4])
                else:
                    found.append((which, first, count, k, at))
                at += count
        return found


def feed_up(x, pieces, b):
    rows, size = x[0].shape
    width = size * len(x)
    units = pieces.width

    def body(b_ref, *refs):
        x_refs, w_refs, (act_ref, slope_ref) = refs[: len(x)], refs[len(x) : -2], refs[-2:]
        def step(row):
            for col, cols in chunks(units, 512):
                at = (pl.ds(row, min(256, rows)), pl.ds(col, cols))
                hidden = b_ref[:, at[1]]
                for which, first, depth, k, place in pieces.inside(size):
                    hidden = hidden + matmul(
                        x_refs[k][at[0], place : place + depth],
                        w_refs[which][first : first + depth, pl.ds(pieces.first + col, cols)],
                    )
                cdf = 0.5 + 0.5 * lax.erf(hidden * (0.5**0.5))
                act_ref[at] = (hidden * cdf).astype(BF16)
                slope_ref[at] = cdf + hidden * (jnp.exp(-0.5 * hidden * hidden) * 0.3989422804014327)

        each(rows, 256, step)

    return on_chip(
        body,
        "feed_up",
        [b, *x, *pieces.arrays],
        [((rows, units), BF16), ((rows, units), F32)],
        cost(4 * rows * width * units, 2 * (rows + units) * width, 6 * rows * units, 2 * rows * units),
    )


def cotangent_blocks(streams, at, blocks):
    rows, width = streams[0].shape
    size = width // blocks

    def body(at_ref, *refs):
        ins, outs = refs[: len(streams)], refs[len(streams) :]
        for off in range(blocks):
            place = pl.ds(pl.multiple_of((at_ref[2] ^ off) * size, 128), size)
            for n in range(len(streams)):
                outs[off][n * rows : (n + 1) * rows, :] = ins[n][:, place]

    return on_chip(
        body,
        "cotangent_blocks",
        streams,
        [((rows * len(streams), size), BF16)] * blocks,
        cost(0, rows * width * 4, rows * width * 4),
        [at],
    )


def hidden_grad(g, pieces, slope, at):
    rows, size = g[0].shape
    width = size * len(g)
    units = slope.shape[1]

    def body(blocks_ref, at_ref, slope_ref, *refs):
        g_refs, w_refs, (out_ref, sum_ref) = refs[: len(g)], refs[len(g) : -2], refs[-2:]
        for which, first, count, k, place in pieces.runs():
            columns = pl.ds(pl.multiple_of(blocks_ref[k] * pieces.size + place, 128), count)
            total = jnp.zeros((1, count), F32)
            for row, tall in chunks(rows, 256):
                span = pl.ds(row, tall)
                value = jnp.zeros((tall, count), F32)
                for off in range(len(g)):
                    block = pl.ds(pl.multiple_of((at_ref[2] ^ off) * size, 128), size)
                    value = value + times_transposed(
                        g_refs[off][span, :], w_refs[which][first : first + count, block]
                    )
                value = (value * slope_ref[span, columns]).astype(BF16)
                out_ref[span, columns] = value
                total = total + jnp.sum(value.astype(F32), axis=0, keepdims=True)
            sum_ref[:, columns] = total

    return on_chip(
        body,
        "hidden_grad",
        [slope, *g, *pieces.arrays],
        [((rows, units), BF16), ((1, units), F32)],
        cost(4 * rows * width * units, 2 * (rows + units) * width + 4 * rows * units, 2 * rows * units),
        [pieces.blocks, at],
    )


def turn(values, cosine, before, after, sign):
    lanes = cosine.shape[1]
    half = ROT // 2
    first = values[:, :lanes]
    first = first * cosine + sign * (
        pltpu.roll(first, lanes - half, 1) * before + pltpu.roll(first, half, 1) * after
    )
    return jnp.concatenate([first, values[:, lanes:]], axis=1)


def attention_forward(x, pieces, bias, tables, begins):
    count, size = tables[0].shape[:2]
    part = x[0].shape[1]
    width = part * len(x)
    columns = bias.shape[1]

    def body(b_ref, cos_ref, before_ref, after_ref, begin_ref, *refs):
        x_refs, w_refs, (qkv_ref, probs_ref, out_ref) = refs[: len(x)], refs[len(x) : -3], refs[-3:]
        @pl.loop(0, count)
        def _(n):
            turns = (cos_ref[n], before_ref[n], after_ref[n])
            projected = b_ref[...]
            for which, first, rows, k, place in pieces.inside(part):
                projected = projected + matmul(
                    x_refs[k][pl.ds(pl.multiple_of(n * size, size), size), place : place + rows],
                    w_refs[which][first : first + rows, pl.ds(pieces.first, columns)],
                )
            queries = turn(projected[:, :HS], *turns, 1.0).astype(BF16)
            keys = turn(projected[:, HS : 2 * HS], *turns, 1.0).astype(BF16)
            values = projected[:, 2 * HS :].astype(BF16)
            qkv_ref[n, :, :HS] = queries
            qkv_ref[n, :, HS : 2 * HS] = keys
            qkv_ref[n, :, 2 * HS :] = values
            for row, tile in chunks(size, 256):
                rows = slice(row, row + tile)
                scores = times_transposed(queries[rows], keys) * (HS**-0.5)
                places = lax.broadcasted_iota(jnp.int32, (tile, size), 1)
                here = lax.broadcasted_iota(jnp.int32, (tile, size), 0) + row
                allowed = (places >= begin_ref[n, rows, :]) & (places <= here)
                masked = jnp.where(allowed, scores, -1e30)
                exponent = jnp.exp(masked - jnp.max(masked, axis=-1, keepdims=True))
                probs = exponent / jnp.sum(exponent, axis=-1, keepdims=True)
                probs_ref[n, rows, :] = probs
                out_ref[n, rows, :] = matmul(probs.astype(BF16), values).astype(BF16)

    return on_chip(
        body,
        "attention_forward",
        [bias, *tables, begins, *x, *pieces.arrays],
        [
            ((count, size, columns), BF16),
            ((count, size, size), F32),
            ((count, size, HS), BF16),
        ],
        cost(
            count * size * (size * HS * 8 + 4 * width * columns),
            count * size * width * 2,
            count * size * (columns * 2 + size * 4),
            count * size * size,
        ),
    )


def attention_backward(qkv, probs, g, w_dense, tables, at):
    count, size, columns = qkv.shape
    scale = HS**-0.5
    part = g[0].shape[1]

    def body(at_ref, qkv_ref, probs_ref, w_ref, cos_ref, before_ref, after_ref, *refs):
        g_refs, (out_ref, sum_ref) = refs[:-2], refs[-2:]
        sum_ref[...] = jnp.zeros((1, columns), F32)

        @pl.loop(0, count)
        def _(n):
            turns = (cos_ref[n], before_ref[n], after_ref[n])
            queries = qkv_ref[n, :, :HS]
            keys = qkv_ref[n, :, HS : 2 * HS]
            values = qkv_ref[n, :, 2 * HS :]
            grad = jnp.zeros((size, HS), F32)
            for off in range(len(g)):
                block = pl.ds(pl.multiple_of((at_ref[2] ^ off) * part, 128), part)
                grad = grad + times_transposed(g_refs[off][pl.ds(pl.multiple_of(n * size, size), size), :], w_ref[:, block])
            grad = grad.astype(BF16)
            probs_now = probs_ref[n]
            grad_probs = times_transposed(grad, values)
            inner = jnp.sum(probs_now * grad_probs, axis=-1, keepdims=True)
            grad_scores = (probs_now * (grad_probs - inner)).astype(BF16)
            grad_queries = turn(matmul(grad_scores, keys) * scale, *turns, -1.0).astype(BF16)
            grad_keys = turn(left_transposed(grad_scores, queries) * scale, *turns, -1.0).astype(BF16)
            grad_values = left_transposed(probs_now.astype(BF16), grad).astype(BF16)
            whole = jnp.concatenate([grad_queries, grad_keys, grad_values], axis=1)
            out_ref[n] = whole
            sum_ref[...] += jnp.sum(whole.astype(F32), axis=0, keepdims=True)

    return on_chip(
        body,
        "attention_backward",
        [qkv, probs, w_dense, *tables, *g],
        [((count, size, columns), BF16), ((1, columns), F32)],
        cost(
            count * size * (size * HS * 16 + 4 * HS * part * len(g)),
            count * size * (columns * 4 + size * 4),
            count * size * columns * 2,
        ),
        [at],
    )


def branch_rows_of(attended, w_dense, activated, pieces, first, count, extra=None):
    width = w_dense.shape[1]
    inner, units = attended.shape[1], activated.shape[1]
    arrays = [attended, w_dense, activated] + ([] if extra is None else [extra])

    def body(blocks_ref, a_ref, wa_ref, b_ref, *refs):
        if extra is not None:
            extra_ref, *refs = refs
        for row, rows in chunks(count, 256):
            span = pl.ds(first * count + row, rows)
            for col, cols in chunks(width, 512):
                at = pl.ds(col, cols)
                value = matmul(a_ref[span, :], wa_ref[:, at])
                for which, start, depth, k, place in pieces.runs():
                    columns = pl.ds(pl.multiple_of(blocks_ref[k] * pieces.size + place, 128), depth)
                    value = value + matmul(b_ref[span, columns], refs[which][start : start + depth, at])
                if extra is not None:
                    value = value + extra_ref[pl.ds(row, rows), at].astype(F32)
                refs[-1][pl.ds(row, rows), at] = value.astype(BF16)

    return on_chip(
        body,
        "branch_rows",
        arrays + pieces.arrays,
        [((count, width), BF16)],
        cost(4 * count * (inner + units) * width, 2 * (inner + units) * (width + count), 2 * count * width),
        [pieces.blocks],
    )[0]


def input_terms(grad_proj, qkv_pieces, grad_hid, up_pieces, x, stats, scales, first, extra=None):
    count, width = x.shape
    tile = up_pieces.size
    columns, units = grad_proj.shape[1], grad_hid.shape[1]
    weights = up_pieces.arrays
    arrays = [grad_proj, grad_hid, x, stats, scales] + ([] if extra is None else [extra])

    def body(gp_ref, gh_ref, x_ref, stats_ref, scales_ref, *refs):
        if extra is not None:
            extra_ref, *refs = refs
        out_ref, sums_ref = refs[-2:]
        for k, up_tile in enumerate(up_pieces.tiles):
            ((which, start, _),) = up_tile
            wq = refs[which][start : start + tile, pl.ds(qkv_pieces.first, columns)]
            wu = refs[which][start : start + tile, pl.ds(up_pieces.first, units)]
            at = pl.ds(k * tile, tile)
            sums = [jnp.zeros((1, tile), F32)] * 4
            for row, rows in chunks(count, 256):
                span = pl.ds(row, rows)
                there = pl.ds(first * count + row, rows)
                one = times_transposed(gp_ref[there, :], wq)
                two = times_transposed(gh_ref[there, :], wu)
                xhat = (x_ref[span, at].astype(F32) - stats_ref[there, 0:1]) * stats_ref[there, 1:2]
                value = one * scales_ref[0:1, at] + two * scales_ref[2:3, at]
                if extra is not None:
                    value = value + extra_ref[span, at].astype(F32)
                out_ref[span, at] = value.astype(BF16)
                for n, term in enumerate((one * xhat, one, two * xhat, two)):
                    sums[n] = sums[n] + jnp.sum(term, axis=0, keepdims=True)
            sums_ref[:, at] = jnp.concatenate(sums, axis=0)

    return on_chip(
        body,
        "input_terms",
        arrays + weights,
        [((count, width), BF16), ((4, width), F32)],
        cost(
            4 * count * (columns + units) * width,
            2 * (columns + units) * (width + count) + 2 * count * width,
            2 * count * width,
        ),
    )


def weight_grad(left, right, extras=(), halves=False, kind=BF16):
    depth, rows = left.shape
    cols = right.shape[1]

    def body(l_ref, r_ref, *refs):
        extra_refs, outs = refs[: len(extras)], refs[len(extras) :]
        for row, size in chunks(rows, min(256, rows // 2)):
            value = left_transposed(l_ref[:, pl.ds(row, size)], r_ref[...])
            for ref, (array, first) in zip(extra_refs, extras):
                if first <= row < first + array.shape[0]:
                    value = value + ref[pl.ds(row - first, size), :].astype(F32)
            if halves:
                half = rows // 2
                outs[row // half][pl.ds(row % half, size), :] = value.astype(kind)
            else:
                outs[0][pl.ds(row, size), :] = value.astype(kind)

    shapes = [((rows // 2, cols), kind)] * 2 if halves else [((rows, cols), kind)]
    found = on_chip(
        body,
        "weight_grad",
        [left, right, *[e[0] for e in extras]],
        shapes,
        cost(4 * depth * rows * cols, 2 * depth * (rows + cols), rows * cols * 2),
    )
    return found if halves else found[0]


ANY = pl.BlockSpec(memory_space=pl.ANY)


def copies(name, scalars, arrays, shapes, moves):
    def body(at_ref, *refs):
        ins, outs, sems = refs[: len(arrays)], refs[len(arrays) : -1], refs[-1]
        jobs = [
            pltpu.make_async_copy(source, target, sems.at[n])
            for n, (source, target) in enumerate(moves(at_ref, ins, outs))
        ]
        for job in jobs:
            job.start()
        for job in jobs:
            job.wait()

    return pl.pallas_call(
        body,
        in_specs=[SMEM] + [ANY] * len(arrays),
        out_specs=[VMEM] * len(shapes),
        out_shape=[jax.ShapeDtypeStruct(shape, BF16) for shape in shapes],
        scratch_shapes=[pltpu.SemaphoreType.DMA((24,))],
        compiler_params=pltpu.CompilerParams(vmem_limit_bytes=48 * 1024 * 1024),
        cost_estimate=cost(0, 2 * sum(int(np.prod(shape)) for shape in shapes), 0),
        name=name,
    )(scalars, *arrays)


def rotary_tables(lengths, size):
    lanes, half = 128, ROT // 2
    power = -(np.arange(half, dtype=np.float32) * np.float32(2.0 / ROT))
    inverse = np.zeros((1, lanes), np.float32)
    inverse[0, :half] = inverse[0, half:ROT] = np.float32(10000.0) ** power
    count = len(lengths)

    def body(*refs):
        inverse_ref, cos_ref, before_ref, after_ref, begin_ref = refs[count:]
        for n in range(count):
            row = lax.broadcasted_iota(jnp.int32, (size, 1), 0)
            begin = jnp.zeros((size, 1), jnp.int32)
            start = jnp.int32(0)
            for k in range(lengths[n].shape[1]):
                begin = jnp.where(row >= start, start, begin)
                start = start + refs[n][0, k]
            angle = (row - begin).astype(F32) * inverse_ref[...]
            sine = jnp.sin(angle)
            lane = lax.broadcasted_iota(jnp.int32, (size, lanes), 1)
            cos_ref[n] = jnp.cos(angle)
            before_ref[n] = jnp.where(lane < half, -sine, 0.0)
            after_ref[n] = jnp.where((lane >= half) & (lane < ROT), sine, 0.0)
            begin_ref[n] = begin

    table = ((count, size, lanes), F32)
    *tables, begins = on_chip(
        body,
        "rotary_tables",
        [jnp.asarray(inverse)],
        [table, table, table, ((count, size, 1), jnp.int32)],
        cost(0, 0, 12 * count * size * lanes),
        lengths,
    )
    return tuple(tables), begins


def small_params(packed, at, spans, blocks, slice_rows):
    rows = packed.shape[0]
    first = np.cumsum([0] + spans)
    width = spans[2] * rows

    def body(at_ref, p_ref, qkv_ref, up_ref, out_ref, scales_ref, table):
        z, part, block = at_ref[0], at_ref[1], at_ref[2]
        table[...] = p_ref[...].astype(F32)
        qkv_ref[...] = table[pl.ds(2 * z + part, 1), : spans[0]]
        for k in range(blocks):
            columns = pl.ds(pl.multiple_of(first[1] + z * slice_rows, 128), slice_rows)
            up_ref[:, k * slice_rows : (k + 1) * slice_rows] = table[pl.ds(2 * k + part, 1), columns]
        each = spans[2]
        for i in range(rows):
            out_ref[:, i * each : (i + 1) * each] = (
                table[i : i + 1, first[2] : first[3]] + table[i : i + 1, first[3] : first[4]]
            )
        for off in range(blocks):
            for c in range(2):
                row = pl.ds(2 * (block ^ off) + c, 1)
                place = (off * 2 + c) * each
                for k in range(4):
                    scales_ref[k : k + 1, place : place + each] = table[row, first[4 + k] : first[5 + k]]

    return pl.pallas_call(
        body,
        in_specs=[SMEM, VMEM],
        out_specs=[VMEM] * 4,
        out_shape=[
            jax.ShapeDtypeStruct(shape, F32)
            for shape in ((1, spans[0]), (1, blocks * slice_rows), (1, width), (4, width))
        ],
        scratch_shapes=[pltpu.VMEM(packed.shape, F32)],
        compiler_params=pltpu.CompilerParams(vmem_limit_bytes=4 * 1024 * 1024),
        cost_estimate=cost(0, 0, 0),
        name="small_params",
    )(at, packed)


def copied(value):
    def body(from_ref, to_ref):
        to_ref[...] = from_ref[...]

    return on_chip(body, "copied", [value], [(value.shape, value.dtype)], cost(0, 0, 2 * value.size))[0]


def chip_pair(own, other, at):
    rows, columns = own.shape

    def body(at_ref, own_ref, other_ref, out_ref):
        part = at_ref[1]
        out_ref[pl.ds(pl.multiple_of(part * rows, rows), rows), :] = own_ref[...]
        out_ref[pl.ds(pl.multiple_of((1 - part) * rows, rows), rows), :] = other_ref[...]

    return on_chip(
        body, "chip_pair", [own, other], [((2 * rows, columns), BF16)], cost(0, 0, 0), [at]
    )[0]


class Place:
    def __init__(self):
        self.n_dp = lax.axis_size("dp")
        self.n_seq = lax.axis_size("seq")
        assert self.n_dp == 2 * self.n_seq
        self.split = 2 if H % (2 * self.n_seq) == 0 else 1
        self.blocks = self.n_dp // self.split
        self.dp = lax.axis_index("dp")
        self.z = lax.axis_index("seq")
        self.block = self.dp // self.split
        self.part = self.dp % self.split
        self.at = jnp.stack([self.z, self.part, self.block]).astype(jnp.int32)
        self.masks = [1 << k for k in range(self.blocks.bit_length() - 1)]
        self.order = list(range(self.blocks))
        self.paired = self.split == 2 and self.blocks == 4

    def swap(self, value, mask):
        return lax.ppermute(value, "dp", [(i, i ^ mask) for i in range(self.n_dp)])

    def to_relative(self, value, axis):
        size = value.shape[axis] // self.blocks
        return jnp.concatenate(
            [
                lax.dynamic_slice_in_dim(value, (self.block ^ off) * size, size, axis)
                for off in self.order
            ],
            axis=axis,
        )

    def to_natural(self, value, axis):
        return self.to_relative(value, axis)

    def pair(self, own, other, axis):
        return jnp.where(
            self.part == 0,
            jnp.concatenate([own, other], axis=axis),
            jnp.concatenate([other, own], axis=axis),
        )

    def gather(self, piece):
        half = piece.shape[0] // 2
        gathered = []
        for rows, masks in ((piece[:half], self.masks), (piece[half:], self.masks[::-1])):
            have = {0: rows}
            for mask in masks:
                offs = list(have)
                sent = jnp.concatenate([have[o] for o in offs], 0) if len(offs) > 1 else have[offs[0]]
                got = self.swap(sent, mask * self.split)
                for k, o in enumerate(offs):
                    have[o ^ mask] = got[k * half : (k + 1) * half]
            gathered.append(have)
        return gathered

    def scatter_sum(self, product, halves):
        out = []
        for half, masks in zip(halves, (self.masks, self.masks[::-1])):
            live = list(range(self.blocks))
            extra = {}

            def total(offs):
                whole = product(half, offs)
                if all(o not in extra for o in offs):
                    return whole
                axis, size = whole.ndim and product.axis, whole.shape[product.axis] // len(offs)
                parts = []
                for k, o in enumerate(offs):
                    value = lax.slice_in_dim(whole, k * size, (k + 1) * size, axis=axis)
                    for more in extra.get(o, ()):
                        value = value + more.astype(F32)
                    parts.append(value)
                return parts[0] if len(parts) == 1 else jnp.concatenate(parts, axis=axis)

            for mask in masks:
                away = [o for o in self.order if o in live and o & mask]
                sent = total(away).astype(BF16)
                got = self.swap(sent, mask * self.split)
                size = got.shape[product.axis] // len(away)
                for k, o in enumerate(away):
                    extra.setdefault(o ^ mask, []).append(
                        lax.slice_in_dim(got, k * size, (k + 1) * size, axis=product.axis)
                    )
                live = [o for o in live if not o & mask]
            out.append(total([0]))
        return out


class Product:
    def __init__(self, place, by_block, other, axis):
        self.place, self.by_block, self.other, self.axis = place, by_block, other, axis
        self.size = by_block.shape[1] // place.blocks

    def __call__(self, half, offs):
        where = [self.place.order.index(o) for o in offs]
        if where == list(range(where[0], where[0] + len(where))):
            blocks = self.by_block[:, where[0] * self.size : (where[-1] + 1) * self.size]
        else:
            blocks = jnp.concatenate(
                [self.by_block[:, w * self.size : (w + 1) * self.size] for w in where], axis=1
            )
        width = self.other.shape[1] // 2
        others = self.other[:, half * width : (half + 1) * width]
        if self.axis == 0:
            return left_transposed(blocks, others)
        return left_transposed(others, blocks)


class Chain:
    def __init__(self):
        self.last = None

    def __call__(self, *values):
        if self.last is not None:
            values = tuple(lax.optimization_barrier((values, self.last))[0])
        return values if len(values) > 1 else values[0]

    def done(self, value):
        self.last = value
        return value

    def wait(self, value):
        if value is not None:
            self.last = (self.last, value)


class Gathered:
    def __init__(self, here, piece):
        self.here, self.piece = here, piece
        self.half = piece.shape[0] // 2

    def send(self):
        here = self.here
        if here.paired:
            self.by_x, self.by_y = here.swap(self.piece, 2), here.swap(self.piece, 4)
            return self.by_x, self.by_y

    def hand_on(self, chain):
        if self.here.paired:
            half = self.half
            columns = self.piece.shape[1]

            def body(x_ref, y_ref, first_ref, second_ref):
                first_ref[...] = x_ref[:half, :]
                second_ref[...] = y_ref[half:, :]

            first, second = on_chip(
                body,
                "hand_on",
                chain(self.by_x, self.by_y),
                [((half, columns), BF16)] * 2,
                cost(0, 0, 4 * half * columns),
            )
            chain.done((first, second))
            self.handed = (self.here.swap(first, 4), self.here.swap(second, 2))
            return self.handed

    def rows(self, size, moving, columns=None):
        here, block = self.here, self.piece.shape[0]
        if here.paired:
            arrays = [self.piece, self.by_x, self.by_y, *self.handed]
            tiles, now, left = [], [], size
            for which, count in enumerate([block] * 3 + [self.half] * 2):
                first = 0
                while count:
                    take = min(left, count)
                    now.append((which, first, take))
                    first, count, left = first + take, count - take, left - take
                    if not left:
                        tiles.append(now)
                        now, left = [], size
            blocks = None
            if moving:
                assert size == block
                blocks = here.block ^ jnp.arange(here.blocks, dtype=jnp.int32)
            return Pieces(arrays, tiles, size, blocks, columns)
        if not hasattr(self, "whole"):
            halves = here.gather(self.piece)
            whole = jnp.concatenate([half[o] for o in range(here.blocks) for half in halves], axis=0)
            self.whole = here.to_natural(whole, 0) if moving else whole
        count = self.whole.shape[0] // size
        blocks = jnp.arange(count, dtype=jnp.int32) if moving else None
        return Pieces([self.whole], [[(0, k * size, size)] for k in range(count)], size, blocks, columns)


class Spread:
    def __init__(self, here, piece):
        self.here, self.step = here, 0
        chips = here.n_dp // 2
        masks = [1 << k for k in range(chips.bit_length() - 1)]
        self.steps = len(masks)
        self.offset = (here.dp // 2) ^ here.z
        self.states = [(piece[0], masks, [0]), (piece[1], masks[::-1], [0])]

    def send(self):
        here, self.got = self.here, []
        for rows, order, held in self.states:
            pairs = [
                (
                    (2 * (z ^ o) + c) * here.n_seq + z,
                    (2 * (z ^ o ^ order[self.step]) + c) * here.n_seq + z,
                )
                for z in range(here.n_seq)
                for o in held
                for c in range(2)
            ]
            self.got.append(lax.ppermute(rows, ("dp", "seq"), pairs))
        return tuple(self.got)

    def take(self, chain):
        got = chain(*self.got)
        after = []
        for new, (rows, order, held) in zip(got, self.states):
            takes = jnp.zeros((), jnp.bool_)
            for o in held:
                takes = takes | (self.offset == (o ^ order[self.step]))
            after.append(
                (
                    jnp.where(takes, new, rows),
                    order,
                    held + [o ^ order[self.step] for o in held],
                )
            )
        self.states = after
        self.step += 1
        chain.done(tuple(state[0] for state in after))

    def finish(self, chain):
        self.take(chain)
        here = self.here
        rows = jnp.concatenate([state[0] for state in self.states], axis=0)
        if here.split == 1:
            other = here.swap(rows, 1)
            rows = jnp.where(
                here.dp % 2 == 0,
                jnp.concatenate([rows, other], 0),
                jnp.concatenate([other, rows], 0),
            )
        return rows


class Scattered:
    def __init__(self, here, left, right):
        self.here, self.left, self.right = here, left, right
        self.axis = 0 if isinstance(left, (list, tuple)) else 1

    def part(self, off, **more):
        if self.axis == 0:
            return weight_grad(self.left[off], self.right, **more)
        return weight_grad(self.left, self.right[off], **more)

    def first(self, chain):
        if self.here.paired:
            if self.axis == 0:
                self.right = chain(self.right)
            else:
                self.left = chain(self.left)
            one, two = chain.done(self.part(3, halves=True))
            self.by_x, self.by_y = self.here.swap(one, 2), self.here.swap(two, 4)
            return self.by_x, self.by_y

    def second(self, chain):
        if self.here.paired:
            by_x, by_y = chain(self.by_x, self.by_y)
            half = by_x.shape[0]
            to_x = self.part(1, extras=((by_y, half),))
            to_y = self.part(2, extras=((by_x, 0),))
            chain.done((to_x, to_y))
            self.by_x, self.by_y = self.here.swap(to_x, 2), self.here.swap(to_y, 4)
            return self.by_x, self.by_y

    def last(self, chain, kind):
        if self.here.paired:
            by_x, by_y = chain(self.by_x, self.by_y)
            return chain.done(self.part(0, extras=((by_x, 0), (by_y, 0)), kind=kind))
        if self.axis == 1:
            product = Product(self.here, jnp.concatenate(self.right, axis=1), self.left, 1)
        else:
            product = Product(self.here, jnp.concatenate(self.left, axis=1), self.right, 0)
        halves = self.here.scatter_sum(product, (0, 1))
        return jnp.concatenate(halves, axis=1 - self.axis).astype(kind)


def on_device(
    tokens,
    doc_lengths,
    qkv_weight,
    qkv_bias,
    dense_weight,
    dense_bias,
    up_weight,
    up_bias,
    down_weight,
    down_bias,
    norm1_gain,
    norm1_shift,
    norm2_gain,
    norm2_shift,
    cotangent,
):
    here = Place()
    chain = Chain()
    n_dp, n_seq, split, blocks = here.n_dp, here.n_seq, here.split, here.blocks
    z, part = here.z, here.part
    rows_here, width = tokens.shape
    seq_len = rows_here * n_seq
    hidden_rows = down_weight.shape[0]
    slice_rows = hidden_rows // n_seq
    assert H == n_seq * split
    head_cols = 3 * HS

    def column_places(core):
        head = (z * split + core) * head_cols
        return head, [(k * split + core) * hidden_rows + z * slice_rows for k in range(blocks)]

    half_dense = dense_weight.shape[0] // 2
    wide_cols = head_cols + blocks * slice_rows
    if here.paired:
        size = width // blocks

        def moves(at, ins, outs):
            tokens_in, qkv_in, up_in, down_in, dense_in = ins
            plane, core, block = at[0], at[1], at[2]
            jobs = []
            for off in range(blocks):
                place = pl.multiple_of((block ^ off) * size, size)
                jobs.append((tokens_in.at[:, pl.ds(place, size)], outs[0].at[:, off * size : (off + 1) * size]))
            for out, its in ((outs[1], 1 - core), (outs[2], core)):
                place = pl.multiple_of((plane * split + its) * head_cols, 128)
                jobs.append((qkv_in.at[:, pl.ds(place, head_cols)], out.at[:, :head_cols]))
                for k in range(blocks):
                    place = pl.multiple_of((k * split + its) * hidden_rows + plane * slice_rows, 128)
                    to = head_cols + k * slice_rows
                    jobs.append((up_in.at[:, pl.ds(place, slice_rows)], out.at[:, to : to + slice_rows]))
            place = pl.multiple_of(plane * slice_rows, slice_rows)
            jobs.append((down_in.at[pl.ds(place, slice_rows), :], outs[3]))
            jobs.append((dense_in.at[:half_dense], outs[4]))
            jobs.append((dense_in.at[half_dense:], outs[5]))
            return jobs

        shapes = [tokens.shape] + [(qkv_weight.shape[0], wide_cols)] * 2 + [(slice_rows, width)]
        shapes = shapes + [(half_dense, width)] * 2
        tokens_rel, wide_other, wide_piece, down_piece, *dense_halves = chain.done(
            copies(
                "first_copies",
                here.at,
                (tokens, qkv_weight, up_weight, down_weight, dense_weight),
                shapes,
                moves,
            )
        )
        got = here.swap(wide_other, 1)
    else:
        tokens_rel = here.to_relative(tokens, 1)
        head, places = column_places(part)
        wide_piece = jnp.concatenate(
            [lax.dynamic_slice_in_dim(qkv_weight, head, head_cols, 1)]
            + [lax.dynamic_slice_in_dim(up_weight, place, slice_rows, 1) for place in places],
            axis=1,
        )
        down_piece = lax.dynamic_slice_in_dim(down_weight, z * slice_rows, slice_rows, 0)
        dense_halves = dense_weight[:half_dense], dense_weight[half_dense:]
    x_own = lax.all_gather(tokens_rel, "seq", axis=0, tiled=True)
    g_own = lax.all_gather(chain(cotangent), "seq", axis=0, tiled=True)
    dense_rows = Spread(here, dense_halves)
    dense_pair = dense_rows.send()
    small = (qkv_bias, up_bias, dense_bias, down_bias, norm1_gain, norm1_shift, norm2_gain, norm2_shift)
    packed_small = chain.done(jnp.concatenate(chain(*small)))
    packed_small = jnp.broadcast_to(packed_small[None], (n_dp,) + packed_small.shape)
    packed_small = lax.all_to_all(packed_small, "dp", 0, 0, tiled=True)
    lengths = [doc_lengths] + ([here.swap(doc_lengths, 1)] if split == 2 else [])
    if here.paired:
        wide_piece = chain.done(chip_pair(chain(wide_piece), got, here.at))
    wide_rows = Gathered(here, wide_piece)
    wide_pair = wide_rows.send()
    lengths = [chain(v) for v in lengths]
    tables, begins = chain.done(rotary_tables(lengths, seq_len))
    spans = [v.shape[0] for v in small]

    chain.wait(dense_pair)
    while dense_rows.step < dense_rows.steps - 1:
        dense_rows.take(chain)
        dense_pair = dense_rows.send()
        chain.wait(dense_pair)
    chain.wait(wide_pair)
    wide_pair = wide_rows.hand_on(chain)
    down_rows = Gathered(here, chain(down_piece))
    down_pair = down_rows.send()
    w_dense = dense_rows.finish(chain)
    if here.paired:
        b_qkv, b_up, b_out, scales = chain.done(
            small_params(chain(packed_small), here.at, spans, blocks, slice_rows)
        )
    else:
        pieces, first = [], 0
        for span in spans:
            pieces.append(packed_small[:, first : first + span].astype(F32))
            first += span
        b_qkv, b_up, b_dense, b_down = pieces[:4]
        head = (z * split + part) * head_cols
        b_qkv = lax.dynamic_slice_in_dim(b_qkv.reshape(1, -1), head, head_cols, 1)
        b_up = lax.dynamic_slice_in_dim(b_up, z * slice_rows, slice_rows, 1)
        b_up = b_up.reshape(blocks, split, slice_rows)
        b_up = lax.dynamic_index_in_dim(b_up, part, 1, keepdims=False).reshape(1, -1)
        b_out = (b_dense + b_down).reshape(1, -1)
        scales = here.to_relative(jnp.stack([v.reshape(-1) for v in pieces[4:]]), 1)
    streams = [x_own] + ([here.swap(chain(x_own), 1)] if split == 2 else [])
    normed = chain.done(two_norms(chain(*streams) if split == 2 else streams, scales, blocks))
    normed_one, normed_two, stats = normed[:blocks], normed[blocks:-1], normed[-1]
    chain.wait(wide_pair)
    g_own = chain(g_own)
    streams_g = [g_own] + ([here.swap(g_own, 1)] if split == 2 else [])
    qkv_pieces = wide_rows.rows(256, False, (0, head_cols))
    up_pieces = wide_rows.rows(256, False, (head_cols, blocks * slice_rows))
    activated, slope = chain.done(feed_up(normed_two, up_pieces, chain(b_up)))
    qkv, probs, attended = chain.done(
        attention_forward(normed_one, qkv_pieces, chain(b_qkv), tables, begins)
    )
    attended = attended.reshape(split * seq_len, HS)
    chain.wait(down_pair)

    down_pair = down_rows.hand_on(chain)
    g_blocks = chain.done(cotangent_blocks(chain(*streams_g) if split == 2 else streams_g, here.at, blocks))
    sum_down = Scattered(here, activated, g_blocks)
    sum_dense = Scattered(here, attended, g_blocks)
    pair_down = sum_down.first(chain)
    grad_projected, grad_qkv_bias = chain.done(
        attention_backward(chain(qkv), probs, g_blocks, w_dense, tables, here.at)
    )
    grad_projected = grad_projected.reshape(split * seq_len, head_cols)
    sum_qkv = Scattered(here, normed_one, grad_projected)
    chain.wait(down_pair)
    pair_qkv = sum_qkv.first(chain)
    down_pieces = down_rows.rows(down_piece.shape[0] if here.paired else 256, True)

    def join(value):
        return lax.psum_scatter(value, "seq", scatter_dimension=0, tiled=True).astype(F32)

    def branches(first, extra=None):
        return chain.done(
            branch_rows_of(chain(attended), w_dense, activated, down_pieces, first, seq_len, extra)
        )

    def terms(first, extra=None):
        return chain.done(
            input_terms(
                chain(grad_projected),
                qkv_pieces,
                grad_hidden,
                up_pieces,
                streams[first],
                stats,
                scales,
                first,
                extra,
            )
        )

    branch_other = branches(1) if split == 2 else None
    chain.wait(pair_down)
    chain.wait(pair_qkv)
    if split == 2:
        branch_other = here.swap(chain(branch_other), 1)
    branch_rows = join(branches(0, branch_other))
    pair_down = sum_down.second(chain)
    pair_dense = sum_dense.first(chain)
    grad_hidden, grad_up_bias = chain.done(hidden_grad(g_blocks, down_pieces, chain(slope), here.at))
    sum_up = Scattered(here, normed_two, grad_hidden)
    term_other, norm_sums = None, jnp.zeros((4, width), F32)
    if split == 2:
        term_other, norm_sums = terms(1)
    chain.wait(pair_dense)
    chain.wait(pair_down)
    sum_down_last = sum_down.last(chain, BF16)
    if split == 2:
        term_other = here.swap(chain(term_other), 1)
    pair_up = sum_up.first(chain)
    pair_dense = sum_dense.second(chain)
    term_own, more_sums = terms(0, term_other)
    norm_sums = norm_sums + more_sums

    norm_sums = here.to_natural(chain(norm_sums), 1)
    wide_qkv = lax.dynamic_update_slice_in_dim(
        jnp.zeros((H * head_cols,), F32), grad_qkv_bias.reshape(-1), (z * split + part) * head_cols, 0
    )
    wide_up = lax.dynamic_update_slice(
        jnp.zeros((blocks, split, n_seq, slice_rows), F32),
        grad_up_bias.reshape(blocks, 1, 1, slice_rows),
        (0, part, z, 0),
    )
    cotan_rows = cotangent.astype(F32)
    column_total = jnp.sum(cotan_rows, axis=0)
    devices = n_dp * n_seq
    wide = [wide_qkv, wide_up, column_total] + [norm_sums[k] for k in range(4)]
    wide = [v.reshape(devices, -1) for v in wide]
    sizes = [v.shape[1] for v in wide]
    swapped = lax.all_to_all(
        chain.done(jnp.concatenate(wide, axis=1)), ("dp", "seq"), split_axis=0, concat_axis=0, tiled=True
    )

    chain.wait(pair_up)
    chain.wait(pair_dense)
    term_rows = join(chain.done(copied(chain(term_own))))
    pair_up = sum_up.second(chain)
    pair_qkv = sum_qkv.second(chain)
    sum_dense_last = sum_dense.last(chain, F32)
    output = chain.done((chain(branch_rows) + tokens.astype(F32) + b_out).astype(BF16))
    chain.wait(pair_up)
    chain.wait(pair_qkv)
    chain.wait(swapped)
    sum_up_last = sum_up.last(chain, BF16)
    sum_qkv_last = sum_qkv.last(chain, F32)

    values = tokens_rel.astype(F32)
    centred = values - jnp.mean(values, axis=-1, keepdims=True)
    inverse = lax.rsqrt(jnp.mean(centred * centred, axis=-1, keepdims=True) + 1e-05)
    xhat = centred * inverse
    term_rows = chain(term_rows)
    term = (
        term_rows
        - jnp.mean(term_rows, axis=-1, keepdims=True)
        - xhat * jnp.mean(term_rows * xhat, axis=-1, keepdims=True)
    ) * inverse
    input_grad = chain.done((cotan_rows + here.to_natural(term, 1)).astype(BF16))
    total = jnp.sum(swapped, axis=0)
    sums, first = [], 0
    for size in sizes:
        sums.append(total[first : first + size])
        first += size
    sum_qkv_bias, sum_up_bias, sum_column, sum_gain_one, sum_shift_one, sum_gain_two, sum_shift_two = sums

    def to_plane(whole, axis):
        moved = lax.all_to_all(whole, "seq", split_axis=axis, concat_axis=axis, tiled=True)
        if split == 1:
            per = moved.shape[axis] // (n_seq * 2)
            if axis == 0:
                moved = moved.reshape(n_seq, 2, per, -1).transpose(1, 0, 2, 3).reshape(moved.shape)
            else:
                moved = moved.reshape(-1, n_seq, 2, per).transpose(0, 2, 1, 3).reshape(moved.shape)
        return moved

    def to_cores(value, axis):
        if split == 1:
            return value.astype(F32)
        size = value.shape[axis] // 2
        mine = lax.dynamic_slice_in_dim(value, part * size, size, axis)
        other = lax.dynamic_slice_in_dim(value, (1 - part) * size, size, axis)
        return here.pair(mine, here.swap(other, 1), 1 - axis).astype(F32)

    grad_down = to_cores(to_plane(sum_down_last, 0), 1)
    grad_dense = to_cores(sum_dense_last, 1)
    grad_up = to_cores(to_plane(sum_up_last, 1), 0)
    grad_qkv = to_cores(sum_qkv_last, 0)

    return (
        output,
        input_grad,
        grad_qkv,
        sum_qkv_bias,
        grad_dense,
        sum_column,
        grad_up,
        sum_up_bias,
        grad_down,
        sum_column,
        sum_gain_one,
        sum_shift_one,
        sum_gain_two,
        sum_shift_two,
    )


def solution(mesh):
    rows = P(("dp", "seq"), None)
    flat = P(("dp", "seq"))
    placed = (rows,) + (P("dp", None),) * 2 + (P("dp"), P("dp", None)) * 3 + (P("dp"),) * 5 + (rows,)
    return jax.shard_map(
        on_device,
        mesh=mesh,
        in_specs=placed,
        out_specs=(
            rows,
            rows,
            P("dp", "seq"),
            flat,
            P("seq", "dp"),
            flat,
            P("dp", "seq"),
            flat,
            P("seq", "dp"),
            flat,
            flat,
            flat,
            flat,
            flat,
        ),
        check_vma=False,
    )
```

```python
import jax
import jax.numpy as jnp
import numpy as np
from jax import lax
from jax.experimental import pallas as pl
from jax.experimental.pallas import tpu as pltpu
from jax.sharding import PartitionSpec as P

H = 8
HS = 256
ROT = 64
HINT = 1.0
LIMIT = 16 * 1024 * 1024
F32 = jnp.float32
BF16 = jnp.bfloat16


def matmul(left, right):
    return jnp.dot(left, right, preferred_element_type=F32)


def times_transposed(left, right):
    return lax.dot_general(left, right, (((1,), (1,)), ((), ())), preferred_element_type=F32)


def left_transposed(left, right):
    return lax.dot_general(left, right, (((0,), (0,)), ((), ())), preferred_element_type=F32)


def cost(flops, reads, writes, transcendentals=0):
    return pl.CostEstimate(
        flops=int(flops * HINT),
        bytes_accessed=int((reads + writes) * HINT),
        transcendentals=int(transcendentals * HINT),
    )


VMEM = pl.BlockSpec(memory_space=pltpu.VMEM)
SMEM = pl.BlockSpec(memory_space=pltpu.SMEM)


def on_chip(body, name, arrays, shapes, estimate, scalars=()):
    return pl.pallas_call(
        body,
        in_specs=[SMEM] * len(scalars) + [VMEM] * len(arrays),
        out_specs=[VMEM] * len(shapes),
        out_shape=[jax.ShapeDtypeStruct(*shape) for shape in shapes],
        compiler_params=pltpu.CompilerParams(vmem_limit_bytes=LIMIT),
        cost_estimate=estimate,
        name=name,
    )(*scalars, *arrays)


def each(total, size, step):
    if total <= size:
        return step(0)

    @pl.loop(0, total // size)
    def _(i):
        step(pl.multiple_of(i * size, size))


def chunks(total, size):
    return [(at, min(size, total - at)) for at in range(0, total, size)]


def two_norms(arrays, scales, blocks):
    rows, width = arrays[0].shape
    total = rows * len(arrays)
    tile = 32

    size = width // blocks

    def body(scales_ref, *refs):
        ones, twos, stats_ref = refs[len(arrays) : -1 - blocks], refs[-1 - blocks : -1], refs[-1]
        for k in range(len(arrays)):

            @pl.loop(0, rows // tile)
            def _(i, k=k):
                values = refs[k][pl.ds(pl.multiple_of(i * tile, tile), tile), :].astype(F32)
                average = jnp.mean(values, axis=-1, keepdims=True)
                centred = values - average
                variance = jnp.mean(centred * centred, axis=-1, keepdims=True)
                inverse = lax.rsqrt(variance + 1e-05)
                xhat = centred * inverse
                span = pl.ds(pl.multiple_of(k * rows + i * tile, tile), tile)
                one = (xhat * scales_ref[0:1, :] + scales_ref[1:2, :]).astype(BF16)
                two = (xhat * scales_ref[2:3, :] + scales_ref[3:4, :]).astype(BF16)
                for n in range(blocks):
                    ones[n][span, :] = one[:, n * size : (n + 1) * size]
                    twos[n][span, :] = two[:, n * size : (n + 1) * size]
                stats_ref[span, :] = jnp.concatenate([average, inverse], axis=1)

    return on_chip(
        body,
        "two_norms",
        [scales, *arrays],
        [((total, size), BF16)] * (2 * blocks) + [((total, 2), F32)],
        cost(total * width * 24, total * width * 2, total * width * 4),
    )


class Pieces:
    def __init__(self, arrays, tiles, size, blocks=None, columns=None):
        self.arrays, self.tiles, self.size, self.blocks = arrays, tiles, size, blocks
        self.first, self.width = columns or (0, arrays[0].shape[1])

    def inside(self, size):
        cut = []
        for which, first, count, k, place in self.runs():
            start = k * self.size + place
            while count:
                take = min(count, size - start % size)
                cut.append((which, first, take, start // size, start % size))
                first, start, count = first + take, start + take, count - take
        return cut

    def runs(self):
        found = []
        for k, tile in enumerate(self.tiles):
            at = 0
            for which, first, count in tile:
                last = found[-1] if found else None
                joins = last and self.blocks is None and last[0] == which and last[1] + last[2] == first
                if joins:
                    found[-1] = (which, last[1], last[2] + count, last[3], last[4])
                else:
                    found.append((which, first, count, k, at))
                at += count
        return found


def feed_up(x, pieces, b):
    rows, size = x[0].shape
    width = size * len(x)
    units = pieces.width

    def body(b_ref, *refs):
        x_refs, w_refs, (act_ref, slope_ref) = refs[: len(x)], refs[len(x) : -2], refs[-2:]
        def step(row):
            for col, cols in chunks(units, 512):
                at = (pl.ds(row, min(256, rows)), pl.ds(col, cols))
                hidden = b_ref[:, at[1]]
                for which, first, depth, k, place in pieces.inside(size):
                    hidden = hidden + matmul(
                        x_refs[k][at[0], place : place + depth],
                        w_refs[which][first : first + depth, pl.ds(pieces.first + col, cols)],
                    )
                cdf = 0.5 + 0.5 * lax.erf(hidden * (0.5**0.5))
                act_ref[at] = (hidden * cdf).astype(BF16)
                slope_ref[at] = cdf + hidden * (jnp.exp(-0.5 * hidden * hidden) * 0.3989422804014327)

        each(rows, 256, step)

    return on_chip(
        body,
        "feed_up",
        [b, *x, *pieces.arrays],
        [((rows, units), BF16), ((rows, units), F32)],
        cost(4 * rows * width * units, 2 * (rows + units) * width, 6 * rows * units, 2 * rows * units),
    )


def cotangent_blocks(streams, at, blocks):
    rows, width = streams[0].shape
    size = width // blocks

    def body(at_ref, *refs):
        ins, outs = refs[: len(streams)], refs[len(streams) :]
        for off in range(blocks):
            place = pl.ds(pl.multiple_of((at_ref[2] ^ off) * size, 128), size)
            for n in range(len(streams)):
                outs[off][n * rows : (n + 1) * rows, :] = ins[n][:, place]

    return on_chip(
        body,
        "cotangent_blocks",
        streams,
        [((rows * len(streams), size), BF16)] * blocks,
        cost(0, rows * width * 4, rows * width * 4),
        [at],
    )


def hidden_grad(g, pieces, slope, at):
    rows, size = g[0].shape
    width = size * len(g)
    units = slope.shape[1]

    def body(blocks_ref, at_ref, slope_ref, *refs):
        g_refs, w_refs, (out_ref, sum_ref) = refs[: len(g)], refs[len(g) : -2], refs[-2:]
        for which, first, count, k, place in pieces.runs():
            columns = pl.ds(pl.multiple_of(blocks_ref[k] * pieces.size + place, 128), count)
            total = jnp.zeros((1, count), F32)
            for row, tall in chunks(rows, 256):
                span = pl.ds(row, tall)
                value = jnp.zeros((tall, count), F32)
                for off in range(len(g)):
                    block = pl.ds(pl.multiple_of((at_ref[2] ^ off) * size, 128), size)
                    value = value + times_transposed(
                        g_refs[off][span, :], w_refs[which][first : first + count, block]
                    )
                value = (value * slope_ref[span, columns]).astype(BF16)
                out_ref[span, columns] = value
                total = total + jnp.sum(value.astype(F32), axis=0, keepdims=True)
            sum_ref[:, columns] = total

    return on_chip(
        body,
        "hidden_grad",
        [slope, *g, *pieces.arrays],
        [((rows, units), BF16), ((1, units), F32)],
        cost(4 * rows * width * units, 2 * (rows + units) * width + 4 * rows * units, 2 * rows * units),
        [pieces.blocks, at],
    )


def turn(values, cosine, before, after, sign):
    lanes = cosine.shape[1]
    half = ROT // 2
    first = values[:, :lanes]
    first = first * cosine + sign * (
        pltpu.roll(first, lanes - half, 1) * before + pltpu.roll(first, half, 1) * after
    )
    return jnp.concatenate([first, values[:, lanes:]], axis=1)


def attention_forward(x, pieces, bias, tables, begins):
    count, size = tables[0].shape[:2]
    part = x[0].shape[1]
    width = part * len(x)
    columns = bias.shape[1]

    def body(b_ref, cos_ref, before_ref, after_ref, begin_ref, *refs):
        x_refs, w_refs, (qkv_ref, probs_ref, out_ref) = refs[: len(x)], refs[len(x) : -3], refs[-3:]
        @pl.loop(0, count)
        def _(n):
            turns = (cos_ref[n], before_ref[n], after_ref[n])
            projected = b_ref[...]
            for which, first, rows, k, place in pieces.inside(part):
                projected = projected + matmul(
                    x_refs[k][pl.ds(pl.multiple_of(n * size, size), size), place : place + rows],
                    w_refs[which][first : first + rows, pl.ds(pieces.first, columns)],
                )
            queries = turn(projected[:, :HS], *turns, 1.0).astype(BF16)
            keys = turn(projected[:, HS : 2 * HS], *turns, 1.0).astype(BF16)
            values = projected[:, 2 * HS :].astype(BF16)
            qkv_ref[n, :, :HS] = queries
            qkv_ref[n, :, HS : 2 * HS] = keys
            qkv_ref[n, :, 2 * HS :] = values
            for row, tile in chunks(size, 256):
                rows = slice(row, row + tile)
                scores = times_transposed(queries[rows], keys) * (HS**-0.5)
                places = lax.broadcasted_iota(jnp.int32, (tile, size), 1)
                here = lax.broadcasted_iota(jnp.int32, (tile, size), 0) + row
                allowed = (places >= begin_ref[n, rows, :]) & (places <= here)
                masked = jnp.where(allowed, scores, -1e30)
                exponent = jnp.exp(masked - jnp.max(masked, axis=-1, keepdims=True))
                probs = exponent / jnp.sum(exponent, axis=-1, keepdims=True)
                probs_ref[n, rows, :] = probs
                out_ref[n, rows, :] = matmul(probs.astype(BF16), values).astype(BF16)

    return on_chip(
        body,
        "attention_forward",
        [bias, *tables, begins, *x, *pieces.arrays],
        [
            ((count, size, columns), BF16),
            ((count, size, size), F32),
            ((count, size, HS), BF16),
        ],
        cost(
            count * size * (size * HS * 8 + 4 * width * columns),
            count * size * width * 2,
            count * size * (columns * 2 + size * 4),
            count * size * size,
        ),
    )


def attention_backward(qkv, probs, g, w_dense, tables, at):
    count, size, columns = qkv.shape
    scale = HS**-0.5
    part = g[0].shape[1]

    def body(at_ref, qkv_ref, probs_ref, w_ref, cos_ref, before_ref, after_ref, *refs):
        g_refs, (out_ref, sum_ref) = refs[:-2], refs[-2:]
        sum_ref[...] = jnp.zeros((1, columns), F32)

        @pl.loop(0, count)
        def _(n):
            turns = (cos_ref[n], before_ref[n], after_ref[n])
            queries = qkv_ref[n, :, :HS]
            keys = qkv_ref[n, :, HS : 2 * HS]
            values = qkv_ref[n, :, 2 * HS :]
            grad = jnp.zeros((size, HS), F32)
            for off in range(len(g)):
                block = pl.ds(pl.multiple_of((at_ref[2] ^ off) * part, 128), part)
                grad = grad + times_transposed(g_refs[off][pl.ds(pl.multiple_of(n * size, size), size), :], w_ref[:, block])
            grad = grad.astype(BF16)
            probs_now = probs_ref[n]
            grad_probs = times_transposed(grad, values)
            inner = jnp.sum(probs_now * grad_probs, axis=-1, keepdims=True)
            grad_scores = (probs_now * (grad_probs - inner)).astype(BF16)
            grad_queries = turn(matmul(grad_scores, keys) * scale, *turns, -1.0).astype(BF16)
            grad_keys = turn(left_transposed(grad_scores, queries) * scale, *turns, -1.0).astype(BF16)
            grad_values = left_transposed(probs_now.astype(BF16), grad).astype(BF16)
            whole = jnp.concatenate([grad_queries, grad_keys, grad_values], axis=1)
            out_ref[n] = whole
            sum_ref[...] += jnp.sum(whole.astype(F32), axis=0, keepdims=True)

    return on_chip(
        body,
        "attention_backward",
        [qkv, probs, w_dense, *tables, *g],
        [((count, size, columns), BF16), ((1, columns), F32)],
        cost(
            count * size * (size * HS * 16 + 4 * HS * part * len(g)),
            count * size * (columns * 4 + size * 4),
            count * size * columns * 2,
        ),
        [at],
    )


def branch_rows_of(attended, w_dense, activated, pieces, first, count, extra=None):
    width = w_dense.shape[1]
    inner, units = attended.shape[1], activated.shape[1]
    arrays = [attended, w_dense, activated] + ([] if extra is None else [extra])

    def body(blocks_ref, a_ref, wa_ref, b_ref, *refs):
        if extra is not None:
            extra_ref, *refs = refs
        for row, rows in chunks(count, 256):
            span = pl.ds(first * count + row, rows)
            for col, cols in chunks(width, 512):
                at = pl.ds(col, cols)
                value = matmul(a_ref[span, :], wa_ref[:, at])
                for which, start, depth, k, place in pieces.runs():
                    columns = pl.ds(pl.multiple_of(blocks_ref[k] * pieces.size + place, 128), depth)
                    value = value + matmul(b_ref[span, columns], refs[which][start : start + depth, at])
                if extra is not None:
                    value = value + extra_ref[pl.ds(row, rows), at].astype(F32)
                refs[-1][pl.ds(row, rows), at] = value.astype(BF16)

    return on_chip(
        body,
        "branch_rows",
        arrays + pieces.arrays,
        [((count, width), BF16)],
        cost(4 * count * (inner + units) * width, 2 * (inner + units) * (width + count), 2 * count * width),
        [pieces.blocks],
    )[0]


def input_terms(grad_proj, qkv_pieces, grad_hid, up_pieces, x, stats, scales, first, extra=None):
    count, width = x.shape
    tile = up_pieces.size
    columns, units = grad_proj.shape[1], grad_hid.shape[1]
    weights = up_pieces.arrays
    arrays = [grad_proj, grad_hid, x, stats, scales] + ([] if extra is None else [extra])

    def body(gp_ref, gh_ref, x_ref, stats_ref, scales_ref, *refs):
        if extra is not None:
            extra_ref, *refs = refs
        out_ref, sums_ref = refs[-2:]
        for k, up_tile in enumerate(up_pieces.tiles):
            ((which, start, _),) = up_tile
            wq = refs[which][start : start + tile, pl.ds(qkv_pieces.first, columns)]
            wu = refs[which][start : start + tile, pl.ds(up_pieces.first, units)]
            at = pl.ds(k * tile, tile)
            sums = [jnp.zeros((1, tile), F32)] * 4
            for row, rows in chunks(count, 256):
                span = pl.ds(row, rows)
                there = pl.ds(first * count + row, rows)
                one = times_transposed(gp_ref[there, :], wq)
                two = times_transposed(gh_ref[there, :], wu)
                xhat = (x_ref[span, at].astype(F32) - stats_ref[there, 0:1]) * stats_ref[there, 1:2]
                value = one * scales_ref[0:1, at] + two * scales_ref[2:3, at]
                if extra is not None:
                    value = value + extra_ref[span, at].astype(F32)
                out_ref[span, at] = value.astype(BF16)
                for n, term in enumerate((one * xhat, one, two * xhat, two)):
                    sums[n] = sums[n] + jnp.sum(term, axis=0, keepdims=True)
            sums_ref[:, at] = jnp.concatenate(sums, axis=0)

    return on_chip(
        body,
        "input_terms",
        arrays + weights,
        [((count, width), BF16), ((4, width), F32)],
        cost(
            4 * count * (columns + units) * width,
            2 * (columns + units) * (width + count) + 2 * count * width,
            2 * count * width,
        ),
    )


def weight_grad(left, right, extras=(), halves=False, kind=BF16):
    depth, rows = left.shape
    cols = right.shape[1]

    def body(l_ref, r_ref, *refs):
        extra_refs, outs = refs[: len(extras)], refs[len(extras) :]
        for row, size in chunks(rows, min(256, rows // 2)):
            value = left_transposed(l_ref[:, pl.ds(row, size)], r_ref[...])
            for ref, (array, first) in zip(extra_refs, extras):
                if first <= row < first + array.shape[0]:
                    value = value + ref[pl.ds(row - first, size), :].astype(F32)
            if halves:
                half = rows // 2
                outs[row // half][pl.ds(row % half, size), :] = value.astype(kind)
            else:
                outs[0][pl.ds(row, size), :] = value.astype(kind)

    shapes = [((rows // 2, cols), kind)] * 2 if halves else [((rows, cols), kind)]
    found = on_chip(
        body,
        "weight_grad",
        [left, right, *[e[0] for e in extras]],
        shapes,
        cost(4 * depth * rows * cols, 2 * depth * (rows + cols), rows * cols * 2),
    )
    return found if halves else found[0]


ANY = pl.BlockSpec(memory_space=pl.ANY)


def copies(name, scalars, arrays, shapes, moves):
    def body(at_ref, *refs):
        ins, outs, sems = refs[: len(arrays)], refs[len(arrays) : -1], refs[-1]
        jobs = [
            pltpu.make_async_copy(source, target, sems.at[n])
            for n, (source, target) in enumerate(moves(at_ref, ins, outs))
        ]
        for job in jobs:
            job.start()
        for job in jobs:
            job.wait()

    return pl.pallas_call(
        body,
        in_specs=[SMEM] + [ANY] * len(arrays),
        out_specs=[VMEM] * len(shapes),
        out_shape=[jax.ShapeDtypeStruct(shape, BF16) for shape in shapes],
        scratch_shapes=[pltpu.SemaphoreType.DMA((24,))],
        compiler_params=pltpu.CompilerParams(vmem_limit_bytes=48 * 1024 * 1024),
        cost_estimate=cost(0, 2 * sum(int(np.prod(shape)) for shape in shapes), 0),
        name=name,
    )(scalars, *arrays)


def rotary_tables(lengths, size):
    lanes, half = 128, ROT // 2
    power = -(np.arange(half, dtype=np.float32) * np.float32(2.0 / ROT))
    inverse = np.zeros((1, lanes), np.float32)
    inverse[0, :half] = inverse[0, half:ROT] = np.float32(10000.0) ** power
    count = len(lengths)

    def body(*refs):
        inverse_ref, cos_ref, before_ref, after_ref, begin_ref = refs[count:]
        for n in range(count):
            row = lax.broadcasted_iota(jnp.int32, (size, 1), 0)
            begin = jnp.zeros((size, 1), jnp.int32)
            start = jnp.int32(0)
            for k in range(lengths[n].shape[1]):
                begin = jnp.where(row >= start, start, begin)
                start = start + refs[n][0, k]
            angle = (row - begin).astype(F32) * inverse_ref[...]
            sine = jnp.sin(angle)
            lane = lax.broadcasted_iota(jnp.int32, (size, lanes), 1)
            cos_ref[n] = jnp.cos(angle)
            before_ref[n] = jnp.where(lane < half, -sine, 0.0)
            after_ref[n] = jnp.where((lane >= half) & (lane < ROT), sine, 0.0)
            begin_ref[n] = begin

    table = ((count, size, lanes), F32)
    *tables, begins = on_chip(
        body,
        "rotary_tables",
        [jnp.asarray(inverse)],
        [table, table, table, ((count, size, 1), jnp.int32)],
        cost(0, 0, 12 * count * size * lanes),
        lengths,
    )
    return tuple(tables), begins


def small_params(packed, at, spans, blocks, slice_rows):
    rows = packed.shape[0]
    first = np.cumsum([0] + spans)
    width = spans[2] * rows

    def body(at_ref, p_ref, qkv_ref, up_ref, out_ref, scales_ref, table):
        z, part, block = at_ref[0], at_ref[1], at_ref[2]
        table[...] = p_ref[...].astype(F32)
        qkv_ref[...] = table[pl.ds(2 * z + part, 1), : spans[0]]
        for k in range(blocks):
            columns = pl.ds(pl.multiple_of(first[1] + z * slice_rows, 128), slice_rows)
            up_ref[:, k * slice_rows : (k + 1) * slice_rows] = table[pl.ds(2 * k + part, 1), columns]
        each = spans[2]
        for i in range(rows):
            out_ref[:, i * each : (i + 1) * each] = (
                table[i : i + 1, first[2] : first[3]] + table[i : i + 1, first[3] : first[4]]
            )
        for off in range(blocks):
            for c in range(2):
                row = pl.ds(2 * (block ^ off) + c, 1)
                place = (off * 2 + c) * each
                for k in range(4):
                    scales_ref[k : k + 1, place : place + each] = table[row, first[4 + k] : first[5 + k]]

    return pl.pallas_call(
        body,
        in_specs=[SMEM, VMEM],
        out_specs=[VMEM] * 4,
        out_shape=[
            jax.ShapeDtypeStruct(shape, F32)
            for shape in ((1, spans[0]), (1, blocks * slice_rows), (1, width), (4, width))
        ],
        scratch_shapes=[pltpu.VMEM(packed.shape, F32)],
        compiler_params=pltpu.CompilerParams(vmem_limit_bytes=4 * 1024 * 1024),
        cost_estimate=cost(0, 0, 0),
        name="small_params",
    )(at, packed)


def chunk_rows(value, count):
    rows, columns = value.shape
    size = columns // count

    def body(from_ref, to_ref):
        for k in range(count):
            to_ref[k * rows : (k + 1) * rows, :] = from_ref[:, k * size : (k + 1) * size]

    return on_chip(
        body, "chunk_rows", [value], [((rows * count, size), value.dtype)], cost(0, 0, 4 * value.size)
    )[0]


def core_shares(value, axis, at, count=1):
    rows, columns = value.shape[0] // count, value.shape[1]
    shape = (rows // 2, columns * count) if axis == 0 else (rows, columns // 2)

    def body(at_ref, from_ref, mine_ref, other_ref):
        part = at_ref[1]
        for ref, which in ((mine_ref, part), (other_ref, 1 - part)):
            if axis == 0:
                for k in range(count):
                    place = pl.multiple_of(k * rows + which * shape[0], shape[0])
                    ref[:, k * columns : (k + 1) * columns] = from_ref[pl.ds(place, shape[0]), :]
            else:
                ref[...] = from_ref[:, pl.ds(pl.multiple_of(which * shape[1], shape[1]), shape[1])]

    return on_chip(
        body, "core_shares", [value], [(shape, value.dtype)] * 2, cost(0, 0, 4 * value.size), [at]
    )


def core_join(mine, got, axis, at):
    rows, columns = mine.shape
    shape = (2 * rows, columns) if axis == 0 else (rows, 2 * columns)

    def body(at_ref, mine_ref, got_ref, out_ref):
        part = at_ref[1]
        for ref, which in ((mine_ref, part), (got_ref, 1 - part)):
            if axis == 0:
                out_ref[pl.ds(pl.multiple_of(which * rows, rows), rows), :] = ref[...].astype(F32)
            else:
                place = pl.multiple_of(which * columns, columns)
                out_ref[:, pl.ds(place, columns)] = ref[...].astype(F32)

    return on_chip(body, "core_join", [mine, got], [(shape, F32)], cost(0, 0, 8 * mine.size), [at])[0]


def copied(value):
    def body(from_ref, to_ref):
        to_ref[...] = from_ref[...]

    return on_chip(body, "copied", [value], [(value.shape, value.dtype)], cost(0, 0, 2 * value.size))[0]


def chip_pair(own, other, at):
    rows, columns = own.shape

    def body(at_ref, own_ref, other_ref, out_ref):
        part = at_ref[1]
        out_ref[pl.ds(pl.multiple_of(part * rows, rows), rows), :] = own_ref[...]
        out_ref[pl.ds(pl.multiple_of((1 - part) * rows, rows), rows), :] = other_ref[...]

    return on_chip(
        body, "chip_pair", [own, other], [((2 * rows, columns), BF16)], cost(0, 0, 0), [at]
    )[0]


class Place:
    def __init__(self):
        self.n_dp = lax.axis_size("dp")
        self.n_seq = lax.axis_size("seq")
        assert self.n_dp == 2 * self.n_seq
        self.split = 2 if H % (2 * self.n_seq) == 0 else 1
        self.blocks = self.n_dp // self.split
        self.dp = lax.axis_index("dp")
        self.z = lax.axis_index("seq")
        self.block = self.dp // self.split
        self.part = self.dp % self.split
        self.at = jnp.stack([self.z, self.part, self.block]).astype(jnp.int32)
        self.masks = [1 << k for k in range(self.blocks.bit_length() - 1)]
        self.order = list(range(self.blocks))
        self.paired = self.split == 2 and self.blocks == 4

    def swap(self, value, mask):
        return lax.ppermute(value, "dp", [(i, i ^ mask) for i in range(self.n_dp)])

    def to_relative(self, value, axis):
        size = value.shape[axis] // self.blocks
        return jnp.concatenate(
            [
                lax.dynamic_slice_in_dim(value, (self.block ^ off) * size, size, axis)
                for off in self.order
            ],
            axis=axis,
        )

    def to_natural(self, value, axis):
        return self.to_relative(value, axis)

    def pair(self, own, other, axis):
        return jnp.where(
            self.part == 0,
            jnp.concatenate([own, other], axis=axis),
            jnp.concatenate([other, own], axis=axis),
        )

    def gather(self, piece):
        half = piece.shape[0] // 2
        gathered = []
        for rows, masks in ((piece[:half], self.masks), (piece[half:], self.masks[::-1])):
            have = {0: rows}
            for mask in masks:
                offs = list(have)
                sent = jnp.concatenate([have[o] for o in offs], 0) if len(offs) > 1 else have[offs[0]]
                got = self.swap(sent, mask * self.split)
                for k, o in enumerate(offs):
                    have[o ^ mask] = got[k * half : (k + 1) * half]
            gathered.append(have)
        return gathered

    def scatter_sum(self, product, halves):
        out = []
        for half, masks in zip(halves, (self.masks, self.masks[::-1])):
            live = list(range(self.blocks))
            extra = {}

            def total(offs):
                whole = product(half, offs)
                if all(o not in extra for o in offs):
                    return whole
                axis, size = whole.ndim and product.axis, whole.shape[product.axis] // len(offs)
                parts = []
                for k, o in enumerate(offs):
                    value = lax.slice_in_dim(whole, k * size, (k + 1) * size, axis=axis)
                    for more in extra.get(o, ()):
                        value = value + more.astype(F32)
                    parts.append(value)
                return parts[0] if len(parts) == 1 else jnp.concatenate(parts, axis=axis)

            for mask in masks:
                away = [o for o in self.order if o in live and o & mask]
                sent = total(away).astype(BF16)
                got = self.swap(sent, mask * self.split)
                size = got.shape[product.axis] // len(away)
                for k, o in enumerate(away):
                    extra.setdefault(o ^ mask, []).append(
                        lax.slice_in_dim(got, k * size, (k + 1) * size, axis=product.axis)
                    )
                live = [o for o in live if not o & mask]
            out.append(total([0]))
        return out


class Product:
    def __init__(self, place, by_block, other, axis):
        self.place, self.by_block, self.other, self.axis = place, by_block, other, axis
        self.size = by_block.shape[1] // place.blocks

    def __call__(self, half, offs):
        where = [self.place.order.index(o) for o in offs]
        if where == list(range(where[0], where[0] + len(where))):
            blocks = self.by_block[:, where[0] * self.size : (where[-1] + 1) * self.size]
        else:
            blocks = jnp.concatenate(
                [self.by_block[:, w * self.size : (w + 1) * self.size] for w in where], axis=1
            )
        width = self.other.shape[1] // 2
        others = self.other[:, half * width : (half + 1) * width]
        if self.axis == 0:
            return left_transposed(blocks, others)
        return left_transposed(others, blocks)


class Chain:
    def __init__(self):
        self.last = None

    def __call__(self, *values):
        if self.last is not None:
            values = tuple(lax.optimization_barrier((values, self.last))[0])
        return values if len(values) > 1 else values[0]

    def done(self, value):
        self.last = value
        return value

    def wait(self, value):
        if value is not None:
            self.last = (self.last, value)


class Gathered:
    def __init__(self, here, piece):
        self.here, self.piece = here, piece
        self.half = piece.shape[0] // 2

    def send(self):
        here = self.here
        if here.paired:
            self.by_x, self.by_y = here.swap(self.piece, 2), here.swap(self.piece, 4)
            return self.by_x, self.by_y

    def hand_on(self, chain):
        if self.here.paired:
            half = self.half
            columns = self.piece.shape[1]

            def body(x_ref, y_ref, first_ref, second_ref):
                first_ref[...] = x_ref[:half, :]
                second_ref[...] = y_ref[half:, :]

            first, second = on_chip(
                body,
                "hand_on",
                chain(self.by_x, self.by_y),
                [((half, columns), BF16)] * 2,
                cost(0, 0, 4 * half * columns),
            )
            chain.done((first, second))
            self.handed = (self.here.swap(first, 4), self.here.swap(second, 2))
            return self.handed

    def rows(self, size, moving, columns=None):
        here, block = self.here, self.piece.shape[0]
        if here.paired:
            arrays = [self.piece, self.by_x, self.by_y, *self.handed]
            tiles, now, left = [], [], size
            for which, count in enumerate([block] * 3 + [self.half] * 2):
                first = 0
                while count:
                    take = min(left, count)
                    now.append((which, first, take))
                    first, count, left = first + take, count - take, left - take
                    if not left:
                        tiles.append(now)
                        now, left = [], size
            blocks = None
            if moving:
                assert size == block
                blocks = here.block ^ jnp.arange(here.blocks, dtype=jnp.int32)
            return Pieces(arrays, tiles, size, blocks, columns)
        if not hasattr(self, "whole"):
            halves = here.gather(self.piece)
            whole = jnp.concatenate([half[o] for o in range(here.blocks) for half in halves], axis=0)
            self.whole = here.to_natural(whole, 0) if moving else whole
        count = self.whole.shape[0] // size
        blocks = jnp.arange(count, dtype=jnp.int32) if moving else None
        return Pieces([self.whole], [[(0, k * size, size)] for k in range(count)], size, blocks, columns)


class Spread:
    def __init__(self, here, piece):
        self.here, self.step = here, 0
        chips = here.n_dp // 2
        masks = [1 << k for k in range(chips.bit_length() - 1)]
        self.steps = len(masks)
        self.offset = (here.dp // 2) ^ here.z
        self.states = [(piece[0], masks, [0]), (piece[1], masks[::-1], [0])]

    def send(self):
        here, self.got = self.here, []
        for rows, order, held in self.states:
            pairs = [
                (
                    (2 * (z ^ o) + c) * here.n_seq + z,
                    (2 * (z ^ o ^ order[self.step]) + c) * here.n_seq + z,
                )
                for z in range(here.n_seq)
                for o in held
                for c in range(2)
            ]
            self.got.append(lax.ppermute(rows, ("dp", "seq"), pairs))
        return tuple(self.got)

    def take(self, chain):
        got = chain(*self.got)
        after = []
        for new, (rows, order, held) in zip(got, self.states):
            takes = jnp.zeros((), jnp.bool_)
            for o in held:
                takes = takes | (self.offset == (o ^ order[self.step]))
            after.append(
                (
                    jnp.where(takes, new, rows),
                    order,
                    held + [o ^ order[self.step] for o in held],
                )
            )
        self.states = after
        self.step += 1
        chain.done(tuple(state[0] for state in after))

    def hold(self, chain):
        self.states = [(chain(rows), order, held) for rows, order, held in self.states]

    def finish(self, chain):
        self.take(chain)
        here = self.here
        rows = jnp.concatenate([state[0] for state in self.states], axis=0)
        if here.split == 1:
            other = here.swap(rows, 1)
            rows = jnp.where(
                here.dp % 2 == 0,
                jnp.concatenate([rows, other], 0),
                jnp.concatenate([other, rows], 0),
            )
        return rows


class Scattered:
    def __init__(self, here, left, right):
        self.here, self.left, self.right = here, left, right
        self.axis = 0 if isinstance(left, (list, tuple)) else 1

    def part(self, off, **more):
        if self.axis == 0:
            return weight_grad(self.left[off], self.right, **more)
        return weight_grad(self.left, self.right[off], **more)

    def first(self, chain):
        if self.here.paired:
            if self.axis == 0:
                self.right = chain(self.right)
            else:
                self.left = chain(self.left)
            one, two = chain.done(self.part(3, halves=True))
            self.by_x, self.by_y = self.here.swap(one, 2), self.here.swap(two, 4)
            return self.by_x, self.by_y

    def second(self, chain):
        if self.here.paired:
            by_x, by_y = chain(self.by_x, self.by_y)
            half = by_x.shape[0]
            to_x = self.part(1, extras=((by_y, half),))
            to_y = self.part(2, extras=((by_x, 0),))
            chain.done((to_x, to_y))
            self.by_x, self.by_y = self.here.swap(to_x, 2), self.here.swap(to_y, 4)
            return self.by_x, self.by_y

    def last(self, chain, kind):
        if self.here.paired:
            by_x, by_y = chain(self.by_x, self.by_y)
            return chain.done(self.part(0, extras=((by_x, 0), (by_y, 0)), kind=kind))
        if self.axis == 1:
            product = Product(self.here, jnp.concatenate(self.right, axis=1), self.left, 1)
        else:
            product = Product(self.here, jnp.concatenate(self.left, axis=1), self.right, 0)
        halves = self.here.scatter_sum(product, (0, 1))
        return jnp.concatenate(halves, axis=1 - self.axis).astype(kind)


def on_device(
    tokens,
    doc_lengths,
    qkv_weight,
    qkv_bias,
    dense_weight,
    dense_bias,
    up_weight,
    up_bias,
    down_weight,
    down_bias,
    norm1_gain,
    norm1_shift,
    norm2_gain,
    norm2_shift,
    cotangent,
):
    here = Place()
    chain = Chain()
    n_dp, n_seq, split, blocks = here.n_dp, here.n_seq, here.split, here.blocks
    z, part = here.z, here.part
    rows_here, width = tokens.shape
    seq_len = rows_here * n_seq
    hidden_rows = down_weight.shape[0]
    slice_rows = hidden_rows // n_seq
    assert H == n_seq * split
    head_cols = 3 * HS

    def column_places(core):
        head = (z * split + core) * head_cols
        return head, [(k * split + core) * hidden_rows + z * slice_rows for k in range(blocks)]

    half_dense = dense_weight.shape[0] // 2
    wide_cols = head_cols + blocks * slice_rows
    if here.paired:
        size = width // blocks

        def moves(at, ins, outs):
            tokens_in, qkv_in, up_in, down_in, dense_in = ins
            plane, core, block = at[0], at[1], at[2]
            jobs = []
            for off in range(blocks):
                place = pl.multiple_of((block ^ off) * size, size)
                jobs.append((tokens_in.at[:, pl.ds(place, size)], outs[0].at[:, off * size : (off + 1) * size]))
            for out, its in ((outs[1], 1 - core), (outs[2], core)):
                place = pl.multiple_of((plane * split + its) * head_cols, 128)
                jobs.append((qkv_in.at[:, pl.ds(place, head_cols)], out.at[:, :head_cols]))
                for k in range(blocks):
                    place = pl.multiple_of((k * split + its) * hidden_rows + plane * slice_rows, 128)
                    to = head_cols + k * slice_rows
                    jobs.append((up_in.at[:, pl.ds(place, slice_rows)], out.at[:, to : to + slice_rows]))
            place = pl.multiple_of(plane * slice_rows, slice_rows)
            jobs.append((down_in.at[pl.ds(place, slice_rows), :], outs[3]))
            jobs.append((dense_in.at[:half_dense], outs[4]))
            jobs.append((dense_in.at[half_dense:], outs[5]))
            return jobs

        shapes = [tokens.shape] + [(qkv_weight.shape[0], wide_cols)] * 2 + [(slice_rows, width)]
        shapes = shapes + [(half_dense, width)] * 2
        tokens_rel, wide_other, wide_piece, down_piece, *dense_halves = chain.done(
            copies(
                "first_copies",
                here.at,
                (tokens, qkv_weight, up_weight, down_weight, dense_weight),
                shapes,
                moves,
            )
        )
        got = here.swap(wide_other, 1)
    else:
        tokens_rel = here.to_relative(tokens, 1)
        head, places = column_places(part)
        wide_piece = jnp.concatenate(
            [lax.dynamic_slice_in_dim(qkv_weight, head, head_cols, 1)]
            + [lax.dynamic_slice_in_dim(up_weight, place, slice_rows, 1) for place in places],
            axis=1,
        )
        down_piece = lax.dynamic_slice_in_dim(down_weight, z * slice_rows, slice_rows, 0)
        dense_halves = dense_weight[:half_dense], dense_weight[half_dense:]
    x_own = lax.all_gather(tokens_rel, "seq", axis=0, tiled=True)
    g_own = lax.all_gather(chain(cotangent), "seq", axis=0, tiled=True)
    dense_rows = Spread(here, dense_halves)
    dense_pair = dense_rows.send()
    small = (qkv_bias, up_bias, dense_bias, down_bias, norm1_gain, norm1_shift, norm2_gain, norm2_shift)
    packed_small = chain.done(jnp.concatenate(chain(*small)))
    packed_small = jnp.broadcast_to(packed_small[None], (n_dp,) + packed_small.shape)
    packed_small = lax.all_to_all(packed_small, "dp", 0, 0, tiled=True)
    lengths = [doc_lengths] + ([here.swap(doc_lengths, 1)] if split == 2 else [])
    if here.paired:
        wide_piece = chain.done(chip_pair(chain(wide_piece), got, here.at))
    wide_rows = Gathered(here, wide_piece)
    wide_pair = wide_rows.send()
    lengths = [chain(v) for v in lengths]
    tables, begins = chain.done(rotary_tables(lengths, seq_len))
    spans = [v.shape[0] for v in small]

    chain.wait(dense_pair)
    dense_rows.take(chain)
    chain.wait(wide_pair)
    wide_pair = wide_rows.hand_on(chain)
    if here.paired:
        b_qkv, b_up, b_out, scales = chain.done(
            small_params(chain(packed_small), here.at, spans, blocks, slice_rows)
        )
    else:
        pieces, first = [], 0
        for span in spans:
            pieces.append(packed_small[:, first : first + span].astype(F32))
            first += span
        b_qkv, b_up, b_dense, b_down = pieces[:4]
        head = (z * split + part) * head_cols
        b_qkv = lax.dynamic_slice_in_dim(b_qkv.reshape(1, -1), head, head_cols, 1)
        b_up = lax.dynamic_slice_in_dim(b_up, z * slice_rows, slice_rows, 1)
        b_up = b_up.reshape(blocks, split, slice_rows)
        b_up = lax.dynamic_index_in_dim(b_up, part, 1, keepdims=False).reshape(1, -1)
        b_out = (b_dense + b_down).reshape(1, -1)
        scales = here.to_relative(jnp.stack([v.reshape(-1) for v in pieces[4:]]), 1)
    streams = [x_own] + ([here.swap(chain(x_own), 1)] if split == 2 else [])
    normed = chain.done(two_norms(chain(*streams) if split == 2 else streams, scales, blocks))
    normed_one, normed_two, stats = normed[:blocks], normed[blocks:-1], normed[-1]
    chain.wait(wide_pair)
    down_rows = Gathered(here, chain(down_piece))
    down_pair = down_rows.send()
    dense_rows.hold(chain)
    dense_pair = dense_rows.send()
    while dense_rows.step < dense_rows.steps - 1:
        dense_rows.take(chain)
        dense_pair = dense_rows.send()
    g_own = chain(g_own)
    streams_g = [g_own] + ([here.swap(g_own, 1)] if split == 2 else [])
    qkv_pieces = wide_rows.rows(256, False, (0, head_cols))
    up_pieces = wide_rows.rows(256, False, (head_cols, blocks * slice_rows))
    activated, slope = chain.done(feed_up(normed_two, up_pieces, chain(b_up)))
    qkv, probs, attended = chain.done(
        attention_forward(normed_one, qkv_pieces, chain(b_qkv), tables, begins)
    )
    attended = attended.reshape(split * seq_len, HS)
    chain.wait(down_pair)
    chain.wait(dense_pair)

    down_pair = down_rows.hand_on(chain)
    g_blocks = chain.done(cotangent_blocks(chain(*streams_g) if split == 2 else streams_g, here.at, blocks))
    sum_down = Scattered(here, activated, g_blocks)
    sum_dense = Scattered(here, attended, g_blocks)
    pair_down = sum_down.first(chain)
    w_dense = dense_rows.finish(chain)
    grad_projected, grad_qkv_bias = chain.done(
        attention_backward(chain(qkv), probs, g_blocks, w_dense, tables, here.at)
    )
    grad_projected = grad_projected.reshape(split * seq_len, head_cols)
    sum_qkv = Scattered(here, normed_one, grad_projected)
    chain.wait(down_pair)
    pair_qkv = sum_qkv.first(chain)
    down_pieces = down_rows.rows(down_piece.shape[0] if here.paired else 256, True)

    def to_plane(whole, axis):
        if here.paired:
            whole = chunk_rows(whole, n_seq) if axis == 1 else whole
            return lax.all_to_all(whole, "seq", split_axis=0, concat_axis=0, tiled=True)
        moved = lax.all_to_all(whole, "seq", split_axis=axis, concat_axis=axis, tiled=True)
        per = moved.shape[axis] // (n_seq * 2)
        if axis == 0:
            return moved.reshape(n_seq, 2, per, -1).transpose(1, 0, 2, 3).reshape(moved.shape)
        return moved.reshape(-1, n_seq, 2, per).transpose(0, 2, 1, 3).reshape(moved.shape)

    def join(value):
        return lax.psum_scatter(value, "seq", scatter_dimension=0, tiled=True).astype(F32)

    def branches(first, extra=None):
        return chain.done(
            branch_rows_of(chain(attended), w_dense, activated, down_pieces, first, seq_len, extra)
        )

    def terms(first, extra=None):
        return chain.done(
            input_terms(
                chain(grad_projected),
                qkv_pieces,
                grad_hidden,
                up_pieces,
                streams[first],
                stats,
                scales,
                first,
                extra,
            )
        )

    branch_other = branches(1) if split == 2 else None
    chain.wait(pair_down)
    chain.wait(pair_qkv)
    if split == 2:
        branch_other = here.swap(chain(branch_other), 1)
    pair_down = sum_down.second(chain)
    branch_rows = join(branches(0, branch_other))
    pair_dense = sum_dense.first(chain)
    grad_hidden, grad_up_bias = chain.done(hidden_grad(g_blocks, down_pieces, chain(slope), here.at))
    sum_up = Scattered(here, normed_two, grad_hidden)
    term_other, norm_sums = None, jnp.zeros((4, width), F32)
    if split == 2:
        term_other, norm_sums = terms(1)
    chain.wait(pair_dense)
    chain.wait(pair_down)
    plane_down = to_plane(sum_down.last(chain, BF16), 0)
    if split == 2:
        term_other = here.swap(chain(term_other), 1)
    pair_up = sum_up.first(chain)
    pair_qkv = sum_qkv.second(chain)
    term_own, more_sums = terms(0, term_other)
    norm_sums = norm_sums + more_sums

    norm_sums = here.to_natural(chain(norm_sums), 1)
    wide_qkv = lax.dynamic_update_slice_in_dim(
        jnp.zeros((H * head_cols,), F32), grad_qkv_bias.reshape(-1), (z * split + part) * head_cols, 0
    )
    wide_up = lax.dynamic_update_slice(
        jnp.zeros((blocks, split, n_seq, slice_rows), F32),
        grad_up_bias.reshape(blocks, 1, 1, slice_rows),
        (0, part, z, 0),
    )
    cotan_rows = cotangent.astype(F32)
    column_total = jnp.sum(cotan_rows, axis=0)
    devices = n_dp * n_seq
    wide = [wide_qkv, wide_up, column_total] + [norm_sums[k] for k in range(4)]
    wide = [v.reshape(devices, -1) for v in wide]
    sizes = [v.shape[1] for v in wide]
    wide = chain.done(jnp.concatenate(wide, axis=1))

    def to_cores(value, axis, count=1):
        if not here.paired:
            return lambda: value.astype(F32)
        mine, other = chain.done(core_shares(chain(value), axis, here.at, count))
        got = here.swap(other, 1)
        return lambda: chain.done(core_join(*chain(mine, got), 1 - axis, here.at))

    chain.wait(pair_up)
    chain.wait(pair_qkv)
    chain.wait(plane_down)
    term_rows = join(chain.done(copied(chain(term_own))))
    pair_up = sum_up.second(chain)
    pair_dense = sum_dense.second(chain)
    sum_qkv_last = sum_qkv.last(chain, F32)
    output = chain.done((chain(branch_rows) + tokens.astype(F32) + b_out).astype(BF16))
    chain.wait(pair_up)
    plane_up = to_plane(sum_up.last(chain, BF16), 1)
    grad_qkv = to_cores(sum_qkv_last, 0)
    grad_down = to_cores(plane_down, 1)
    chain.wait(pair_dense)
    grad_dense = to_cores(sum_dense.last(chain, F32), 1)
    grad_qkv, grad_down = grad_qkv(), grad_down()

    values = chain(tokens_rel).astype(F32)
    centred = values - jnp.mean(values, axis=-1, keepdims=True)
    inverse = lax.rsqrt(jnp.mean(centred * centred, axis=-1, keepdims=True) + 1e-05)
    xhat = centred * inverse
    term_rows = chain(term_rows)
    term = (
        term_rows
        - jnp.mean(term_rows, axis=-1, keepdims=True)
        - xhat * jnp.mean(term_rows * xhat, axis=-1, keepdims=True)
    ) * inverse
    input_grad = chain.done((cotan_rows + here.to_natural(term, 1)).astype(BF16))
    grad_dense = grad_dense()
    wide, plane_up = lax.optimization_barrier((wide, plane_up))
    swapped = lax.all_to_all(wide, ("dp", "seq"), split_axis=0, concat_axis=0, tiled=True)
    total = jnp.sum(swapped, axis=0)
    sums, first = [], 0
    for size in sizes:
        sums.append(total[first : first + size])
        first += size
    sum_qkv_bias, sum_up_bias, sum_column, sum_gain_one, sum_shift_one, sum_gain_two, sum_shift_two = sums

    grad_up = to_cores(plane_up, 0, n_seq)()
    return (
        output,
        input_grad,
        grad_qkv,
        sum_qkv_bias,
        grad_dense,
        sum_column,
        grad_up,
        sum_up_bias,
        grad_down,
        sum_column,
        sum_gain_one,
        sum_shift_one,
        sum_gain_two,
        sum_shift_two,
    )


def solution(mesh):
    rows = P(("dp", "seq"), None)
    flat = P(("dp", "seq"))
    placed = (rows,) + (P("dp", None),) * 2 + (P("dp"), P("dp", None)) * 3 + (P("dp"),) * 5 + (rows,)
    return jax.shard_map(
        on_device,
        mesh=mesh,
        in_specs=placed,
        out_specs=(
            rows,
            rows,
            P("dp", "seq"),
            flat,
            P("seq", "dp"),
            flat,
            P("dp", "seq"),
            flat,
            P("seq", "dp"),
            flat,
            flat,
            flat,
            flat,
            flat,
        ),
        check_vma=False,
    )
```

```python
import jax
import jax.numpy as jnp
import numpy as np
from jax import lax
from jax.experimental import pallas as pl
from jax.experimental.pallas import tpu as pltpu
from jax.sharding import PartitionSpec as P

H = 8
HS = 256
ROT = 64
HINT = 1.0
LIMIT = 16 * 1024 * 1024
F32 = jnp.float32
BF16 = jnp.bfloat16


def matmul(left, right):
    return jnp.dot(left, right, preferred_element_type=F32)


def times_transposed(left, right):
    return lax.dot_general(left, right, (((1,), (1,)), ((), ())), preferred_element_type=F32)


def left_transposed(left, right):
    return lax.dot_general(left, right, (((0,), (0,)), ((), ())), preferred_element_type=F32)


def cost(flops, reads, writes, transcendentals=0):
    return pl.CostEstimate(
        flops=int(flops * HINT),
        bytes_accessed=int((reads + writes) * HINT),
        transcendentals=int(transcendentals * HINT),
    )


VMEM = pl.BlockSpec(memory_space=pltpu.VMEM)
SMEM = pl.BlockSpec(memory_space=pltpu.SMEM)


def on_chip(body, name, arrays, shapes, estimate, scalars=()):
    return pl.pallas_call(
        body,
        in_specs=[SMEM] * len(scalars) + [VMEM] * len(arrays),
        out_specs=[VMEM] * len(shapes),
        out_shape=[jax.ShapeDtypeStruct(*shape) for shape in shapes],
        compiler_params=pltpu.CompilerParams(vmem_limit_bytes=LIMIT),
        cost_estimate=estimate,
        name=name,
    )(*scalars, *arrays)


def each(total, size, step):
    if total <= size:
        return step(0)

    @pl.loop(0, total // size)
    def _(i):
        step(pl.multiple_of(i * size, size))


def chunks(total, size):
    return [(at, min(size, total - at)) for at in range(0, total, size)]


def two_norms(arrays, scales, blocks):
    rows, width = arrays[0].shape
    total = rows * len(arrays)
    tile, step = 128, 32
    size = width // blocks
    steps = rows // tile

    def body(scales_ref, *refs):
        ins, outs, stats_ref = refs[: len(arrays)], refs[len(arrays) : -1], refs[-1]
        for k in range(len(arrays)):

            @pl.when(pl.program_id(0) // steps == k)
            def _(k=k):
                @pl.loop(0, tile // step)
                def _(i):
                    span = pl.ds(pl.multiple_of(i * step, step), step)
                    values = ins[k][span, :].astype(F32)
                    average = jnp.mean(values, axis=-1, keepdims=True)
                    centred = values - average
                    variance = jnp.mean(centred * centred, axis=-1, keepdims=True)
                    inverse = lax.rsqrt(variance + 1e-05)
                    xhat = centred * inverse
                    one = (xhat * scales_ref[0:1, :] + scales_ref[1:2, :]).astype(BF16)
                    two = (xhat * scales_ref[2:3, :] + scales_ref[3:4, :]).astype(BF16)
                    for n in range(blocks):
                        outs[n][span, :] = one[:, n * size : (n + 1) * size]
                        outs[blocks + n][span, :] = two[:, n * size : (n + 1) * size]
                    stats_ref[span, :] = jnp.concatenate([average, inverse], axis=1)

    return pl.pallas_call(
        body,
        grid=(total // tile,),
        in_specs=[pl.BlockSpec(scales.shape, lambda i: (0, 0))]
        + [
            pl.BlockSpec((tile, width), lambda i, k=k: (jnp.clip(i - k * steps, 0, steps - 1), 0))
            for k in range(len(arrays))
        ],
        out_specs=[pl.BlockSpec((tile, size), lambda i: (i, 0))] * (2 * blocks)
        + [pl.BlockSpec((tile, 2), lambda i: (i, 0))],
        out_shape=[jax.ShapeDtypeStruct((total, size), BF16)] * (2 * blocks)
        + [jax.ShapeDtypeStruct((total, 2), F32)],
        compiler_params=pltpu.CompilerParams(vmem_limit_bytes=LIMIT),
        cost_estimate=cost(total * width * 24, total * width * 2, total * width * 4),
        name="two_norms",
    )(scales, *arrays)


class Pieces:
    def __init__(self, arrays, tiles, size, blocks=None, columns=None):
        self.arrays, self.tiles, self.size, self.blocks = arrays, tiles, size, blocks
        self.first, self.width = columns or (0, arrays[0].shape[1])

    def inside(self, size):
        cut = []
        for which, first, count, k, place in self.runs():
            start = k * self.size + place
            while count:
                take = min(count, size - start % size)
                cut.append((which, first, take, start // size, start % size))
                first, start, count = first + take, start + take, count - take
        return cut

    def runs(self):
        found = []
        for k, tile in enumerate(self.tiles):
            at = 0
            for which, first, count in tile:
                last = found[-1] if found else None
                joins = last and self.blocks is None and last[0] == which and last[1] + last[2] == first
                if joins:
                    found[-1] = (which, last[1], last[2] + count, last[3], last[4])
                else:
                    found.append((which, first, count, k, at))
                at += count
        return found


def feed_up(x, pieces, b):
    rows, size = x[0].shape
    width = size * len(x)
    units = pieces.width

    def body(b_ref, *refs):
        x_refs, w_refs, (act_ref, slope_ref) = refs[: len(x)], refs[len(x) : -2], refs[-2:]
        def step(row):
            for col, cols in chunks(units, 512):
                at = (pl.ds(row, min(256, rows)), pl.ds(col, cols))
                hidden = b_ref[:, at[1]]
                for which, first, depth, k, place in pieces.inside(size):
                    hidden = hidden + matmul(
                        x_refs[k][at[0], place : place + depth],
                        w_refs[which][first : first + depth, pl.ds(pieces.first + col, cols)],
                    )
                cdf = 0.5 + 0.5 * lax.erf(hidden * (0.5**0.5))
                act_ref[at] = (hidden * cdf).astype(BF16)
                slope_ref[at] = cdf + hidden * (jnp.exp(-0.5 * hidden * hidden) * 0.3989422804014327)

        each(rows, 256, step)

    return on_chip(
        body,
        "feed_up",
        [b, *x, *pieces.arrays],
        [((rows, units), BF16), ((rows, units), F32)],
        cost(4 * rows * width * units, 2 * (rows + units) * width, 6 * rows * units, 2 * rows * units),
    )


def cotangent_blocks(streams, at, blocks):
    rows, width = streams[0].shape
    size = width // blocks

    def body(at_ref, *refs):
        ins, outs = refs[: len(streams)], refs[len(streams) :]
        for off in range(blocks):
            place = pl.ds(pl.multiple_of((at_ref[2] ^ off) * size, 128), size)
            for n in range(len(streams)):
                outs[off][n * rows : (n + 1) * rows, :] = ins[n][:, place]

    return on_chip(
        body,
        "cotangent_blocks",
        streams,
        [((rows * len(streams), size), BF16)] * blocks,
        cost(0, rows * width * 4, rows * width * 4),
        [at],
    )


def hidden_grad(g, pieces, slope, at):
    rows, size = g[0].shape
    width = size * len(g)
    units = slope.shape[1]

    def body(blocks_ref, at_ref, slope_ref, *refs):
        g_refs, w_refs, (out_ref, sum_ref) = refs[: len(g)], refs[len(g) : -2], refs[-2:]
        for which, first, count, k, place in pieces.runs():
            columns = pl.ds(pl.multiple_of(blocks_ref[k] * pieces.size + place, 128), count)
            total = jnp.zeros((1, count), F32)
            for row, tall in chunks(rows, 256):
                span = pl.ds(row, tall)
                value = jnp.zeros((tall, count), F32)
                for off in range(len(g)):
                    block = pl.ds(pl.multiple_of((at_ref[2] ^ off) * size, 128), size)
                    value = value + times_transposed(
                        g_refs[off][span, :], w_refs[which][first : first + count, block]
                    )
                value = (value * slope_ref[span, columns]).astype(BF16)
                out_ref[span, columns] = value
                total = total + jnp.sum(value.astype(F32), axis=0, keepdims=True)
            sum_ref[:, columns] = total

    return on_chip(
        body,
        "hidden_grad",
        [slope, *g, *pieces.arrays],
        [((rows, units), BF16), ((1, units), F32)],
        cost(4 * rows * width * units, 2 * (rows + units) * width + 4 * rows * units, 2 * rows * units),
        [pieces.blocks, at],
    )


def turn(values, cosine, before, after, sign):
    lanes = cosine.shape[1]
    half = ROT // 2
    first = values[:, :lanes]
    first = first * cosine + sign * (
        pltpu.roll(first, lanes - half, 1) * before + pltpu.roll(first, half, 1) * after
    )
    return jnp.concatenate([first, values[:, lanes:]], axis=1)


def attention_forward(x, pieces, bias, tables, begins):
    count, size = tables[0].shape[:2]
    part = x[0].shape[1]
    width = part * len(x)
    columns = bias.shape[1]

    def body(b_ref, cos_ref, before_ref, after_ref, begin_ref, *refs):
        x_refs, w_refs, (qkv_ref, probs_ref, out_ref) = refs[: len(x)], refs[len(x) : -3], refs[-3:]
        @pl.loop(0, count)
        def _(n):
            turns = (cos_ref[n], before_ref[n], after_ref[n])
            projected = b_ref[...]
            for which, first, rows, k, place in pieces.inside(part):
                projected = projected + matmul(
                    x_refs[k][pl.ds(pl.multiple_of(n * size, size), size), place : place + rows],
                    w_refs[which][first : first + rows, pl.ds(pieces.first, columns)],
                )
            queries = turn(projected[:, :HS], *turns, 1.0).astype(BF16)
            keys = turn(projected[:, HS : 2 * HS], *turns, 1.0).astype(BF16)
            values = projected[:, 2 * HS :].astype(BF16)
            qkv_ref[n, :, :HS] = queries
            qkv_ref[n, :, HS : 2 * HS] = keys
            qkv_ref[n, :, 2 * HS :] = values
            for row, tile in chunks(size, 256):
                rows = slice(row, row + tile)
                scores = times_transposed(queries[rows], keys) * (HS**-0.5)
                places = lax.broadcasted_iota(jnp.int32, (tile, size), 1)
                here = lax.broadcasted_iota(jnp.int32, (tile, size), 0) + row
                allowed = (places >= begin_ref[n, rows, :]) & (places <= here)
                masked = jnp.where(allowed, scores, -1e30)
                exponent = jnp.exp(masked - jnp.max(masked, axis=-1, keepdims=True))
                probs = exponent / jnp.sum(exponent, axis=-1, keepdims=True)
                probs_ref[n, rows, :] = probs
                out_ref[n, rows, :] = matmul(probs.astype(BF16), values).astype(BF16)

    return on_chip(
        body,
        "attention_forward",
        [bias, *tables, begins, *x, *pieces.arrays],
        [
            ((count, size, columns), BF16),
            ((count, size, size), F32),
            ((count, size, HS), BF16),
        ],
        cost(
            count * size * (size * HS * 8 + 4 * width * columns),
            count * size * width * 2,
            count * size * (columns * 2 + size * 4),
            count * size * size,
        ),
    )


def attention_backward(qkv, probs, g, w_dense, tables, at):
    count, size, columns = qkv.shape
    scale = HS**-0.5
    part = g[0].shape[1]

    def body(at_ref, qkv_ref, probs_ref, w_ref, cos_ref, before_ref, after_ref, *refs):
        g_refs, (out_ref, sum_ref) = refs[:-2], refs[-2:]
        sum_ref[...] = jnp.zeros((1, columns), F32)

        @pl.loop(0, count)
        def _(n):
            turns = (cos_ref[n], before_ref[n], after_ref[n])
            queries = qkv_ref[n, :, :HS]
            keys = qkv_ref[n, :, HS : 2 * HS]
            values = qkv_ref[n, :, 2 * HS :]
            grad = jnp.zeros((size, HS), F32)
            for off in range(len(g)):
                block = pl.ds(pl.multiple_of((at_ref[2] ^ off) * part, 128), part)
                grad = grad + times_transposed(g_refs[off][pl.ds(pl.multiple_of(n * size, size), size), :], w_ref[:, block])
            grad = grad.astype(BF16)
            probs_now = probs_ref[n]
            grad_probs = times_transposed(grad, values)
            inner = jnp.sum(probs_now * grad_probs, axis=-1, keepdims=True)
            grad_scores = (probs_now * (grad_probs - inner)).astype(BF16)
            grad_queries = turn(matmul(grad_scores, keys) * scale, *turns, -1.0).astype(BF16)
            grad_keys = turn(left_transposed(grad_scores, queries) * scale, *turns, -1.0).astype(BF16)
            grad_values = left_transposed(probs_now.astype(BF16), grad).astype(BF16)
            whole = jnp.concatenate([grad_queries, grad_keys, grad_values], axis=1)
            out_ref[n] = whole
            sum_ref[...] += jnp.sum(whole.astype(F32), axis=0, keepdims=True)

    return on_chip(
        body,
        "attention_backward",
        [qkv, probs, w_dense, *tables, *g],
        [((count, size, columns), BF16), ((1, columns), F32)],
        cost(
            count * size * (size * HS * 16 + 4 * HS * part * len(g)),
            count * size * (columns * 4 + size * 4),
            count * size * columns * 2,
        ),
        [at],
    )


def branch_rows_of(attended, w_dense, activated, pieces, first, count, extra=None):
    width = w_dense.shape[1]
    inner, units = attended.shape[1], activated.shape[1]
    arrays = [attended, w_dense, activated] + ([] if extra is None else [extra])

    def body(blocks_ref, a_ref, wa_ref, b_ref, *refs):
        if extra is not None:
            extra_ref, *refs = refs
        for row, rows in chunks(count, 256):
            span = pl.ds(first * count + row, rows)
            for col, cols in chunks(width, 512):
                at = pl.ds(col, cols)
                value = matmul(a_ref[span, :], wa_ref[:, at])
                for which, start, depth, k, place in pieces.runs():
                    columns = pl.ds(pl.multiple_of(blocks_ref[k] * pieces.size + place, 128), depth)
                    value = value + matmul(b_ref[span, columns], refs[which][start : start + depth, at])
                if extra is not None:
                    value = value + extra_ref[pl.ds(row, rows), at].astype(F32)
                refs[-1][pl.ds(row, rows), at] = value.astype(BF16)

    return on_chip(
        body,
        "branch_rows",
        arrays + pieces.arrays,
        [((count, width), BF16)],
        cost(4 * count * (inner + units) * width, 2 * (inner + units) * (width + count), 2 * count * width),
        [pieces.blocks],
    )[0]


def input_terms(grad_proj, qkv_pieces, grad_hid, up_pieces, x, stats, scales, first, extra=None):
    count, width = x.shape
    tile = up_pieces.size
    columns, units = grad_proj.shape[1], grad_hid.shape[1]
    weights = up_pieces.arrays
    arrays = [grad_proj, grad_hid, x, stats, scales] + ([] if extra is None else [extra])

    def body(gp_ref, gh_ref, x_ref, stats_ref, scales_ref, *refs):
        if extra is not None:
            extra_ref, *refs = refs
        out_ref, sums_ref = refs[-2:]
        for k, up_tile in enumerate(up_pieces.tiles):
            ((which, start, _),) = up_tile
            wq = refs[which][start : start + tile, pl.ds(qkv_pieces.first, columns)]
            wu = refs[which][start : start + tile, pl.ds(up_pieces.first, units)]
            at = pl.ds(k * tile, tile)
            sums = [jnp.zeros((1, tile), F32)] * 4
            for row, rows in chunks(count, 256):
                span = pl.ds(row, rows)
                there = pl.ds(first * count + row, rows)
                one = times_transposed(gp_ref[there, :], wq)
                two = times_transposed(gh_ref[there, :], wu)
                xhat = (x_ref[span, at].astype(F32) - stats_ref[there, 0:1]) * stats_ref[there, 1:2]
                value = one * scales_ref[0:1, at] + two * scales_ref[2:3, at]
                if extra is not None:
                    value = value + extra_ref[span, at].astype(F32)
                out_ref[span, at] = value.astype(BF16)
                for n, term in enumerate((one * xhat, one, two * xhat, two)):
                    sums[n] = sums[n] + jnp.sum(term, axis=0, keepdims=True)
            sums_ref[:, at] = jnp.concatenate(sums, axis=0)

    return on_chip(
        body,
        "input_terms",
        arrays + weights,
        [((count, width), BF16), ((4, width), F32)],
        cost(
            4 * count * (columns + units) * width,
            2 * (columns + units) * (width + count) + 2 * count * width,
            2 * count * width,
        ),
    )


def weight_grad(left, right, extras=(), halves=False, kind=BF16):
    depth, rows = left.shape
    cols = right.shape[1]

    def body(l_ref, r_ref, *refs):
        extra_refs, outs = refs[: len(extras)], refs[len(extras) :]
        for row, size in chunks(rows, min(256, rows // 2)):
            value = left_transposed(l_ref[:, pl.ds(row, size)], r_ref[...])
            for ref, (array, first) in zip(extra_refs, extras):
                if first <= row < first + array.shape[0]:
                    value = value + ref[pl.ds(row - first, size), :].astype(F32)
            if halves:
                half = rows // 2
                outs[row // half][pl.ds(row % half, size), :] = value.astype(kind)
            else:
                outs[0][pl.ds(row, size), :] = value.astype(kind)

    shapes = [((rows // 2, cols), kind)] * 2 if halves else [((rows, cols), kind)]
    found = on_chip(
        body,
        "weight_grad",
        [left, right, *[e[0] for e in extras]],
        shapes,
        cost(4 * depth * rows * cols, 2 * depth * (rows + cols), rows * cols * 2),
    )
    return found if halves else found[0]


ANY = pl.BlockSpec(memory_space=pl.ANY)


def copies(name, scalars, arrays, shapes, moves):
    def body(at_ref, *refs):
        ins, outs, sems = refs[: len(arrays)], refs[len(arrays) : -1], refs[-1]
        jobs = [
            pltpu.make_async_copy(source, target, sems.at[n])
            for n, (source, target) in enumerate(moves(at_ref, ins, outs))
        ]
        for job in jobs:
            job.start()
        for job in jobs:
            job.wait()

    return pl.pallas_call(
        body,
        in_specs=[SMEM] + [ANY] * len(arrays),
        out_specs=[VMEM] * len(shapes),
        out_shape=[jax.ShapeDtypeStruct(shape, BF16) for shape in shapes],
        scratch_shapes=[pltpu.SemaphoreType.DMA((24,))],
        compiler_params=pltpu.CompilerParams(vmem_limit_bytes=48 * 1024 * 1024),
        cost_estimate=cost(0, 2 * sum(int(np.prod(shape)) for shape in shapes), 0),
        name=name,
    )(scalars, *arrays)


def rotary_tables(lengths, size):
    lanes, half = 128, ROT // 2
    power = -(np.arange(half, dtype=np.float32) * np.float32(2.0 / ROT))
    inverse = np.zeros((1, lanes), np.float32)
    inverse[0, :half] = inverse[0, half:ROT] = np.float32(10000.0) ** power
    count = len(lengths)

    def body(*refs):
        inverse_ref, cos_ref, before_ref, after_ref, begin_ref = refs[count:]
        for n in range(count):
            row = lax.broadcasted_iota(jnp.int32, (size, 1), 0)
            begin = jnp.zeros((size, 1), jnp.int32)
            start = jnp.int32(0)
            for k in range(lengths[n].shape[1]):
                begin = jnp.where(row >= start, start, begin)
                start = start + refs[n][0, k]
            angle = (row - begin).astype(F32) * inverse_ref[...]
            sine = jnp.sin(angle)
            lane = lax.broadcasted_iota(jnp.int32, (size, lanes), 1)
            cos_ref[n] = jnp.cos(angle)
            before_ref[n] = jnp.where(lane < half, -sine, 0.0)
            after_ref[n] = jnp.where((lane >= half) & (lane < ROT), sine, 0.0)
            begin_ref[n] = begin

    table = ((count, size, lanes), F32)
    *tables, begins = on_chip(
        body,
        "rotary_tables",
        [jnp.asarray(inverse)],
        [table, table, table, ((count, size, 1), jnp.int32)],
        cost(0, 0, 12 * count * size * lanes),
        lengths,
    )
    return tuple(tables), begins


def small_params(packed, at, spans, blocks, slice_rows):
    rows = packed.shape[0]
    first = np.cumsum([0] + spans)
    width = spans[2] * rows

    def body(at_ref, p_ref, qkv_ref, up_ref, out_ref, scales_ref, table):
        z, part, block = at_ref[0], at_ref[1], at_ref[2]
        table[...] = p_ref[...].astype(F32)
        qkv_ref[...] = table[pl.ds(2 * z + part, 1), : spans[0]]
        for k in range(blocks):
            columns = pl.ds(pl.multiple_of(first[1] + z * slice_rows, 128), slice_rows)
            up_ref[:, k * slice_rows : (k + 1) * slice_rows] = table[pl.ds(2 * k + part, 1), columns]
        each = spans[2]
        for i in range(rows):
            out_ref[:, i * each : (i + 1) * each] = (
                table[i : i + 1, first[2] : first[3]] + table[i : i + 1, first[3] : first[4]]
            )
        for off in range(blocks):
            for c in range(2):
                row = pl.ds(2 * (block ^ off) + c, 1)
                place = (off * 2 + c) * each
                for k in range(4):
                    scales_ref[k : k + 1, place : place + each] = table[row, first[4 + k] : first[5 + k]]

    return pl.pallas_call(
        body,
        in_specs=[SMEM, VMEM],
        out_specs=[VMEM] * 4,
        out_shape=[
            jax.ShapeDtypeStruct(shape, F32)
            for shape in ((1, spans[0]), (1, blocks * slice_rows), (1, width), (4, width))
        ],
        scratch_shapes=[pltpu.VMEM(packed.shape, F32)],
        compiler_params=pltpu.CompilerParams(vmem_limit_bytes=4 * 1024 * 1024),
        cost_estimate=cost(0, 0, 0),
        name="small_params",
    )(at, packed)


def chunk_rows(value, count):
    rows, columns = value.shape
    size = columns // count

    def body(from_ref, to_ref):
        for k in range(count):
            to_ref[k * rows : (k + 1) * rows, :] = from_ref[:, k * size : (k + 1) * size]

    return on_chip(
        body, "chunk_rows", [value], [((rows * count, size), value.dtype)], cost(0, 0, 4 * value.size)
    )[0]


def core_shares(value, axis, at, count=1):
    rows, columns = value.shape[0] // count, value.shape[1]
    shape = (rows // 2, columns * count) if axis == 0 else (rows, columns // 2)

    def body(at_ref, from_ref, mine_ref, other_ref):
        part = at_ref[1]
        for ref, which in ((mine_ref, part), (other_ref, 1 - part)):
            if axis == 0:
                for k in range(count):
                    place = pl.multiple_of(k * rows + which * shape[0], shape[0])
                    ref[:, k * columns : (k + 1) * columns] = from_ref[pl.ds(place, shape[0]), :]
            else:
                ref[...] = from_ref[:, pl.ds(pl.multiple_of(which * shape[1], shape[1]), shape[1])]

    return on_chip(
        body, "core_shares", [value], [(shape, value.dtype)] * 2, cost(0, 0, 4 * value.size), [at]
    )


def core_join(mine, got, axis, at):
    rows, columns = mine.shape
    shape = (2 * rows, columns) if axis == 0 else (rows, 2 * columns)

    def body(at_ref, mine_ref, got_ref, out_ref):
        part = at_ref[1]
        for ref, which in ((mine_ref, part), (got_ref, 1 - part)):
            if axis == 0:
                out_ref[pl.ds(pl.multiple_of(which * rows, rows), rows), :] = ref[...].astype(F32)
            else:
                place = pl.multiple_of(which * columns, columns)
                out_ref[:, pl.ds(place, columns)] = ref[...].astype(F32)

    return on_chip(body, "core_join", [mine, got], [(shape, F32)], cost(0, 0, 8 * mine.size), [at])[0]


def copied(value):
    def body(from_ref, to_ref):
        to_ref[...] = from_ref[...]

    return on_chip(body, "copied", [value], [(value.shape, value.dtype)], cost(0, 0, 2 * value.size))[0]


def chip_pair(own, other, at):
    rows, columns = own.shape

    def body(at_ref, own_ref, other_ref, out_ref):
        part = at_ref[1]
        out_ref[pl.ds(pl.multiple_of(part * rows, rows), rows), :] = own_ref[...]
        out_ref[pl.ds(pl.multiple_of((1 - part) * rows, rows), rows), :] = other_ref[...]

    return on_chip(
        body, "chip_pair", [own, other], [((2 * rows, columns), BF16)], cost(0, 0, 0), [at]
    )[0]


class Place:
    def __init__(self):
        self.n_dp = lax.axis_size("dp")
        self.n_seq = lax.axis_size("seq")
        assert self.n_dp == 2 * self.n_seq
        self.split = 2 if H % (2 * self.n_seq) == 0 else 1
        self.blocks = self.n_dp // self.split
        self.dp = lax.axis_index("dp")
        self.z = lax.axis_index("seq")
        self.block = self.dp // self.split
        self.part = self.dp % self.split
        self.at = jnp.stack([self.z, self.part, self.block]).astype(jnp.int32)
        self.masks = [1 << k for k in range(self.blocks.bit_length() - 1)]
        self.order = list(range(self.blocks))
        self.paired = self.split == 2 and self.blocks == 4

    def swap(self, value, mask):
        return lax.ppermute(value, "dp", [(i, i ^ mask) for i in range(self.n_dp)])

    def to_relative(self, value, axis):
        size = value.shape[axis] // self.blocks
        return jnp.concatenate(
            [
                lax.dynamic_slice_in_dim(value, (self.block ^ off) * size, size, axis)
                for off in self.order
            ],
            axis=axis,
        )

    def to_natural(self, value, axis):
        return self.to_relative(value, axis)

    def pair(self, own, other, axis):
        return jnp.where(
            self.part == 0,
            jnp.concatenate([own, other], axis=axis),
            jnp.concatenate([other, own], axis=axis),
        )

    def gather(self, piece):
        half = piece.shape[0] // 2
        gathered = []
        for rows, masks in ((piece[:half], self.masks), (piece[half:], self.masks[::-1])):
            have = {0: rows}
            for mask in masks:
                offs = list(have)
                sent = jnp.concatenate([have[o] for o in offs], 0) if len(offs) > 1 else have[offs[0]]
                got = self.swap(sent, mask * self.split)
                for k, o in enumerate(offs):
                    have[o ^ mask] = got[k * half : (k + 1) * half]
            gathered.append(have)
        return gathered

    def scatter_sum(self, product, halves):
        out = []
        for half, masks in zip(halves, (self.masks, self.masks[::-1])):
            live = list(range(self.blocks))
            extra = {}

            def total(offs):
                whole = product(half, offs)
                if all(o not in extra for o in offs):
                    return whole
                axis, size = whole.ndim and product.axis, whole.shape[product.axis] // len(offs)
                parts = []
                for k, o in enumerate(offs):
                    value = lax.slice_in_dim(whole, k * size, (k + 1) * size, axis=axis)
                    for more in extra.get(o, ()):
                        value = value + more.astype(F32)
                    parts.append(value)
                return parts[0] if len(parts) == 1 else jnp.concatenate(parts, axis=axis)

            for mask in masks:
                away = [o for o in self.order if o in live and o & mask]
                sent = total(away).astype(BF16)
                got = self.swap(sent, mask * self.split)
                size = got.shape[product.axis] // len(away)
                for k, o in enumerate(away):
                    extra.setdefault(o ^ mask, []).append(
                        lax.slice_in_dim(got, k * size, (k + 1) * size, axis=product.axis)
                    )
                live = [o for o in live if not o & mask]
            out.append(total([0]))
        return out


class Product:
    def __init__(self, place, by_block, other, axis):
        self.place, self.by_block, self.other, self.axis = place, by_block, other, axis
        self.size = by_block.shape[1] // place.blocks

    def __call__(self, half, offs):
        where = [self.place.order.index(o) for o in offs]
        if where == list(range(where[0], where[0] + len(where))):
            blocks = self.by_block[:, where[0] * self.size : (where[-1] + 1) * self.size]
        else:
            blocks = jnp.concatenate(
                [self.by_block[:, w * self.size : (w + 1) * self.size] for w in where], axis=1
            )
        width = self.other.shape[1] // 2
        others = self.other[:, half * width : (half + 1) * width]
        if self.axis == 0:
            return left_transposed(blocks, others)
        return left_transposed(others, blocks)


class Chain:
    def __init__(self):
        self.last = None

    def __call__(self, *values):
        if self.last is not None:
            values = tuple(lax.optimization_barrier((values, self.last))[0])
        return values if len(values) > 1 else values[0]

    def done(self, value):
        self.last = value
        return value

    def wait(self, value):
        if value is not None:
            self.last = (self.last, value)


class Gathered:
    def __init__(self, here, piece):
        self.here, self.piece = here, piece
        self.half = piece.shape[0] // 2

    def send(self):
        here = self.here
        if here.paired:
            self.by_x, self.by_y = here.swap(self.piece, 2), here.swap(self.piece, 4)
            return self.by_x, self.by_y

    def hand_on(self, chain):
        if self.here.paired:
            half = self.half
            columns = self.piece.shape[1]

            def body(x_ref, y_ref, first_ref, second_ref):
                first_ref[...] = x_ref[:half, :]
                second_ref[...] = y_ref[half:, :]

            first, second = on_chip(
                body,
                "hand_on",
                chain(self.by_x, self.by_y),
                [((half, columns), BF16)] * 2,
                cost(0, 0, 4 * half * columns),
            )
            chain.done((first, second))
            self.handed = (self.here.swap(first, 4), self.here.swap(second, 2))
            return self.handed

    def rows(self, size, moving, columns=None):
        here, block = self.here, self.piece.shape[0]
        if here.paired:
            arrays = [self.piece, self.by_x, self.by_y, *self.handed]
            tiles, now, left = [], [], size
            for which, count in enumerate([block] * 3 + [self.half] * 2):
                first = 0
                while count:
                    take = min(left, count)
                    now.append((which, first, take))
                    first, count, left = first + take, count - take, left - take
                    if not left:
                        tiles.append(now)
                        now, left = [], size
            blocks = None
            if moving:
                assert size == block
                blocks = here.block ^ jnp.arange(here.blocks, dtype=jnp.int32)
            return Pieces(arrays, tiles, size, blocks, columns)
        if not hasattr(self, "whole"):
            halves = here.gather(self.piece)
            whole = jnp.concatenate([half[o] for o in range(here.blocks) for half in halves], axis=0)
            self.whole = here.to_natural(whole, 0) if moving else whole
        count = self.whole.shape[0] // size
        blocks = jnp.arange(count, dtype=jnp.int32) if moving else None
        return Pieces([self.whole], [[(0, k * size, size)] for k in range(count)], size, blocks, columns)


class Spread:
    def __init__(self, here, piece):
        self.here, self.step = here, 0
        chips = here.n_dp // 2
        masks = [1 << k for k in range(chips.bit_length() - 1)]
        self.steps = len(masks)
        self.offset = (here.dp // 2) ^ here.z
        self.states = [(piece[0], masks, [0]), (piece[1], masks[::-1], [0])]

    def send(self):
        here, self.got = self.here, []
        for rows, order, held in self.states:
            pairs = [
                (
                    (2 * (z ^ o) + c) * here.n_seq + z,
                    (2 * (z ^ o ^ order[self.step]) + c) * here.n_seq + z,
                )
                for z in range(here.n_seq)
                for o in held
                for c in range(2)
            ]
            self.got.append(lax.ppermute(rows, ("dp", "seq"), pairs))
        return tuple(self.got)

    def take(self, chain):
        got = chain(*self.got)
        after = []
        for new, (rows, order, held) in zip(got, self.states):
            takes = jnp.zeros((), jnp.bool_)
            for o in held:
                takes = takes | (self.offset == (o ^ order[self.step]))
            after.append(
                (
                    jnp.where(takes, new, rows),
                    order,
                    held + [o ^ order[self.step] for o in held],
                )
            )
        self.states = after
        self.step += 1
        chain.done(tuple(state[0] for state in after))

    def hold(self, chain):
        self.states = [(chain(rows), order, held) for rows, order, held in self.states]

    def finish(self, chain):
        self.take(chain)
        here = self.here
        rows = jnp.concatenate([state[0] for state in self.states], axis=0)
        if here.split == 1:
            other = here.swap(rows, 1)
            rows = jnp.where(
                here.dp % 2 == 0,
                jnp.concatenate([rows, other], 0),
                jnp.concatenate([other, rows], 0),
            )
        return rows


class Scattered:
    def __init__(self, here, left, right):
        self.here, self.left, self.right = here, left, right
        self.axis = 0 if isinstance(left, (list, tuple)) else 1

    def part(self, off, **more):
        if self.axis == 0:
            return weight_grad(self.left[off], self.right, **more)
        return weight_grad(self.left, self.right[off], **more)

    def first(self, chain):
        if self.here.paired:
            if self.axis == 0:
                self.right = chain(self.right)
            else:
                self.left = chain(self.left)
            one, two = chain.done(self.part(3, halves=True))
            self.by_x, self.by_y = self.here.swap(one, 2), self.here.swap(two, 4)
            return self.by_x, self.by_y

    def second(self, chain):
        if self.here.paired:
            by_x, by_y = chain(self.by_x, self.by_y)
            half = by_x.shape[0]
            to_x = self.part(1, extras=((by_y, half),))
            to_y = self.part(2, extras=((by_x, 0),))
            chain.done((to_x, to_y))
            self.by_x, self.by_y = self.here.swap(to_x, 2), self.here.swap(to_y, 4)
            return self.by_x, self.by_y

    def last(self, chain, kind):
        if self.here.paired:
            by_x, by_y = chain(self.by_x, self.by_y)
            return chain.done(self.part(0, extras=((by_x, 0), (by_y, 0)), kind=kind))
        if self.axis == 1:
            product = Product(self.here, jnp.concatenate(self.right, axis=1), self.left, 1)
        else:
            product = Product(self.here, jnp.concatenate(self.left, axis=1), self.right, 0)
        halves = self.here.scatter_sum(product, (0, 1))
        return jnp.concatenate(halves, axis=1 - self.axis).astype(kind)


def on_device(
    tokens,
    doc_lengths,
    qkv_weight,
    qkv_bias,
    dense_weight,
    dense_bias,
    up_weight,
    up_bias,
    down_weight,
    down_bias,
    norm1_gain,
    norm1_shift,
    norm2_gain,
    norm2_shift,
    cotangent,
):
    here = Place()
    chain = Chain()
    n_dp, n_seq, split, blocks = here.n_dp, here.n_seq, here.split, here.blocks
    z, part = here.z, here.part
    rows_here, width = tokens.shape
    seq_len = rows_here * n_seq
    hidden_rows = down_weight.shape[0]
    slice_rows = hidden_rows // n_seq
    assert H == n_seq * split
    head_cols = 3 * HS

    def column_places(core):
        head = (z * split + core) * head_cols
        return head, [(k * split + core) * hidden_rows + z * slice_rows for k in range(blocks)]

    half_dense = dense_weight.shape[0] // 2
    wide_cols = head_cols + blocks * slice_rows
    if here.paired:
        size = width // blocks

        def moves(at, ins, outs):
            tokens_in, qkv_in, up_in, down_in, dense_in = ins
            plane, core, block = at[0], at[1], at[2]
            jobs = []
            for off in range(blocks):
                place = pl.multiple_of((block ^ off) * size, size)
                jobs.append((tokens_in.at[:, pl.ds(place, size)], outs[0].at[:, off * size : (off + 1) * size]))
            for out, its in ((outs[1], 1 - core), (outs[2], core)):
                place = pl.multiple_of((plane * split + its) * head_cols, 128)
                jobs.append((qkv_in.at[:, pl.ds(place, head_cols)], out.at[:, :head_cols]))
                for k in range(blocks):
                    place = pl.multiple_of((k * split + its) * hidden_rows + plane * slice_rows, 128)
                    to = head_cols + k * slice_rows
                    jobs.append((up_in.at[:, pl.ds(place, slice_rows)], out.at[:, to : to + slice_rows]))
            place = pl.multiple_of(plane * slice_rows, slice_rows)
            jobs.append((down_in.at[pl.ds(place, slice_rows), :], outs[3]))
            jobs.append((dense_in.at[:half_dense], outs[4]))
            jobs.append((dense_in.at[half_dense:], outs[5]))
            return jobs

        shapes = [tokens.shape] + [(qkv_weight.shape[0], wide_cols)] * 2 + [(slice_rows, width)]
        shapes = shapes + [(half_dense, width)] * 2
        tokens_rel, wide_other, wide_piece, down_piece, *dense_halves = chain.done(
            copies(
                "first_copies",
                here.at,
                (tokens, qkv_weight, up_weight, down_weight, dense_weight),
                shapes,
                moves,
            )
        )
        got = here.swap(wide_other, 1)
    else:
        tokens_rel = here.to_relative(tokens, 1)
        head, places = column_places(part)
        wide_piece = jnp.concatenate(
            [lax.dynamic_slice_in_dim(qkv_weight, head, head_cols, 1)]
            + [lax.dynamic_slice_in_dim(up_weight, place, slice_rows, 1) for place in places],
            axis=1,
        )
        down_piece = lax.dynamic_slice_in_dim(down_weight, z * slice_rows, slice_rows, 0)
        dense_halves = dense_weight[:half_dense], dense_weight[half_dense:]
    x_own = lax.all_gather(tokens_rel, "seq", axis=0, tiled=True)
    g_own = lax.all_gather(chain(cotangent), "seq", axis=0, tiled=True)
    dense_rows = Spread(here, dense_halves)
    dense_pair = dense_rows.send()
    small = (qkv_bias, up_bias, dense_bias, down_bias, norm1_gain, norm1_shift, norm2_gain, norm2_shift)
    packed_small = chain.done(jnp.concatenate(chain(*small)))
    packed_small = jnp.broadcast_to(packed_small[None], (n_dp,) + packed_small.shape)
    packed_small = lax.all_to_all(packed_small, "dp", 0, 0, tiled=True)
    lengths = [doc_lengths] + ([here.swap(doc_lengths, 1)] if split == 2 else [])
    if here.paired:
        wide_piece = chain.done(chip_pair(chain(wide_piece), got, here.at))
    wide_rows = Gathered(here, wide_piece)
    wide_pair = wide_rows.send()
    lengths = [chain(v) for v in lengths]
    tables, begins = chain.done(rotary_tables(lengths, seq_len))
    spans = [v.shape[0] for v in small]

    chain.wait(dense_pair)
    dense_rows.take(chain)
    chain.wait(wide_pair)
    wide_pair = wide_rows.hand_on(chain)
    if here.paired:
        b_qkv, b_up, b_out, scales = chain.done(
            small_params(chain(packed_small), here.at, spans, blocks, slice_rows)
        )
    else:
        pieces, first = [], 0
        for span in spans:
            pieces.append(packed_small[:, first : first + span].astype(F32))
            first += span
        b_qkv, b_up, b_dense, b_down = pieces[:4]
        head = (z * split + part) * head_cols
        b_qkv = lax.dynamic_slice_in_dim(b_qkv.reshape(1, -1), head, head_cols, 1)
        b_up = lax.dynamic_slice_in_dim(b_up, z * slice_rows, slice_rows, 1)
        b_up = b_up.reshape(blocks, split, slice_rows)
        b_up = lax.dynamic_index_in_dim(b_up, part, 1, keepdims=False).reshape(1, -1)
        b_out = (b_dense + b_down).reshape(1, -1)
        scales = here.to_relative(jnp.stack([v.reshape(-1) for v in pieces[4:]]), 1)
    streams = [x_own] + ([here.swap(chain(x_own), 1)] if split == 2 else [])
    normed = chain.done(two_norms(chain(*streams) if split == 2 else streams, scales, blocks))
    normed_one, normed_two, stats = normed[:blocks], normed[blocks:-1], normed[-1]
    chain.wait(wide_pair)
    down_rows = Gathered(here, chain(down_piece))
    down_pair = down_rows.send()
    dense_rows.hold(chain)
    dense_pair = dense_rows.send()
    while dense_rows.step < dense_rows.steps - 1:
        dense_rows.take(chain)
        dense_pair = dense_rows.send()
    g_own = chain(g_own)
    streams_g = [g_own] + ([here.swap(g_own, 1)] if split == 2 else [])
    qkv_pieces = wide_rows.rows(256, False, (0, head_cols))
    up_pieces = wide_rows.rows(256, False, (head_cols, blocks * slice_rows))
    activated, slope = chain.done(feed_up(normed_two, up_pieces, chain(b_up)))
    qkv, probs, attended = chain.done(
        attention_forward(normed_one, qkv_pieces, chain(b_qkv), tables, begins)
    )
    attended = attended.reshape(split * seq_len, HS)
    chain.wait(down_pair)
    chain.wait(dense_pair)

    down_pair = down_rows.hand_on(chain)
    g_blocks = chain.done(cotangent_blocks(chain(*streams_g) if split == 2 else streams_g, here.at, blocks))
    sum_down = Scattered(here, activated, g_blocks)
    sum_dense = Scattered(here, attended, g_blocks)
    pair_down = sum_down.first(chain)
    w_dense = dense_rows.finish(chain)
    grad_projected, grad_qkv_bias = chain.done(
        attention_backward(chain(qkv), probs, g_blocks, w_dense, tables, here.at)
    )
    grad_projected = grad_projected.reshape(split * seq_len, head_cols)
    sum_qkv = Scattered(here, normed_one, grad_projected)
    chain.wait(down_pair)
    pair_qkv = sum_qkv.first(chain)
    down_pieces = down_rows.rows(down_piece.shape[0] if here.paired else 256, True)

    def to_plane(whole, axis):
        if here.paired:
            whole = chain.done(chunk_rows(chain(whole), n_seq)) if axis == 1 else whole
            return lax.all_to_all(whole, "seq", split_axis=0, concat_axis=0, tiled=True)
        moved = lax.all_to_all(whole, "seq", split_axis=axis, concat_axis=axis, tiled=True)
        per = moved.shape[axis] // (n_seq * 2)
        if axis == 0:
            return moved.reshape(n_seq, 2, per, -1).transpose(1, 0, 2, 3).reshape(moved.shape)
        return moved.reshape(-1, n_seq, 2, per).transpose(0, 2, 1, 3).reshape(moved.shape)

    def join(value):
        return lax.psum_scatter(value, "seq", scatter_dimension=0, tiled=True).astype(F32)

    def branches(first, extra=None):
        return chain.done(
            branch_rows_of(chain(attended), w_dense, activated, down_pieces, first, seq_len, extra)
        )

    def terms(first, extra=None):
        return chain.done(
            input_terms(
                chain(grad_projected),
                qkv_pieces,
                grad_hidden,
                up_pieces,
                streams[first],
                stats,
                scales,
                first,
                extra,
            )
        )

    branch_other = branches(1) if split == 2 else None
    chain.wait(pair_down)
    chain.wait(pair_qkv)
    if split == 2:
        branch_other = here.swap(chain(branch_other), 1)
    pair_down = sum_down.second(chain)
    branch_rows = join(branches(0, branch_other))
    pair_dense = sum_dense.first(chain)
    grad_hidden, grad_up_bias = chain.done(hidden_grad(g_blocks, down_pieces, chain(slope), here.at))
    sum_up = Scattered(here, normed_two, grad_hidden)
    term_other, norm_sums = None, jnp.zeros((4, width), F32)
    if split == 2:
        term_other, norm_sums = terms(1)
    chain.wait(pair_dense)
    chain.wait(pair_down)
    if split == 2:
        term_other = here.swap(chain(term_other), 1)
    pair_up = sum_up.first(chain)
    pair_dense = sum_dense.second(chain)
    plane_down = to_plane(sum_down.last(chain, BF16), 0)
    term_own, more_sums = terms(0, term_other)
    norm_sums = norm_sums + more_sums

    norm_sums = here.to_natural(chain(norm_sums), 1)
    wide_qkv = lax.dynamic_update_slice_in_dim(
        jnp.zeros((H * head_cols,), F32), grad_qkv_bias.reshape(-1), (z * split + part) * head_cols, 0
    )
    wide_up = lax.dynamic_update_slice(
        jnp.zeros((blocks, split, n_seq, slice_rows), F32),
        grad_up_bias.reshape(blocks, 1, 1, slice_rows),
        (0, part, z, 0),
    )
    cotan_rows = cotangent.astype(F32)
    column_total = jnp.sum(cotan_rows, axis=0)
    devices = n_dp * n_seq
    wide = [wide_qkv, wide_up, column_total] + [norm_sums[k] for k in range(4)]
    wide = [v.reshape(devices, -1) for v in wide]
    sizes = [v.shape[1] for v in wide]
    wide = chain.done(jnp.concatenate(wide, axis=1))

    def to_cores(value, axis, count=1):
        if not here.paired:
            return lambda: value.astype(F32)
        mine, other = chain.done(core_shares(chain(value), axis, here.at, count))
        got = here.swap(other, 1)
        return lambda: chain.done(core_join(*chain(mine, got), 1 - axis, here.at))

    chain.wait(pair_up)
    chain.wait(pair_dense)
    chain.wait(plane_down)
    term_rows = join(chain.done(copied(chain(term_own))))
    pair_up = sum_up.second(chain)
    wide = chain.done(copied(chain(wide)))
    swapped = lax.all_to_all(wide, ("dp", "seq"), split_axis=0, concat_axis=0, tiled=True)
    sum_dense_last = sum_dense.last(chain, F32)
    output = chain.done((chain(branch_rows) + tokens.astype(F32) + b_out).astype(BF16))
    chain.wait(pair_up)
    chain.wait(swapped)
    plane_up = to_plane(sum_up.last(chain, BF16), 1)
    pair_qkv = sum_qkv.second(chain)
    grad_dense = to_cores(sum_dense_last, 1)
    grad_down = to_cores(plane_down, 1)
    grad_dense, grad_down = grad_dense(), grad_down()

    values = chain(tokens_rel).astype(F32)
    centred = values - jnp.mean(values, axis=-1, keepdims=True)
    inverse = lax.rsqrt(jnp.mean(centred * centred, axis=-1, keepdims=True) + 1e-05)
    xhat = centred * inverse
    term_rows = chain(term_rows)
    term = (
        term_rows
        - jnp.mean(term_rows, axis=-1, keepdims=True)
        - xhat * jnp.mean(term_rows * xhat, axis=-1, keepdims=True)
    ) * inverse
    input_grad = chain.done((cotan_rows + here.to_natural(term, 1)).astype(BF16))
    chain.wait(pair_qkv)
    grad_qkv = to_cores(sum_qkv.last(chain, F32), 0)()
    total = jnp.sum(swapped, axis=0)
    sums, first = [], 0
    for size in sizes:
        sums.append(total[first : first + size])
        first += size
    sum_qkv_bias, sum_up_bias, sum_column, sum_gain_one, sum_shift_one, sum_gain_two, sum_shift_two = sums

    grad_up = to_cores(plane_up, 0, n_seq)()
    return (
        output,
        input_grad,
        grad_qkv,
        sum_qkv_bias,
        grad_dense,
        sum_column,
        grad_up,
        sum_up_bias,
        grad_down,
        sum_column,
        sum_gain_one,
        sum_shift_one,
        sum_gain_two,
        sum_shift_two,
    )


def solution(mesh):
    rows = P(("dp", "seq"), None)
    flat = P(("dp", "seq"))
    placed = (rows,) + (P("dp", None),) * 2 + (P("dp"), P("dp", None)) * 3 + (P("dp"),) * 5 + (rows,)
    return jax.shard_map(
        on_device,
        mesh=mesh,
        in_specs=placed,
        out_specs=(
            rows,
            rows,
            P("dp", "seq"),
            flat,
            P("seq", "dp"),
            flat,
            P("dp", "seq"),
            flat,
            P("seq", "dp"),
            flat,
            flat,
            flat,
            flat,
            flat,
        ),
        check_vma=False,
    )
```
